32 devices in a mesh: sec: 8 (over y, x, core), ch: 4 (over z).
Axes of the slice: x: 2, y: 2, z: 4, core: 2. Of those that a mesh axis runs over, the one named last changes fastest.
Arguments:
- start_amps: bfloat16 [6, 1024, 2048], P(None, 'ch'), may hold values from -6 to 6
- energies: float32 [6], replicated, may hold values from 0.5 to 2
- thresholds: bfloat16 [8, 1024], P('sec', 'ch'), may hold values from -3 to -1
- intersection: bfloat16 [8, 1024, 1024], P('sec', 'ch'), may hold values from -0.2 to 1
Outputs:
- boundary_amps: bfloat16 [8, 6, 1024, 2048], P('sec', None, 'ch')
The draws below stay inside these ranges and needn't reach their ends.
All inputs are finite; a program needn't handle non-finite values.
Results may differ from the reference program's by a relative error of at most 0.04.
Values may be sent and summed in bfloat16 or wider, within the bound.
A program may use at most 64 MiB of HBM per device.

```python
import math
import jax
import jax.numpy as jnp
from jax import lax

CH = 1024
NV = 1024
NE = 6
SECTORS = 8


def draw_intersection(key, part):
    spread = jax.random.truncated_normal(key, -4.0, 4.0, (SECTORS, CH, CH), jnp.float32) * (0.25 / math.sqrt(2.0 * CH))
    skewed = spread - jnp.swapaxes(spread, 1, 2)
    identity = jnp.eye(CH, dtype=jnp.float32)[None, :, :]
    return ((identity + skewed) / math.sqrt(1.0625)).astype(jnp.bfloat16)


def steps_of(key, extent, shards, low, largest):
    def one(axis_at, parts):
        draws = jax.random.uniform(jax.random.fold_in(jax.random.fold_in(key, 6), axis_at), (parts,), jnp.float32, low / len(shards), largest / len(shards))
        return jnp.repeat(jnp.exp(draws), extent[axis_at] // parts).reshape((-1,) + (1,) * (len(extent) - axis_at - 1))

    loudness = one(*shards[0])
    for cut in shards[1:]:
        loudness = loudness * one(*cut)
    return loudness


def scatter_about(rng, shape, scale, limit, cuts=(), kind=jnp.bfloat16):
    array = scale * jax.random.normal(rng, shape, jnp.float32)
    if cuts:
        array = array * steps_of(rng, shape, cuts, -0.22, 0.18)
    return jnp.clip(array, -limit, limit).astype(kind)


def setup_inputs(seed: int = 0) -> dict:
    keys = jax.random.split(jax.random.key(seed), 5)
    return {
        "start_amps": scatter_about(keys[0], (NE, CH, 2 * NV), 1.0, 6.0, ((1, 4),)),
        "energies": jnp.clip(jax.random.uniform(keys[1], (NE,), jnp.float32, 0.5, 2.0), 0.5, 2.0),
        "thresholds": jnp.clip(-3.0 + 2.0 * jax.random.uniform(keys[2], (SECTORS, CH), jnp.float32) ** steps_of(keys[2], (SECTORS, CH), ((0, 8), (1, 4)), -0.2, 0.2), -3.0, -1.0).astype(jnp.bfloat16),
        "intersection": draw_intersection(jax.random.fold_in(keys[4], 71), 0),
    }


def rotate(amplitude, wavenumber):
    half = amplitude.shape[-1] // 2
    values_part = amplitude[..., :half]
    slopes_part = amplitude[..., half:]
    cosine = jnp.cos(wavenumber)
    sine_term = jnp.sin(wavenumber)
    new_values = cosine * values_part + sine_term / wavenumber * slopes_part
    new_slopes = -wavenumber * sine_term * values_part + cosine * slopes_part
    return jnp.concatenate([new_values, new_slopes], axis=-1)

def reference(start_amps, energies, thresholds, intersection):

    def advance(amplitude, sector_data):
        channel_thresholds, basis_change = sector_data
        wavenumber = jnp.sqrt(energies[:, None] - channel_thresholds.astype(jnp.float32)[None, :])[:, :, None]
        rotated = rotate(amplitude, wavenumber).astype(jnp.bfloat16)
        product = jnp.einsum('ij,ejn->ein', basis_change.astype(jnp.float32), rotated.astype(jnp.float32))
        fresh = product.astype(jnp.bfloat16)
        return (fresh.astype(jnp.float32), fresh)
    initial = start_amps.astype(jnp.float32)
    final_state, boundary_amps = lax.scan(advance, initial, (thresholds, intersection))
    return boundary_amps
```

```python
import functools
import jax
import jax.numpy as jnp
from jax import lax
from jax.experimental import pallas as pl
from jax.experimental.pallas import tpu as pltpu
from jax.sharding import PartitionSpec as P


def passed_along(value, axis, steps):
    count = lax.axis_size(axis)
    leading, last = (max(0, -steps), min(count, count - steps))
    return lax.ppermute(value, axis, [(source, source + steps) for source in range(leading, last)])


def per_device_pipelined(start_amps, energies, thresholds, intersection):
    sectors = lax.axis_size("sec")
    sector_index = lax.axis_index("sec")
    groups = lax.axis_size("ch")
    energy_count = energies.shape[0]
    step_count = sectors + energy_count - 1
    row_count = intersection.shape[1]
    width_cols = start_amps.shape[2]
    half_cols = width_cols // 2
    col_width = half_cols // groups
    intersection_whole, thresholds_whole = (
        lax.all_gather(intersection, "ch", axis=1, tiled=True),
        lax.all_gather(thresholds, "ch", axis=1, tiled=True),
    )
    basis_change = intersection_whole[0]
    channel_thresholds = thresholds_whole[0].astype(jnp.float32)
    channel_count = basis_change.shape[0]
    paired = start_amps.reshape(energy_count, row_count, 2, half_cols)
    start_cols = lax.all_to_all(paired, "ch", split_axis=3, concat_axis=1, tiled=True)
    stored_init = jnp.zeros((energy_count, channel_count, 2, col_width), jnp.bfloat16)

    def multiply(flat):
        return jnp.dot(basis_change, flat, preferred_element_type=jnp.float32).astype(jnp.bfloat16)

    def skipped(flat):
        return jnp.zeros((channel_count, 2 * col_width), jnp.bfloat16)

    def step(step_index, state_pair):
        outgoing, stored = state_pair
        incoming = passed_along(outgoing, "sec", 1)
        energy_raw = step_index - sector_index
        active = (energy_raw >= 0) & (energy_raw < energy_count)
        energy_slot = jnp.clip(energy_raw, 0, energy_count - 1)
        initial = lax.dynamic_index_in_dim(start_cols, energy_slot, 0, keepdims=False)
        source = jnp.where(sector_index == 0, initial, incoming).astype(jnp.float32)
        wavenumber = jnp.sqrt(energies[energy_slot] - channel_thresholds)[:, None]
        values_part = source[:, 0, :]
        slopes_part = source[:, 1, :]
        cosine = jnp.cos(wavenumber)
        sine_term = jnp.sin(wavenumber)
        new_values = cosine * values_part + sine_term / wavenumber * slopes_part
        new_slopes = -wavenumber * sine_term * values_part + cosine * slopes_part
        rotated = jnp.stack([new_values, new_slopes], axis=1).astype(jnp.bfloat16)
        flat = rotated.reshape(channel_count, 2 * col_width)
        fresh = lax.cond(active, multiply, skipped, flat)
        fresh = fresh.reshape(channel_count, 2, col_width)
        previous = lax.dynamic_index_in_dim(stored, energy_slot, 0, keepdims=False)
        kept = jnp.where(active, fresh, previous)
        stored = lax.dynamic_update_index_in_dim(stored, kept, energy_slot, 0)
        return (fresh, stored)

    outgoing_init = jnp.zeros((channel_count, 2, col_width), jnp.bfloat16)
    final_pair = lax.fori_loop(0, step_count, step, (outgoing_init, stored_init))
    returned = lax.all_to_all(final_pair[1], "ch", split_axis=1, concat_axis=3, tiled=True)
    return returned.reshape(energy_count, row_count, width_cols)[None]


LANES = 128
STAGES = 5


def sweep_kernel(
    sectors, groups, start, energies, limits, own_block, out,
    basis, amps, rotated, kept, turn, bounds,
    local_sem, block_recv, side_send, over_send, up_send, down_send, core_send,
    start_recv, start_up, start_down, bound_send, bound_recv, out_send, out_recv, out_local,
):
    k = lax.axis_index("sec")
    z = lax.axis_index("ch")
    core = k % 2
    chip = k // 2
    column, row = chip % 2, chip // 2
    partner = k + 1 - 2 * core
    column_peer = k + 2 - 4 * column
    row_peer = k + 4 - 8 * row
    pairs = sectors // 2
    last = sectors - 1
    energy_count, row_count, width_cols = start.shape
    half_cols = width_cols // 2
    width = half_cols // sectors
    channel_count = row_count * groups
    chunks = channel_count // LANES
    devices = sectors * groups
    has_up = z + 1 < groups
    has_down = z >= 1
    rounds = max(pairs, energy_count)
    inputs = 2 * rounds

    def remote(src, dst, send, recv, **where):
        return pltpu.make_async_remote_copy(
            src_ref=src, dst_ref=dst, send_sem=send, recv_sem=recv,
            device_id=where, device_id_type=pl.DeviceIdType.MESH,
        )

    def rows_of(c):
        return pl.ds(pl.multiple_of(c * row_count, row_count), row_count)

    def other(step):
        place = (k * groups + z + step) % devices
        return {"sec": place // groups, "ch": place % groups}

    def block_move(s, b, send, **where):
        part = basis.at[s, rows_of(b), :]
        return remote(part, part, send.at[s // 2, b], block_recv.at[s, b], **where)

    def routes(pair, b):
        s = 2 * pair + core
        across = pair % 2
        near = jnp.where(across == 0, row == pair // 2, column == pair % 2)
        carrier = near != (core == 1)
        home = b == z
        along = (s < last) & carrier
        return s, [
            (along & has_up & (b <= z), lambda: block_move(s, b, up_send, ch=z + 1)),
            (along & has_down & (b >= z), lambda: block_move(s, b, down_send, ch=z - 1)),
            (home & (chip == pair), lambda: block_move(s, b, side_send, sec=jnp.where(across == 0, column_peer, row_peer))),
            (jnp.where(home, near, carrier), lambda: block_move(s, b, over_send, sec=jnp.where(across == 0, row_peer, column_peer))),
            (b >= 0, lambda: block_move(s, b, core_send, sec=partner)),
        ]

    def travels(s, b):
        return (s < last) | (b == z)

    def relay(pair, b):
        for wanted, move in routes(pair, b)[1]:
            @pl.when(wanted)
            def _():
                move().start()

    def block_arrived(s, b):
        block_move(s, b, core_send, sec=partner).wait_recv()

    def arrive_and_relay(pair, b):
        s = 2 * pair + core

        @pl.when((b >= 0) & (b < groups) & travels(s, b))
        def _():
            block_arrived(s, b)
            relay(pair, b)

    def start_part(e, c):
        return amps.at[0, e, rows_of(c), :]

    def start_move(e, c, send, **where):
        return remote(start_part(e, c), start_part(e, c), send.at[c], start_recv.at[e, c], **where)

    def start_relay(e, c):
        @pl.when(has_up & (c <= z))
        def _():
            start_move(e, c, start_up, ch=z + 1).start()

        @pl.when(has_down & (c >= z))
        def _():
            start_move(e, c, start_down, ch=z - 1).start()

    def start_arrive_and_relay(e, c):
        @pl.when((c >= 0) & (c < groups))
        def _():
            start_move(e, c, start_up, sec=partner).wait_recv()
            start_relay(e, c)

    def event(item, stage):
        own = (stage == 0) & (item + 2 < inputs)
        passed = (stage == 1) & (item + 1 < inputs)
        hop = stage - 1
        ahead = item + jnp.where(stage == 0, 2, jnp.where(stage == 1, 1, 0))
        place = ahead // 2
        is_pair = (ahead % 2 == 0) & (place < pairs)
        is_start = (ahead % 2 == 1) & (place < energy_count)

        @pl.when(is_pair & own & (chip == place))
        def _():
            relay(place, z)

        @pl.when(is_pair & passed & (chip != place))
        def _():
            arrive_and_relay(place, z)

        @pl.when(is_pair & (stage >= 2))
        def _():
            @pl.loop(0, 2)
            def _(side):
                arrive_and_relay(place, z - hop + 2 * hop * side)

        @pl.when(is_start & own)
        def _():
            start_relay(place, z)

        @pl.when(is_start & (stage >= 2))
        def _():
            @pl.loop(0, 2)
            def _(side):
                start_arrive_and_relay(place, z - hop + 2 * hop * side)

    loads = [
        pltpu.make_async_copy(own_block, basis.at[k, rows_of(z), :], local_sem.at[0]),
        pltpu.make_async_copy(
            start.at[:, :, pl.ds(pl.multiple_of(k * width, width), width)],
            amps.at[0, :, rows_of(z), pl.ds(0, width)], local_sem.at[1]),
        pltpu.make_async_copy(
            start.at[:, :, pl.ds(pl.multiple_of(half_cols + k * width, width), width)],
            amps.at[0, :, rows_of(z), pl.ds(width, width)], local_sem.at[2]),
        pltpu.make_async_copy(limits, bounds.at[k, z], local_sem.at[3]),
    ]
    for load in loads:
        load.start()

    barrier = pltpu.get_barrier_semaphore()

    @pl.loop(1, devices)
    def _(step):
        pl.semaphore_signal(barrier, inc=1, device_id=other(step), device_id_type=pl.DeviceIdType.MESH)

    pl.semaphore_wait(barrier, devices - 1)
    loads[0].wait()

    @pl.when(chip == 0)
    def _():
        relay(0, z)

    for load in loads[1:]:
        load.wait()

    def bound_move(step):
        return pltpu.make_async_remote_copy(
            src_ref=bounds.at[k, z], dst_ref=bounds.at[k, z], send_sem=bound_send.at[step], recv_sem=bound_recv.at[k, z],
            device_id=other(step), device_id_type=pl.DeviceIdType.MESH,
        )

    @pl.loop(1, devices)
    def _(step):
        bound_move(step).start()

    start_relay(0, z)

    @pl.when(chip != 0)
    def _():
        arrive_and_relay(0, z)

    @pl.loop(0, sectors)
    def _(s):
        for c in range(groups):
            @pl.when((s != k) | (c != z))
            def _():
                remote(bounds.at[s, c], bounds.at[s, c], bound_send.at[0], bound_recv.at[s, c], sec=partner).wait_recv()

        floor = jnp.concatenate([bounds[s, c] for c in range(groups)], axis=0)
        for e in range(energy_count):
            wavenumber = jnp.sqrt(energies[e] - floor)
            cosine = jnp.cos(wavenumber)
            sine_term = jnp.sin(wavenumber)
            filler = jnp.zeros((LANES - 3 * chunks, LANES), jnp.float32)
            stacked = jnp.concatenate(
                [cosine, sine_term / wavenumber, -wavenumber * sine_term, filler], axis=0
            )
            turn[s, e] = stacked.T

    def advance(s, e):
        source = jnp.minimum(s, 1)
        factors = turn[s, e]
        for q in range(chunks):
            place = pl.ds(q * LANES, LANES)
            both = amps[source, e, place, :].astype(jnp.float32)
            values_part, slopes_part = both[:, :width], both[:, width:]
            keep = factors[:, q : q + 1]
            rise = factors[:, chunks + q : chunks + q + 1]
            fall = factors[:, 2 * chunks + q : 2 * chunks + q + 1]
            rotated[place, pl.ds(0, width)] = (keep * values_part + rise * slopes_part).astype(jnp.bfloat16)
            rotated[place, pl.ds(width, width)] = (fall * values_part + keep * slopes_part).astype(jnp.bfloat16)

        @pl.when(s < last)
        def _():
            amps[1, e] = jnp.dot(basis[s], rotated[...], preferred_element_type=jnp.float32).astype(jnp.bfloat16)
            mine = amps[1, e, rows_of(z), :]
            kept[s, 0, e] = mine[:, :width]
            kept[s, 1, e] = mine[:, width:]

        @pl.when(s == last)
        def _():
            mine = jnp.dot(
                basis[s, rows_of(z), :], rotated[...], preferred_element_type=jnp.float32
            ).astype(jnp.bfloat16)
            kept[s, 0, e] = mine[:, :width]
            kept[s, 1, e] = mine[:, width:]

    def send_out(s, e):
        for half in range(2):
            columns = pl.ds(pl.multiple_of(half * half_cols + k * width, width), width)

            @pl.when(s == k)
            def _():
                pltpu.make_async_copy(kept.at[s, half, e], out.at[e, :, columns], out_local.at[0]).start()

            @pl.when(s != k)
            def _():
                remote(kept.at[s, half, e], out.at[e, :, columns], out_send.at[s], out_recv.at[k], sec=s).start()

    @pl.loop(0, inputs + 1)
    def _(upcoming):
        done = upcoming - 1
        place = jnp.maximum(done, 0) // 2
        from_pair = done % 2 == 0
        ready = jnp.minimum(2 * place + 2, sectors)
        pair_steps = jnp.where(place < pairs, 2 * jnp.minimum(place, energy_count), 0)
        start_steps = jnp.where(place < energy_count, ready, 0)
        steps = jnp.where(done < 0, 0, jnp.where(from_pair, pair_steps, start_steps))

        def task(i):
            return (
                jnp.where(from_pair, 2 * place + i % 2, i),
                jnp.where(from_pair, i // 2, place),
            )

        @pl.loop(0, jnp.maximum(steps + 1, STAGES))
        def _(i):
            @pl.when(i < steps)
            def _():
                advance(*task(i))

            @pl.when((i >= 1) & (i <= steps))
            def _():
                send_out(*task(i - 1))

            @pl.when((i < STAGES) & (upcoming < inputs))
            def _():
                event(upcoming, i)

        @pl.when((upcoming % 2 == 0) & (upcoming // 2 < pairs))
        def _():
            s = 2 * (upcoming // 2) + 1 - core
            for b in range(groups):
                @pl.when(travels(s, b))
                def _():
                    block_arrived(s, b)

    @pl.loop(1, devices)
    def _(step):
        bound_move(step).wait_send()

    @pl.loop(0, pairs)
    def _(pair):
        for b in range(groups):
            s, moves = routes(pair, b)

            @pl.when(travels(s, b))
            def _():
                for wanted, move in moves:
                    @pl.when(wanted)
                    def _():
                        move().wait_send()

    for c in range(groups):
        span = amps.at[0, :, pl.ds(c * row_count, row_count), :]

        @pl.when(has_up & (c <= z))
        def _():
            remote(span, span, start_up.at[c], start_recv.at[0, 0], ch=z + 1).wait_send()

        @pl.when(has_down & (c >= z))
        def _():
            remote(span, span, start_down.at[c], start_recv.at[0, 0], ch=z - 1).wait_send()

    @pl.loop(0, sectors)
    def _(s):
        whole = remote(kept.at[s], kept.at[s], out_send.at[s], out_recv.at[s], sec=partner)

        @pl.when(s != k)
        def _():
            whole.wait_send()
            whole.wait_recv()

        @pl.when(s == k)
        def _():
            pltpu.make_async_copy(kept.at[s], kept.at[s], out_local.at[0]).wait()


def per_device_swept(start_amps, energies, thresholds, intersection):
    sectors = lax.axis_size("sec")
    groups = lax.axis_size("ch")
    energy_count, row_count, width_cols = start_amps.shape
    channel_count = intersection.shape[2]
    width = width_cols // 2 // sectors
    pairs = sectors // 2
    limits = thresholds.reshape(row_count // LANES, LANES).astype(jnp.float32)
    dma = pltpu.SemaphoreType.DMA
    stored = jax.ShapeDtypeStruct(start_amps.shape, jnp.bfloat16)
    swept = pl.pallas_call(
        functools.partial(sweep_kernel, sectors, groups),
        out_shape=stored,
        in_specs=[
            pl.BlockSpec(memory_space=pl.ANY),
            pl.BlockSpec(memory_space=pltpu.SMEM),
            pl.BlockSpec(memory_space=pl.ANY),
            pl.BlockSpec(memory_space=pl.ANY),
        ],
        out_specs=pl.BlockSpec(memory_space=pl.ANY),
        scratch_shapes=[
            pltpu.VMEM((sectors, channel_count, channel_count), jnp.bfloat16),
            pltpu.VMEM((2, energy_count, channel_count, 2 * width), jnp.bfloat16),
            pltpu.VMEM((channel_count, 2 * width), jnp.bfloat16),
            pltpu.VMEM((sectors, 2, energy_count, row_count, width), jnp.bfloat16),
            pltpu.VMEM((sectors, energy_count, LANES, LANES), jnp.float32),
            pltpu.VMEM((sectors, groups, row_count // LANES, LANES), jnp.float32),
            dma((4,)),
            dma((sectors, groups)),
            dma((pairs, groups)),
            dma((pairs, groups)),
            dma((pairs, groups)),
            dma((pairs, groups)),
            dma((pairs, groups)),
            dma((energy_count, groups)),
            dma((groups,)),
            dma((groups,)),
            dma((sectors * groups,)),
            dma((sectors, groups)),
            dma((sectors,)),
            dma((sectors,)),
            dma((1,)),
        ],
        compiler_params=pltpu.CompilerParams(
            collective_id=0, has_side_effects=True, vmem_limit_bytes=60 * 2**20
        ),
    )(start_amps, energies, limits, intersection[0])
    return swept[None]


GATHERED_LIMIT = 24 * 2**20


def per_device(start_amps, energies, thresholds, intersection):
    sectors = lax.axis_size("sec")
    row_count, channel_count = intersection.shape[1:]
    gathered_bytes = sectors * channel_count**2 * intersection.dtype.itemsize
    even = sectors // 2 == 4 and (start_amps.shape[2] // 2) % (sectors * LANES) == 0
    even = even and row_count % LANES == 0 and 3 * (channel_count // LANES) <= LANES
    if even and gathered_bytes <= GATHERED_LIMIT:
        return per_device_swept(start_amps, energies, thresholds, intersection)
    return per_device_pipelined(start_amps, energies, thresholds, intersection)


def solution(mesh):
    in_specs = (P(None, "ch", None), P(), P("sec", "ch"), P("sec", "ch", None))
    out_specs = P("sec", None, "ch", None)
    return jax.shard_map(
        per_device, mesh=mesh, in_specs=in_specs, out_specs=out_specs, check_vma=False
    )
```

```python
import functools
import jax
import jax.numpy as jnp
from jax import lax
from jax.experimental import pallas as pl
from jax.experimental.pallas import tpu as pltpu
from jax.sharding import PartitionSpec as P


def passed_along(value, axis, steps):
    count = lax.axis_size(axis)
    leading, last = (max(0, -steps), min(count, count - steps))
    return lax.ppermute(value, axis, [(source, source + steps) for source in range(leading, last)])


def per_device_pipelined(start_amps, energies, thresholds, intersection):
    sectors = lax.axis_size("sec")
    sector_index = lax.axis_index("sec")
    groups = lax.axis_size("ch")
    energy_count = energies.shape[0]
    step_count = sectors + energy_count - 1
    row_count = intersection.shape[1]
    width_cols = start_amps.shape[2]
    half_cols = width_cols // 2
    col_width = half_cols // groups
    intersection_whole, thresholds_whole = (
        lax.all_gather(intersection, "ch", axis=1, tiled=True),
        lax.all_gather(thresholds, "ch", axis=1, tiled=True),
    )
    basis_change = intersection_whole[0]
    channel_thresholds = thresholds_whole[0].astype(jnp.float32)
    channel_count = basis_change.shape[0]
    paired = start_amps.reshape(energy_count, row_count, 2, half_cols)
    start_cols = lax.all_to_all(paired, "ch", split_axis=3, concat_axis=1, tiled=True)
    stored_init = jnp.zeros((energy_count, channel_count, 2, col_width), jnp.bfloat16)

    def multiply(flat):
        return jnp.dot(basis_change, flat, preferred_element_type=jnp.float32).astype(jnp.bfloat16)

    def skipped(flat):
        return jnp.zeros((channel_count, 2 * col_width), jnp.bfloat16)

    def step(step_index, state_pair):
        outgoing, stored = state_pair
        incoming = passed_along(outgoing, "sec", 1)
        energy_raw = step_index - sector_index
        active = (energy_raw >= 0) & (energy_raw < energy_count)
        energy_slot = jnp.clip(energy_raw, 0, energy_count - 1)
        initial = lax.dynamic_index_in_dim(start_cols, energy_slot, 0, keepdims=False)
        source = jnp.where(sector_index == 0, initial, incoming).astype(jnp.float32)
        wavenumber = jnp.sqrt(energies[energy_slot] - channel_thresholds)[:, None]
        values_part = source[:, 0, :]
        slopes_part = source[:, 1, :]
        cosine = jnp.cos(wavenumber)
        sine_term = jnp.sin(wavenumber)
        new_values = cosine * values_part + sine_term / wavenumber * slopes_part
        new_slopes = -wavenumber * sine_term * values_part + cosine * slopes_part
        rotated = jnp.stack([new_values, new_slopes], axis=1).astype(jnp.bfloat16)
        flat = rotated.reshape(channel_count, 2 * col_width)
        fresh = lax.cond(active, multiply, skipped, flat)
        fresh = fresh.reshape(channel_count, 2, col_width)
        previous = lax.dynamic_index_in_dim(stored, energy_slot, 0, keepdims=False)
        kept = jnp.where(active, fresh, previous)
        stored = lax.dynamic_update_index_in_dim(stored, kept, energy_slot, 0)
        return (fresh, stored)

    outgoing_init = jnp.zeros((channel_count, 2, col_width), jnp.bfloat16)
    final_pair = lax.fori_loop(0, step_count, step, (outgoing_init, stored_init))
    returned = lax.all_to_all(final_pair[1], "ch", split_axis=1, concat_axis=3, tiled=True)
    return returned.reshape(energy_count, row_count, width_cols)[None]


LANES = 128
HOME, LIFT, HOP, SIDE, TWIN, FEED, FEED_HOP, STEP, ANGLES, END = range(10)
TUNED = (
    (5, 0, 0), (5, 1, 0), (6, 0, 1), (6, 0, 2), (0, 0, 0), (1, 0, 0), (2, 0, 1), (3, 0, 1), (0, 1, 0), (2, 0, 2),
    (1, 1, 0), (3, 0, 2), (2, 0, 3), (2, 1, 1), (0, 3, 0), (1, 3, 0), (2, 1, 2), (0, 2, 0), (2, 1, 3), (3, 1, 2),
    (1, 2, 0), (3, 0, 3), (4, 0, 0), (3, 1, 1), (2, 2, 1), (2, 3, 1), (3, 1, 3), (2, 2, 2), (2, 3, 2), (3, 2, 1),
    (3, 3, 1), (4, 1, 0), (6, 0, 3), (3, 2, 2), (2, 2, 3), (7, 0, 0), (2, 3, 3), (3, 2, 3), (3, 3, 2), (3, 3, 3),
    (6, 1, 1), (5, 2, 0), (7, 1, 0), (7, 2, 0), (4, 2, 0), (6, 1, 2), (5, 3, 0), (7, 3, 0), (7, 4, 0), (6, 2, 1),
    (7, 5, 0), (4, 3, 0), (7, 6, 0), (6, 1, 3), (7, 0, 1), (7, 7, 0), (7, 1, 1), (7, 2, 1), (6, 3, 1), (7, 3, 1),
    (7, 4, 1), (6, 2, 2), (7, 5, 1), (6, 2, 3), (5, 4, 0), (6, 3, 2), (7, 6, 1), (7, 0, 2), (7, 7, 1), (5, 5, 0),
    (7, 1, 2), (7, 2, 2), (6, 3, 3), (7, 3, 2), (7, 4, 2), (7, 0, 3), (6, 5, 1), (7, 1, 3), (6, 4, 1), (7, 5, 2),
    (7, 6, 2), (6, 5, 2), (7, 2, 3), (7, 7, 2), (7, 3, 3), (7, 4, 3), (7, 5, 3), (7, 6, 3), (6, 4, 2), (6, 5, 3),
    (7, 0, 5), (7, 1, 5), (6, 4, 3), (7, 7, 3), (7, 0, 4), (7, 2, 5), (7, 3, 5), (7, 1, 4), (7, 2, 4), (7, 4, 5),
    (7, 5, 5), (7, 3, 4), (7, 4, 4), (7, 6, 5), (7, 5, 4), (7, 7, 5), (7, 6, 4), (7, 7, 4),
)


def plain_order(pairs, sectors, energy_count, groups):
    order = [(HOME, j, 0) for j in range(pairs)]
    order += [(FEED, e, 0) for e in range(energy_count)] + [(LIFT, j, 0) for j in range(pairs)]
    for tick in range(pairs + groups):
        for d in range(groups - 1, 0, -1):
            if 0 <= tick - d < pairs:
                order.append((HOP, tick - d, d))
            if 0 <= tick - d - 1 < pairs:
                order.append((SIDE, tick - d - 1, d))
    order += [(TWIN, j, 0) for j in range(pairs)]
    for e in range(energy_count):
        order += [(FEED_HOP, e, d) for d in range(1, groups)]
        order += [(STEP, s, e) for s in range(sectors)]
    return order


def order_of(pairs, sectors, energy_count, groups):
    plain = plain_order(pairs, sectors, energy_count, groups)
    chosen = TUNED if sorted(TUNED) == sorted(plain) else plain
    order, left = [], list(range(sectors))
    for entry in chosen:
        while left and entry[0] == STEP:
            order.append((ANGLES, left.pop(0), 0))
        order.append(entry)
        if left:
            order.append((ANGLES, left.pop(0), 0))
    return order


def sweep_kernel(
    sectors, groups, start, energies, limits, own_block, out,
    basis, amps, rotated, kept, turn, bounds,
    local_sem, block_recv, column_send, row_send, up_send, down_send, core_send,
    start_recv, start_up, start_down, bound_send, bound_recv, out_send, out_recv, out_local,
):
    k = lax.axis_index("sec")
    z = lax.axis_index("ch")
    core = k % 2
    chip = k // 2
    column, row = chip % 2, chip // 2
    partner = k + 1 - 2 * core
    column_peer = k + 2 - 4 * column
    row_peer = k + 4 - 8 * row
    pairs = sectors // 2
    last = sectors - 1
    energy_count, row_count, width_cols = start.shape
    half_cols = width_cols // 2
    width = half_cols // sectors
    channel_count = row_count * groups
    chunks = channel_count // LANES
    devices = sectors * groups
    has_up = z + 1 < groups
    has_down = z >= 1
    piece = row_count // 4
    order = order_of(pairs, sectors, energy_count, groups)

    def remote(src, dst, send, recv, **where):
        return pltpu.make_async_remote_copy(
            src_ref=src, dst_ref=dst, send_sem=send, recv_sem=recv,
            device_id=where, device_id_type=pl.DeviceIdType.MESH,
        )

    def rows_of(c):
        return pl.ds(pl.multiple_of(c * row_count, row_count), row_count)

    def other(step):
        place = (k * groups + z + step) % devices
        return {"sec": place // groups, "ch": place % groups}

    def part_of(s, b, q, h, count=1):
        return basis.at[s, pl.ds(pl.multiple_of(b * row_count + (2 * q + h) * piece, piece), count * piece), :]

    def piece_move(s, b, q, h, send, **where):
        part = part_of(s, b, q, h)
        return remote(part, part, send.at[s // 2, b], block_recv.at[s, b, 2 * q + h], **where)

    def near(j, q):
        return row == j // 2 if q == 0 else column == j % 2

    def carried(j, q):
        return jnp.where(near(j, q), 0, 1)

    def lift(s, b, q, h):
        @pl.when((s < last) & has_up & (b <= z))
        def _():
            piece_move(s, b, q, h, up_send, ch=z + 1).start()

        @pl.when((s < last) & has_down & (b >= z))
        def _():
            piece_move(s, b, q, h, down_send, ch=z - 1).start()

    def over(s, b, q, h):
        if q == 0:
            piece_move(s, b, q, h, row_send, sec=row_peer).start()
        else:
            piece_move(s, b, q, h, column_send, sec=column_peer).start()

    def to_core(s, b, q, h):
        piece_move(s, b, q, h, core_send, sec=partner).start()

    def piece_arrived(s, b, q, h):
        piece_move(s, b, q, h, core_send, sec=partner).wait_recv()

    def give_own():
        for h in (1, 0):
            for q in range(2):
                piece_move(k, z, q, h, column_send, sec=column_peer).start()
                piece_move(k, z, q, h, row_send, sec=row_peer).start()
        for h in (1, 0):
            for q in range(2):
                to_core(k, z, q, h)

    def home(j):
        s = 2 * j + core

        @pl.when(chip != j)
        def _():
            for h in (1, 0):
                for q in range(2):
                    piece_arrived(s, z, q, h)

                    @pl.when(near(j, q))
                    def _():
                        over(s, z, q, h)

                    to_core(s, z, q, h)

    def lift_own(j):
        for q in range(2):
            lift(2 * j + core, z, q, carried(j, q))

    def hop_from(j, d):
        s = 2 * j + core
        for q in range(2):
            for b in (z - d, z + d):
                @pl.when((s < last) & (b >= 0) & (b < groups))
                def _():
                    h = carried(j, q)
                    piece_arrived(s, b, q, h)
                    lift(s, b, q, h)
                    over(s, b, q, h)
                    to_core(s, b, q, h)

    def side_from(j, d):
        s = 2 * j + core
        for q in range(2):
            for b in (z - d, z + d):
                @pl.when((s < last) & (b >= 0) & (b < groups))
                def _():
                    h = 1 - carried(j, q)
                    piece_arrived(s, b, q, h)
                    to_core(s, b, q, h)

    def twin(j):
        s = 2 * j + 1 - core
        for b in range(groups):
            @pl.when((s < last) | (b == z))
            def _():
                for q in range(2):
                    for h in range(2):
                        piece_arrived(s, b, q, h)

    def start_part(e, c):
        return amps.at[0, e, rows_of(c), :]

    def start_move(e, c, send, **where):
        return remote(start_part(e, c), start_part(e, c), send.at[c], start_recv.at[e, c], **where)

    def start_relay(e, c):
        @pl.when(has_up & (c <= z))
        def _():
            start_move(e, c, start_up, ch=z + 1).start()

        @pl.when(has_down & (c >= z))
        def _():
            start_move(e, c, start_down, ch=z - 1).start()

    def start_arrive_and_relay(e, c):
        @pl.when((c >= 0) & (c < groups))
        def _():
            start_move(e, c, start_up, sec=partner).wait_recv()
            start_relay(e, c)

    loads = [
        pltpu.make_async_copy(own_block, basis.at[k, rows_of(z), :], local_sem.at[0]),
        pltpu.make_async_copy(
            start.at[:, :, pl.ds(pl.multiple_of(k * width, width), width)],
            amps.at[0, :, rows_of(z), pl.ds(0, width)], local_sem.at[1]),
        pltpu.make_async_copy(
            start.at[:, :, pl.ds(pl.multiple_of(half_cols + k * width, width), width)],
            amps.at[0, :, rows_of(z), pl.ds(width, width)], local_sem.at[2]),
        pltpu.make_async_copy(limits, bounds.at[k, z], local_sem.at[3]),
    ]
    for load in loads:
        load.start()

    barrier = pltpu.get_barrier_semaphore()

    @pl.loop(1, devices)
    def _(step):
        pl.semaphore_signal(barrier, inc=1, device_id=other(step), device_id_type=pl.DeviceIdType.MESH)

    pl.semaphore_wait(barrier, devices - 1)
    loads[0].wait()

    give_own()
    for load in loads[1:]:
        load.wait()

    def bound_move(step):
        return pltpu.make_async_remote_copy(
            src_ref=bounds.at[k, z], dst_ref=bounds.at[k, z], send_sem=bound_send.at[step], recv_sem=bound_recv.at[k, z],
            device_id=other(step), device_id_type=pl.DeviceIdType.MESH,
        )

    @pl.loop(1, devices)
    def _(step):
        bound_move(step).start()

    def angles(s):
        for c in range(groups):
            @pl.when((s != k) | (c != z))
            def _():
                remote(bounds.at[s, c], bounds.at[s, c], bound_send.at[0], bound_recv.at[s, c], sec=partner).wait_recv()

        floor = jnp.concatenate([bounds[s, c] for c in range(groups)], axis=0)
        for e in range(energy_count):
            wavenumber = jnp.sqrt(energies[e] - floor)
            cosine = jnp.cos(wavenumber)
            sine_term = jnp.sin(wavenumber)
            filler = jnp.zeros((LANES - 3 * chunks, LANES), jnp.float32)
            stacked = jnp.concatenate(
                [cosine, sine_term / wavenumber, -wavenumber * sine_term, filler], axis=0
            )
            turn[s, e] = stacked.T

    def advance(s, e):
        source = jnp.minimum(s, 1)
        factors = turn[s, e]
        for q in range(chunks):
            place = pl.ds(q * LANES, LANES)
            both = amps[source, e, place, :].astype(jnp.float32)
            values_part, slopes_part = both[:, :width], both[:, width:]
            keep = factors[:, q : q + 1]
            rise = factors[:, chunks + q : chunks + q + 1]
            fall = factors[:, 2 * chunks + q : 2 * chunks + q + 1]
            rotated[place, pl.ds(0, width)] = (keep * values_part + rise * slopes_part).astype(jnp.bfloat16)
            rotated[place, pl.ds(width, width)] = (fall * values_part + keep * slopes_part).astype(jnp.bfloat16)

        @pl.when(s < last)
        def _():
            amps[1, e] = jnp.dot(basis[s], rotated[...], preferred_element_type=jnp.float32).astype(jnp.bfloat16)
            mine = amps[1, e, rows_of(z), :]
            kept[s, 0, e] = mine[:, :width]
            kept[s, 1, e] = mine[:, width:]

        @pl.when(s == last)
        def _():
            mine = jnp.dot(
                basis[s, rows_of(z), :], rotated[...], preferred_element_type=jnp.float32
            ).astype(jnp.bfloat16)
            kept[s, 0, e] = mine[:, :width]
            kept[s, 1, e] = mine[:, width:]

    def send_out(s, e):
        for half in range(2):
            columns = pl.ds(pl.multiple_of(half * half_cols + k * width, width), width)

            @pl.when(s == k)
            def _():
                pltpu.make_async_copy(kept.at[s, half, e], out.at[e, :, columns], out_local.at[0]).start()

            @pl.when(s != k)
            def _():
                remote(kept.at[s, half, e], out.at[e, :, columns], out_send.at[s], out_recv.at[k], sec=s).start()

    radix = max(sectors, energy_count, groups) + 1
    codes = [(kind * radix + first) * radix + second for kind, first, second in (*order, (END, 0, 0))]
    room = (END + 1) * radix * radix
    packed = 2 if room**2 < 2**30 else 1
    packed = 3 if room**3 < 2**30 else packed
    words = [
        sum(code * room**place for place, code in enumerate(codes[at : at + packed]))
        for at in range(0, len(codes), packed)
    ]

    def entry(n):
        word = jnp.int32(words[-1])
        for at, value in enumerate(words[:-1]):
            word = jnp.where(n // packed == at, value, word)
        code = word % room
        for place in range(1, packed):
            code = jnp.where(n % packed == place, word // room**place % room, code)
        return code // radix**2, code // radix % radix, code % radix

    def act(n, before):
        kind, first, second = entry(n)

        @pl.when(kind == STEP)
        def _():
            advance(first, second)

        @pl.when(kind == ANGLES)
        def _():
            angles(first)

        @pl.when(kind == HOME)
        def _():
            home(first)

        @pl.when(kind == LIFT)
        def _():
            lift_own(first)

        @pl.when(kind == HOP)
        def _():
            hop_from(first, second)

        @pl.when(kind == SIDE)
        def _():
            side_from(first, second)

        @pl.when(kind == TWIN)
        def _():
            twin(first)

        @pl.when(kind == FEED)
        def _():
            start_relay(first, z)

        @pl.when(kind == FEED_HOP)
        def _():
            start_arrive_and_relay(first, z - second)
            start_arrive_and_relay(first, z + second)

        @pl.when(before[0] == STEP)
        def _():
            send_out(before[1], before[2])

        return kind, first, second

    lax.fori_loop(0, len(codes), act, (jnp.int32(END), jnp.int32(0), jnp.int32(0)))

    @pl.loop(1, devices)
    def _(step):
        bound_move(step).wait_send()

    def drain(send, s, b, count, **where):
        part = part_of(s, 0, 0, 0, count)
        remote(part, part, send.at[s // 2, b], block_recv.at[s, b, 0], **where).wait_send()

    @pl.loop(0, pairs)
    def _(j):
        s = 2 * j + core
        for b in range(groups):
            @pl.when((s < last) | (b == z))
            def _():
                drain(core_send, s, b, 4, sec=partner)

            @pl.when((s < last) & has_up & (b <= z))
            def _():
                drain(up_send, s, b, 2, ch=z + 1)

            @pl.when((s < last) & has_down & (b >= z))
            def _():
                drain(down_send, s, b, 2, ch=z - 1)

            for send, target, turned in ((row_send, row_peer, 0), (column_send, column_peer, 1)):
                @pl.when((b == z) & (chip == j))
                def _():
                    drain(send, s, b, 4, sec=target)

                @pl.when((b == z) & (chip != j) & near(j, turned))
                def _():
                    drain(send, s, b, 2, sec=target)

                @pl.when((b != z) & (s < last))
                def _():
                    drain(send, s, b, 1, sec=target)

    for c in range(groups):
        span = amps.at[0, :, pl.ds(c * row_count, row_count), :]

        @pl.when(has_up & (c <= z))
        def _():
            remote(span, span, start_up.at[c], start_recv.at[0, 0], ch=z + 1).wait_send()

        @pl.when(has_down & (c >= z))
        def _():
            remote(span, span, start_down.at[c], start_recv.at[0, 0], ch=z - 1).wait_send()

    @pl.loop(0, sectors)
    def _(s):
        whole = remote(kept.at[s], kept.at[s], out_send.at[s], out_recv.at[s], sec=partner)

        @pl.when(s != k)
        def _():
            whole.wait_send()
            whole.wait_recv()

        @pl.when(s == k)
        def _():
            pltpu.make_async_copy(kept.at[s], kept.at[s], out_local.at[0]).wait()


def per_device_swept(start_amps, energies, thresholds, intersection):
    sectors = lax.axis_size("sec")
    groups = lax.axis_size("ch")
    energy_count, row_count, width_cols = start_amps.shape
    channel_count = intersection.shape[2]
    width = width_cols // 2 // sectors
    pairs = sectors // 2
    limits = thresholds.reshape(row_count // LANES, LANES).astype(jnp.float32)
    dma = pltpu.SemaphoreType.DMA
    stored = jax.ShapeDtypeStruct(start_amps.shape, jnp.bfloat16)
    swept = pl.pallas_call(
        functools.partial(sweep_kernel, sectors, groups),
        out_shape=stored,
        in_specs=[
            pl.BlockSpec(memory_space=pl.ANY),
            pl.BlockSpec(memory_space=pltpu.SMEM),
            pl.BlockSpec(memory_space=pl.ANY),
            pl.BlockSpec(memory_space=pl.ANY),
        ],
        out_specs=pl.BlockSpec(memory_space=pl.ANY),
        scratch_shapes=[
            pltpu.VMEM((sectors, channel_count, channel_count), jnp.bfloat16),
            pltpu.VMEM((2, energy_count, channel_count, 2 * width), jnp.bfloat16),
            pltpu.VMEM((channel_count, 2 * width), jnp.bfloat16),
            pltpu.VMEM((sectors, 2, energy_count, row_count, width), jnp.bfloat16),
            pltpu.VMEM((sectors, energy_count, LANES, LANES), jnp.float32),
            pltpu.VMEM((sectors, groups, row_count // LANES, LANES), jnp.float32),
            dma((4,)),
            dma((sectors, groups, 4)),
            dma((pairs, groups)),
            dma((pairs, groups)),
            dma((pairs, groups)),
            dma((pairs, groups)),
            dma((pairs, groups)),
            dma((energy_count, groups)),
            dma((groups,)),
            dma((groups,)),
            dma((sectors * groups,)),
            dma((sectors, groups)),
            dma((sectors,)),
            dma((sectors,)),
            dma((1,)),
        ],
        compiler_params=pltpu.CompilerParams(
            collective_id=0, has_side_effects=True, vmem_limit_bytes=60 * 2**20
        ),
    )(start_amps, energies, limits, intersection[0])
    return swept[None]


GATHERED_LIMIT = 24 * 2**20


def per_device(start_amps, energies, thresholds, intersection):
    sectors = lax.axis_size("sec")
    row_count, channel_count = intersection.shape[1:]
    gathered_bytes = sectors * channel_count**2 * intersection.dtype.itemsize
    even = sectors // 2 == 4 and (start_amps.shape[2] // 2) % (sectors * LANES) == 0
    even = even and row_count % (4 * 16) == 0 and row_count % LANES == 0 and 3 * (channel_count // LANES) <= LANES
    if even and gathered_bytes <= GATHERED_LIMIT:
        return per_device_swept(start_amps, energies, thresholds, intersection)
    return per_device_pipelined(start_amps, energies, thresholds, intersection)


def solution(mesh):
    in_specs = (P(None, "ch", None), P(), P("sec", "ch"), P("sec", "ch", None))
    out_specs = P("sec", None, "ch", None)
    return jax.shard_map(
        per_device, mesh=mesh, in_specs=in_specs, out_specs=out_specs, check_vma=False
    )
```

```python
import functools
import math
import jax
import jax.numpy as jnp
from jax import lax
from jax.experimental import pallas as pl
from jax.experimental.pallas import tpu as pltpu
from jax.sharding import PartitionSpec as P


def passed_along(value, axis, steps):
    count = lax.axis_size(axis)
    leading, last = (max(0, -steps), min(count, count - steps))
    return lax.ppermute(value, axis, [(source, source + steps) for source in range(leading, last)])


def per_device_pipelined(start_amps, energies, thresholds, intersection):
    sectors = lax.axis_size("sec")
    sector_index = lax.axis_index("sec")
    groups = lax.axis_size("ch")
    energy_count = energies.shape[0]
    step_count = sectors + energy_count - 1
    row_count = intersection.shape[1]
    width_cols = start_amps.shape[2]
    half_cols = width_cols // 2
    col_width = half_cols // groups
    intersection_whole, thresholds_whole = (
        lax.all_gather(intersection, "ch", axis=1, tiled=True),
        lax.all_gather(thresholds, "ch", axis=1, tiled=True),
    )
    basis_change = intersection_whole[0]
    channel_thresholds = thresholds_whole[0].astype(jnp.float32)
    channel_count = basis_change.shape[0]
    paired = start_amps.reshape(energy_count, row_count, 2, half_cols)
    start_cols = lax.all_to_all(paired, "ch", split_axis=3, concat_axis=1, tiled=True)
    stored_init = jnp.zeros((energy_count, channel_count, 2, col_width), jnp.bfloat16)

    def multiply(flat):
        return jnp.dot(basis_change, flat, preferred_element_type=jnp.float32).astype(jnp.bfloat16)

    def skipped(flat):
        return jnp.zeros((channel_count, 2 * col_width), jnp.bfloat16)

    def step(step_index, state_pair):
        outgoing, stored = state_pair
        incoming = passed_along(outgoing, "sec", 1)
        energy_raw = step_index - sector_index
        active = (energy_raw >= 0) & (energy_raw < energy_count)
        energy_slot = jnp.clip(energy_raw, 0, energy_count - 1)
        initial = lax.dynamic_index_in_dim(start_cols, energy_slot, 0, keepdims=False)
        source = jnp.where(sector_index == 0, initial, incoming).astype(jnp.float32)
        wavenumber = jnp.sqrt(energies[energy_slot] - channel_thresholds)[:, None]
        values_part = source[:, 0, :]
        slopes_part = source[:, 1, :]
        cosine = jnp.cos(wavenumber)
        sine_term = jnp.sin(wavenumber)
        new_values = cosine * values_part + sine_term / wavenumber * slopes_part
        new_slopes = -wavenumber * sine_term * values_part + cosine * slopes_part
        rotated = jnp.stack([new_values, new_slopes], axis=1).astype(jnp.bfloat16)
        flat = rotated.reshape(channel_count, 2 * col_width)
        fresh = lax.cond(active, multiply, skipped, flat)
        fresh = fresh.reshape(channel_count, 2, col_width)
        previous = lax.dynamic_index_in_dim(stored, energy_slot, 0, keepdims=False)
        kept = jnp.where(active, fresh, previous)
        stored = lax.dynamic_update_index_in_dim(stored, kept, energy_slot, 0)
        return (fresh, stored)

    outgoing_init = jnp.zeros((channel_count, 2, col_width), jnp.bfloat16)
    final_pair = lax.fori_loop(0, step_count, step, (outgoing_init, stored_init))
    returned = lax.all_to_all(final_pair[1], "ch", split_axis=1, concat_axis=3, tiled=True)
    return returned.reshape(energy_count, row_count, width_cols)[None]


LANES = 128
PAIRED = 2
HOME, LIFT, HOP, SIDE, TWIN, FEED, FEED_HOP, STEP, ANGLES, END = range(10)
TUNED = (
    (5, 0, 0), (5, 3, 0), (6, 0, 1), (5, 1, 0), (6, 0, 2), (0, 1, 0), (1, 1, 0), (0, 2, 0), (1, 2, 0), (0, 0, 0),
    (2, 1, 1), (2, 2, 1), (2, 2, 2), (1, 0, 0), (0, 3, 0), (2, 1, 2), (2, 0, 1), (2, 2, 3), (3, 1, 2), (2, 1, 3),
    (2, 0, 2), (2, 0, 3), (3, 2, 1), (3, 1, 3), (1, 3, 0), (3, 2, 2), (3, 0, 2), (3, 0, 3), (3, 2, 3), (3, 1, 1),
    (3, 0, 1), (2, 3, 1), (4, 1, 0), (2, 3, 2), (6, 1, 1), (2, 3, 3), (3, 3, 2), (6, 0, 3), (4, 2, 0), (4, 0, 0),
    (6, 1, 2), (3, 3, 3), (3, 3, 1), (6, 1, 3), (7, 0, 0), (7, 1, 0), (7, 2, 0), (7, 3, 0), (7, 4, 0), (7, 5, 0),
    (4, 3, 0), (5, 2, 0), (7, 6, 0), (6, 3, 1), (6, 3, 2), (7, 7, 0), (6, 2, 1), (5, 4, 0), (6, 3, 3), (6, 2, 2),
    (5, 5, 0), (6, 2, 3), (7, 0, 1), (6, 4, 1), (7, 1, 1), (7, 2, 1), (7, 3, 1), (7, 4, 1), (6, 4, 2), (7, 5, 1),
    (7, 6, 1), (6, 4, 3), (6, 5, 1), (7, 7, 1), (6, 5, 2), (6, 5, 3), (7, 0, 2), (7, 1, 2), (7, 2, 2), (7, 3, 2),
    (7, 4, 2), (7, 5, 2), (7, 6, 2), (7, 7, 2),
)


def plain_order(pairs, sectors, energy_count, groups):
    order = [(HOME, j, 0) for j in range(pairs)]
    order += [(FEED, e, 0) for e in range(energy_count)] + [(LIFT, j, 0) for j in range(pairs)]
    for tick in range(pairs + groups):
        for d in range(groups - 1, 0, -1):
            if 0 <= tick - d < pairs:
                order.append((HOP, tick - d, d))
            if 0 <= tick - d - 1 < pairs:
                order.append((SIDE, tick - d - 1, d))
    order += [(TWIN, j, 0) for j in range(pairs)]
    for e in range(energy_count):
        order += [(FEED_HOP, e, d) for d in range(1, groups)]
        if (e + 1) % PAIRED == 0:
            order += [(STEP, s, e // PAIRED) for s in range(sectors)]
    return order


def order_of(pairs, sectors, energy_count, groups):
    plain = plain_order(pairs, sectors, energy_count, groups)
    chosen = TUNED if sorted(TUNED) == sorted(plain) else plain
    order, left = [], list(range(sectors))
    for entry in chosen:
        while left and entry[0] == STEP:
            order.append((ANGLES, left.pop(0), 0))
        order.append(entry)
        if left:
            order.append((ANGLES, left.pop(0), 0))
    return order


def cos_and_sin(w):
    u = (w - jnp.float32(1.57079637050628662109375)) + jnp.float32(4.37113900018624283e-8)
    square = u * u
    odd = even = None
    for power in range(12, -1, -2):
        even = (0.0 if even is None else even * square) + (-1.0) ** (power // 2) / math.factorial(power)
        odd = (0.0 if odd is None else odd * square) + (-1.0) ** (power // 2) / math.factorial(power + 1)
    return -u * odd, even


def sweep_kernel(
    sectors, groups, start, energies, limits, own_block, out,
    basis, amps, rotated, kept, turn, bounds,
    local_sem, block_recv, column_send, row_send, up_send, down_send, core_send,
    start_recv, start_up, start_down, bound_send, bound_recv, out_send, out_recv, out_local,
):
    k = lax.axis_index("sec")
    z = lax.axis_index("ch")
    core = k % 2
    chip = k // 2
    column, row = chip % 2, chip // 2
    partner = k + 1 - 2 * core
    column_peer = k + 2 - 4 * column
    row_peer = k + 4 - 8 * row
    pairs = sectors // 2
    last = sectors - 1
    energy_count, row_count, width_cols = start.shape
    half_cols = width_cols // 2
    width = half_cols // sectors
    channel_count = row_count * groups
    chunks = channel_count // LANES
    devices = sectors * groups
    has_up = z + 1 < groups
    has_down = z >= 1
    piece = row_count // 4
    order = order_of(pairs, sectors, energy_count, groups)

    def remote(src, dst, send, recv, **where):
        return pltpu.make_async_remote_copy(
            src_ref=src, dst_ref=dst, send_sem=send, recv_sem=recv,
            device_id=where, device_id_type=pl.DeviceIdType.MESH,
        )

    def rows_of(c):
        return pl.ds(pl.multiple_of(c * row_count, row_count), row_count)

    def other(step):
        place = (k * groups + z + step) % devices
        return {"sec": place // groups, "ch": place % groups}

    def part_of(s, b, q, h, count=1):
        return basis.at[s, pl.ds(pl.multiple_of(b * row_count + (2 * q + h) * piece, piece), count * piece), :]

    def piece_move(s, b, q, h, send, **where):
        part = part_of(s, b, q, h)
        return remote(part, part, send.at[s // 2, b], block_recv.at[s, b, 2 * q + h], **where)

    def near(j, q):
        return row == j // 2 if q == 0 else column == j % 2

    def carried(j, q):
        return jnp.where(near(j, q), 0, 1)

    def lift(s, b, q, h):
        @pl.when((s < last) & has_up & (b <= z))
        def _():
            piece_move(s, b, q, h, up_send, ch=z + 1).start()

        @pl.when((s < last) & has_down & (b >= z))
        def _():
            piece_move(s, b, q, h, down_send, ch=z - 1).start()

    def over(s, b, q, h):
        if q == 0:
            piece_move(s, b, q, h, row_send, sec=row_peer).start()
        else:
            piece_move(s, b, q, h, column_send, sec=column_peer).start()

    def to_core(s, b, q, h):
        piece_move(s, b, q, h, core_send, sec=partner).start()

    def piece_arrived(s, b, q, h):
        piece_move(s, b, q, h, core_send, sec=partner).wait_recv()

    def give_own():
        for h in (1, 0):
            for q in range(2):
                piece_move(k, z, q, h, column_send, sec=column_peer).start()
                piece_move(k, z, q, h, row_send, sec=row_peer).start()
        for h in (1, 0):
            for q in range(2):
                to_core(k, z, q, h)

    def home(j):
        s = 2 * j + core

        @pl.when(chip != j)
        def _():
            for h in (1, 0):
                for q in range(2):
                    piece_arrived(s, z, q, h)

                    @pl.when(near(j, q))
                    def _():
                        over(s, z, q, h)

                    to_core(s, z, q, h)

    def lift_own(j):
        for q in range(2):
            lift(2 * j + core, z, q, carried(j, q))

    def hop_from(j, d):
        s = 2 * j + core
        for q in range(2):
            for b in (z - d, z + d):
                @pl.when((s < last) & (b >= 0) & (b < groups))
                def _():
                    h = carried(j, q)
                    piece_arrived(s, b, q, h)
                    lift(s, b, q, h)
                    over(s, b, q, h)
                    to_core(s, b, q, h)

    def side_from(j, d):
        s = 2 * j + core
        for q in range(2):
            for b in (z - d, z + d):
                @pl.when((s < last) & (b >= 0) & (b < groups))
                def _():
                    h = 1 - carried(j, q)
                    piece_arrived(s, b, q, h)
                    to_core(s, b, q, h)

    def twin(j):
        s = 2 * j + 1 - core
        for b in range(groups):
            @pl.when((s < last) | (b == z))
            def _():
                for q in range(2):
                    for h in range(2):
                        piece_arrived(s, b, q, h)

    def start_part(e, c):
        return amps.at[0, e, rows_of(c), :]

    def start_move(e, c, send, **where):
        return remote(start_part(e, c), start_part(e, c), send.at[c], start_recv.at[e, c], **where)

    def start_relay(e, c):
        @pl.when(has_up & (c <= z))
        def _():
            start_move(e, c, start_up, ch=z + 1).start()

        @pl.when(has_down & (c >= z))
        def _():
            start_move(e, c, start_down, ch=z - 1).start()

    def start_arrive_and_relay(e, c):
        @pl.when((c >= 0) & (c < groups))
        def _():
            start_move(e, c, start_up, sec=partner).wait_recv()
            start_relay(e, c)

    bounds[k, z] = jnp.concatenate(
        [limits[:, q * LANES : (q + 1) * LANES] for q in range(row_count // LANES)], axis=0
    ).astype(jnp.float32)
    loads = [
        pltpu.make_async_copy(own_block, basis.at[k, rows_of(z), :], local_sem.at[0]),
        pltpu.make_async_copy(
            start.at[:, :, pl.ds(pl.multiple_of(k * width, width), width)],
            amps.at[0, :, rows_of(z), pl.ds(0, width)], local_sem.at[1]),
        pltpu.make_async_copy(
            start.at[:, :, pl.ds(pl.multiple_of(half_cols + k * width, width), width)],
            amps.at[0, :, rows_of(z), pl.ds(width, width)], local_sem.at[2]),
    ]
    for load in loads:
        load.start()

    barrier = pltpu.get_barrier_semaphore()

    @pl.loop(1, devices)
    def _(step):
        pl.semaphore_signal(barrier, inc=1, device_id=other(step), device_id_type=pl.DeviceIdType.MESH)

    pl.semaphore_wait(barrier, devices - 1)
    loads[0].wait()

    give_own()
    for load in loads[1:]:
        load.wait()

    def bound_move(step):
        return pltpu.make_async_remote_copy(
            src_ref=bounds.at[k, z], dst_ref=bounds.at[k, z], send_sem=bound_send.at[step], recv_sem=bound_recv.at[k, z],
            device_id=other(step), device_id_type=pl.DeviceIdType.MESH,
        )

    @pl.loop(1, devices)
    def _(step):
        bound_move(step).start()

    def angles(s):
        for c in range(groups):
            @pl.when((s != k) | (c != z))
            def _():
                remote(bounds.at[s, c], bounds.at[s, c], bound_send.at[0], bound_recv.at[s, c], sec=partner).wait_recv()

        floor = jnp.concatenate([bounds[s, c] for c in range(groups)], axis=0)
        wavenumber = jnp.concatenate([jnp.sqrt(energies[e] - floor) for e in range(energy_count)], axis=0)
        cosine, sine = cos_and_sin(wavenumber)
        shear, turned = (1.0 - cosine) / (wavenumber * sine), -wavenumber * sine
        for e in range(energy_count):
            own = slice(e * chunks, (e + 1) * chunks)
            turn[s, e] = jnp.concatenate([shear[own], turned[own]], axis=0).T

    def rotate(s, e, m):
        source = jnp.minimum(s, 1)
        factors = turn[s, e]
        for q in range(chunks):
            place = pl.ds(q * LANES, LANES)
            both = amps[source, e, place, :].astype(jnp.float32)
            shear, turned = factors[:, q : q + 1], factors[:, chunks + q : chunks + q + 1]
            values_part, slopes_part = both[:, :width], both[:, width:]
            values_part = values_part + shear * slopes_part
            slopes_part = slopes_part + turned * values_part
            values_part = values_part + shear * slopes_part
            rotated[m, place, pl.ds(0, width)] = values_part.astype(jnp.bfloat16)
            rotated[m, place, pl.ds(width, width)] = slopes_part.astype(jnp.bfloat16)

    def keep(s, e, mine):
        kept[s, 0, e] = mine[:, :width]
        kept[s, 1, e] = mine[:, width:]

    def advance(s, group):
        @pl.when(s < last)
        def _():
            for m in range(PAIRED):
                rotate(s, PAIRED * group + m, m)
            for m in range(PAIRED):
                e = PAIRED * group + m
                amps[1, e] = jnp.dot(basis[s], rotated[m], preferred_element_type=jnp.float32).astype(jnp.bfloat16)
            for m in range(PAIRED):
                e = PAIRED * group + m
                keep(s, e, amps[1, e, rows_of(z), :])

        @pl.when(s == last)
        def _():
            for m in range(PAIRED):
                rotate(s, PAIRED * group + m, m)
            for m in range(PAIRED):
                mine = jnp.dot(basis[s, rows_of(z), :], rotated[m], preferred_element_type=jnp.float32)
                keep(s, PAIRED * group + m, mine.astype(jnp.bfloat16))

    def send_out(s, e):
        for half in range(2):
            columns = pl.ds(pl.multiple_of(half * half_cols + k * width, width), width)

            @pl.when(s == k)
            def _():
                pltpu.make_async_copy(kept.at[s, half, e], out.at[e, :, columns], out_local.at[0]).start()

            @pl.when(s != k)
            def _():
                remote(kept.at[s, half, e], out.at[e, :, columns], out_send.at[s], out_recv.at[k], sec=s).start()

    bits = max(sectors - 1, energy_count - 1, groups - 1).bit_length()
    span = 2 * bits + END.bit_length()
    packed = max(1, 30 // span)
    codes = [(kind << 2 * bits) | (first << bits) | second for kind, first, second in (*order, (END, 0, 0))]
    words = [
        sum(code << span * place for place, code in enumerate(codes[at : at + packed]))
        for at in range(0, len(codes), packed)
    ]
    low = 2**bits

    def entry(at, place):
        values = words
        while len(values) > 1:
            odd = (at & 1) == 1
            values = [
                jnp.where(odd, values[i + 1], values[i]) if i + 1 < len(values) else values[i]
                for i in range(0, len(values), 2)
            ]
            at = lax.shift_right_logical(at, jnp.int32(1))
        word = values[0]
        for step in range(1, packed):
            word = jnp.where(place == step, lax.shift_right_logical(values[0], jnp.int32(span * step)), word)
        word = word & (2**span - 1)
        return (
            lax.shift_right_logical(word, jnp.int32(2 * bits)),
            lax.shift_right_logical(word, jnp.int32(bits)) & (low - 1),
            word & (low - 1),
        )

    def act(n, before):
        at, place = before[3:]
        kind, first, second = entry(at, place)
        wrapped = place == packed - 1

        @pl.when(kind == STEP)
        def _():
            advance(first, second)

        @pl.when(kind == ANGLES)
        def _():
            angles(first)

        @pl.when(kind == HOME)
        def _():
            home(first)

        @pl.when(kind == LIFT)
        def _():
            lift_own(first)

        @pl.when(kind == HOP)
        def _():
            hop_from(first, second)

        @pl.when(kind == SIDE)
        def _():
            side_from(first, second)

        @pl.when(kind == TWIN)
        def _():
            twin(first)

        @pl.when(kind == FEED)
        def _():
            start_relay(first, z)

        @pl.when(kind == FEED_HOP)
        def _():
            start_arrive_and_relay(first, z - second)
            start_arrive_and_relay(first, z + second)

        @pl.when(before[0] == STEP)
        def _():
            for m in range(PAIRED):
                send_out(before[1], PAIRED * before[2] + m)

        return kind, first, second, jnp.where(wrapped, at + 1, at), jnp.where(wrapped, 0, place + 1)

    lax.fori_loop(0, len(codes), act, (jnp.int32(END),) + (jnp.int32(0),) * 4)

    @pl.loop(1, devices)
    def _(step):
        bound_move(step).wait_send()

    def drain(send, s, b, count, **where):
        part = part_of(s, 0, 0, 0, count)
        remote(part, part, send.at[s // 2, b], block_recv.at[s, b, 0], **where).wait_send()

    @pl.loop(0, pairs)
    def _(j):
        s = 2 * j + core
        for b in range(groups):
            @pl.when((s < last) | (b == z))
            def _():
                drain(core_send, s, b, 4, sec=partner)

            @pl.when((s < last) & has_up & (b <= z))
            def _():
                drain(up_send, s, b, 2, ch=z + 1)

            @pl.when((s < last) & has_down & (b >= z))
            def _():
                drain(down_send, s, b, 2, ch=z - 1)

            for send, target, turned in ((row_send, row_peer, 0), (column_send, column_peer, 1)):
                @pl.when((b == z) & (chip == j))
                def _():
                    drain(send, s, b, 4, sec=target)

                @pl.when((b == z) & (chip != j) & near(j, turned))
                def _():
                    drain(send, s, b, 2, sec=target)

                @pl.when((b != z) & (s < last))
                def _():
                    drain(send, s, b, 1, sec=target)

    for c in range(groups):
        span = amps.at[0, :, pl.ds(c * row_count, row_count), :]

        @pl.when(has_up & (c <= z))
        def _():
            remote(span, span, start_up.at[c], start_recv.at[0, 0], ch=z + 1).wait_send()

        @pl.when(has_down & (c >= z))
        def _():
            remote(span, span, start_down.at[c], start_recv.at[0, 0], ch=z - 1).wait_send()

    @pl.loop(0, sectors)
    def _(s):
        whole = remote(kept.at[s], kept.at[s], out_send.at[s], out_recv.at[s], sec=partner)

        @pl.when(s != k)
        def _():
            whole.wait_send()
            whole.wait_recv()

        @pl.when(s == k)
        def _():
            pltpu.make_async_copy(kept.at[s], kept.at[s], out_local.at[0]).wait()


def per_device_swept(start_amps, energies, thresholds, intersection):
    sectors = lax.axis_size("sec")
    groups = lax.axis_size("ch")
    energy_count, row_count, width_cols = start_amps.shape
    channel_count = intersection.shape[2]
    width = width_cols // 2 // sectors
    pairs = sectors // 2
    dma = pltpu.SemaphoreType.DMA
    stored = pltpu.VMEM(start_amps.shape, jnp.bfloat16)
    swept = pl.pallas_call(
        functools.partial(sweep_kernel, sectors, groups),
        out_shape=stored,
        in_specs=[
            pl.BlockSpec(memory_space=pl.ANY),
            pl.BlockSpec(memory_space=pltpu.SMEM),
            pl.BlockSpec(memory_space=pltpu.VMEM),
            pl.BlockSpec(memory_space=pl.ANY),
        ],
        out_specs=pl.BlockSpec(memory_space=pltpu.VMEM),
        scratch_shapes=[
            pltpu.VMEM((sectors, channel_count, channel_count), jnp.bfloat16),
            pltpu.VMEM((2, energy_count, channel_count, 2 * width), jnp.bfloat16),
            pltpu.VMEM((PAIRED, channel_count, 2 * width), jnp.bfloat16),
            pltpu.VMEM((sectors, 2, energy_count, row_count, width), jnp.bfloat16),
            pltpu.VMEM((sectors, energy_count, LANES, 2 * (channel_count // LANES)), jnp.float32),
            pltpu.VMEM((sectors, groups, row_count // LANES, LANES), jnp.float32),
            dma((3,)),
            dma((sectors, groups, 4)),
            dma((pairs, groups)),
            dma((pairs, groups)),
            dma((pairs, groups)),
            dma((pairs, groups)),
            dma((pairs, groups)),
            dma((energy_count, groups)),
            dma((groups,)),
            dma((groups,)),
            dma((sectors * groups,)),
            dma((sectors, groups)),
            dma((sectors,)),
            dma((sectors,)),
            dma((1,)),
        ],
        compiler_params=pltpu.CompilerParams(
            collective_id=0, has_side_effects=True, vmem_limit_bytes=56 * 2**20
        ),
    )(start_amps, energies, thresholds, intersection[0])
    return swept[None]


GATHERED_LIMIT = 24 * 2**20


def per_device(start_amps, energies, thresholds, intersection):
    sectors = lax.axis_size("sec")
    row_count, channel_count = intersection.shape[1:]
    gathered_bytes = sectors * channel_count**2 * intersection.dtype.itemsize
    even = sectors // 2 == 4 and (start_amps.shape[2] // 2) % (sectors * LANES) == 0
    even = even and energies.shape[0] % PAIRED == 0 and row_count % (4 * 16) == 0 and row_count % LANES == 0 and 3 * (channel_count // LANES) <= LANES
    if even and gathered_bytes <= GATHERED_LIMIT:
        return per_device_swept(start_amps, energies, thresholds, intersection)
    return per_device_pipelined(start_amps, energies, thresholds, intersection)


def solution(mesh):
    in_specs = (P(None, "ch", None), P(), P("sec", "ch"), P("sec", "ch", None))
    out_specs = P("sec", None, "ch", None)
    return jax.shard_map(
        per_device, mesh=mesh, in_specs=in_specs, out_specs=out_specs, check_vma=False
    )
```

```python
import functools
import math
import jax
import jax.numpy as jnp
from jax import lax
from jax.experimental import pallas as pl
from jax.experimental.pallas import tpu as pltpu
from jax.sharding import PartitionSpec as P


def passed_along(value, axis, steps):
    count = lax.axis_size(axis)
    leading, last = (max(0, -steps), min(count, count - steps))
    return lax.ppermute(value, axis, [(source, source + steps) for source in range(leading, last)])


def per_device_pipelined(start_amps, energies, thresholds, intersection):
    sectors = lax.axis_size("sec")
    sector_index = lax.axis_index("sec")
    groups = lax.axis_size("ch")
    energy_count = energies.shape[0]
    step_count = sectors + energy_count - 1
    row_count = intersection.shape[1]
    width_cols = start_amps.shape[2]
    half_cols = width_cols // 2
    col_width = half_cols // groups
    intersection_whole, thresholds_whole = (
        lax.all_gather(intersection, "ch", axis=1, tiled=True),
        lax.all_gather(thresholds, "ch", axis=1, tiled=True),
    )
    basis_change = intersection_whole[0]
    channel_thresholds = thresholds_whole[0].astype(jnp.float32)
    channel_count = basis_change.shape[0]
    paired = start_amps.reshape(energy_count, row_count, 2, half_cols)
    start_cols = lax.all_to_all(paired, "ch", split_axis=3, concat_axis=1, tiled=True)
    stored_init = jnp.zeros((energy_count, channel_count, 2, col_width), jnp.bfloat16)

    def multiply(flat):
        return jnp.dot(basis_change, flat, preferred_element_type=jnp.float32).astype(jnp.bfloat16)

    def skipped(flat):
        return jnp.zeros((channel_count, 2 * col_width), jnp.bfloat16)

    def step(step_index, state_pair):
        outgoing, stored = state_pair
        incoming = passed_along(outgoing, "sec", 1)
        energy_raw = step_index - sector_index
        active = (energy_raw >= 0) & (energy_raw < energy_count)
        energy_slot = jnp.clip(energy_raw, 0, energy_count - 1)
        initial = lax.dynamic_index_in_dim(start_cols, energy_slot, 0, keepdims=False)
        source = jnp.where(sector_index == 0, initial, incoming).astype(jnp.float32)
        wavenumber = jnp.sqrt(energies[energy_slot] - channel_thresholds)[:, None]
        values_part = source[:, 0, :]
        slopes_part = source[:, 1, :]
        cosine = jnp.cos(wavenumber)
        sine_term = jnp.sin(wavenumber)
        new_values = cosine * values_part + sine_term / wavenumber * slopes_part
        new_slopes = -wavenumber * sine_term * values_part + cosine * slopes_part
        rotated = jnp.stack([new_values, new_slopes], axis=1).astype(jnp.bfloat16)
        flat = rotated.reshape(channel_count, 2 * col_width)
        fresh = lax.cond(active, multiply, skipped, flat)
        fresh = fresh.reshape(channel_count, 2, col_width)
        previous = lax.dynamic_index_in_dim(stored, energy_slot, 0, keepdims=False)
        kept = jnp.where(active, fresh, previous)
        stored = lax.dynamic_update_index_in_dim(stored, kept, energy_slot, 0)
        return (fresh, stored)

    outgoing_init = jnp.zeros((channel_count, 2, col_width), jnp.bfloat16)
    final_pair = lax.fori_loop(0, step_count, step, (outgoing_init, stored_init))
    returned = lax.all_to_all(final_pair[1], "ch", split_axis=1, concat_axis=3, tiled=True)
    return returned.reshape(energy_count, row_count, width_cols)[None]


LANES = 128
PAIRED = 2
QUARTERED = (0, 1)
HOME, LIFT, HOP, SIDE, TWIN, FEED, FEED_HOP, STEP, FAR, ANGLES, END = range(11)
TUNED = (
    (5, 0, 0), (6, 0, 1), (5, 1, 0), (6, 1, 1), (5, 2, 0), (0, 1, 0), (1, 1, 0), (0, 2, 0), (1, 2, 0), (0, 3, 0),
    (0, 0, 0), (2, 1, 1), (1, 0, 0), (2, 1, 2), (2, 0, 1), (3, 1, 2), (2, 0, 2), (3, 0, 1), (2, 0, 3), (2, 1, 3),
    (3, 1, 3), (1, 3, 0), (8, 1, 2), (6, 1, 2), (3, 0, 2), (3, 0, 3), (6, 1, 3), (2, 2, 1), (3, 1, 1), (2, 3, 1),
    (2, 3, 2), (8, 0, 1), (2, 3, 3), (8, 0, 3), (2, 2, 2), (8, 0, 2), (2, 2, 3), (6, 0, 2), (8, 1, 3), (3, 3, 1),
    (8, 1, 1), (6, 2, 1), (3, 2, 1), (6, 0, 3), (4, 0, 0), (7, 0, 0), (3, 3, 2), (3, 3, 3), (3, 2, 2), (5, 3, 0),
    (3, 2, 3), (7, 1, 0), (4, 1, 0), (7, 2, 0), (6, 2, 2), (7, 3, 0), (4, 3, 0), (4, 2, 0), (7, 4, 0), (7, 5, 0),
    (7, 6, 0), (6, 2, 3), (6, 3, 1), (7, 7, 0), (5, 4, 0), (6, 3, 2), (6, 4, 1), (6, 3, 3), (7, 0, 1), (7, 1, 1),
    (7, 2, 1), (6, 4, 2), (5, 5, 0), (7, 3, 1), (7, 4, 1), (7, 5, 1), (7, 6, 1), (6, 5, 1), (6, 5, 2), (6, 5, 3),
    (6, 4, 3), (7, 0, 2), (7, 1, 2), (7, 7, 1), (7, 2, 2), (7, 3, 2), (7, 4, 2), (7, 5, 2), (7, 6, 2), (7, 7, 2),
)


def plain_order(pairs, sectors, energy_count, groups):
    order = [(HOME, j, 0) for j in range(pairs)]
    order += [(FEED, e, 0) for e in range(energy_count)] + [(LIFT, j, 0) for j in range(pairs)]
    for tick in range(pairs + groups + 1):
        for d in range(groups - 1, 0, -1):
            if 0 <= tick - d < pairs:
                order.append((HOP, tick - d, d))
            if 0 <= tick - d - 1 < pairs:
                order.append((SIDE, tick - d - 1, d))
            if 0 <= tick - d - 2 < pairs and tick - d - 2 in QUARTERED:
                order.append((FAR, tick - d - 2, d))
    order += [(TWIN, j, 0) for j in range(pairs)]
    for e in range(energy_count):
        order += [(FEED_HOP, e, d) for d in range(1, groups)]
        if (e + 1) % PAIRED == 0:
            order += [(STEP, s, e // PAIRED) for s in range(sectors)]
    return order


def order_of(pairs, sectors, energy_count, groups):
    plain = plain_order(pairs, sectors, energy_count, groups)
    chosen = TUNED if sorted(TUNED) == sorted(plain) else plain
    order, left = [], list(range(sectors))
    for entry in chosen:
        while left and entry[0] == STEP:
            order.append((ANGLES, left.pop(0), 0))
        order.append(entry)
        if left:
            order.append((ANGLES, left.pop(0), 0))
    return order


def cos_and_sin(w):
    u = (w - jnp.float32(1.57079637050628662109375)) + jnp.float32(4.37113900018624283e-8)
    square = u * u
    odd = even = None
    for power in range(12, -1, -2):
        even = (0.0 if even is None else even * square) + (-1.0) ** (power // 2) / math.factorial(power)
        odd = (0.0 if odd is None else odd * square) + (-1.0) ** (power // 2) / math.factorial(power + 1)
    return -u * odd, even


def sweep_kernel(
    sectors, groups, start, energies, limits, own_block, out,
    basis, amps, rotated, kept, turn, bounds,
    local_sem, block_recv, column_send, row_send, up_send, down_send, core_send,
    start_recv, start_up, start_down, bound_send, bound_recv, out_send, out_recv, out_local,
):
    k = lax.axis_index("sec")
    z = lax.axis_index("ch")
    core = k % 2
    chip = k // 2
    column, row = chip % 2, chip // 2
    partner = k + 1 - 2 * core
    column_peer = k + 2 - 4 * column
    row_peer = k + 4 - 8 * row
    pairs = sectors // 2
    last = sectors - 1
    energy_count, row_count, width_cols = start.shape
    half_cols = width_cols // 2
    width = half_cols // sectors
    channel_count = row_count * groups
    chunks = channel_count // LANES
    devices = sectors * groups
    has_up = z + 1 < groups
    has_down = z >= 1
    piece = row_count // 4
    order = order_of(pairs, sectors, energy_count, groups)

    def remote(src, dst, send, recv, **where):
        return pltpu.make_async_remote_copy(
            src_ref=src, dst_ref=dst, send_sem=send, recv_sem=recv,
            device_id=where, device_id_type=pl.DeviceIdType.MESH,
        )

    def rows_of(c):
        return pl.ds(pl.multiple_of(c * row_count, row_count), row_count)

    def other(step):
        place = (k * groups + z + step) % devices
        return {"sec": place // groups, "ch": place % groups}

    def part_of(s, b, r, count=1):
        return basis.at[s, pl.ds(pl.multiple_of(b * row_count + r * piece, piece), count * piece), :]

    def piece_move(s, b, r, send, **where):
        part = part_of(s, b, r)
        return remote(part, part, send.at[s // 2, b], block_recv.at[s, b, r], **where)

    column_chip, row_chip = chip + 1 - 2 * column, chip + 2 - 4 * row

    def quartered(j):
        found = j < 0
        for pair in QUARTERED:
            found = found | (j == pair)
        return found

    def near(j, q):
        return row == j // 2 if q == 0 else column == j % 2

    def carried(j, q):
        return jnp.where(near(j, q), 2 * q, 2 * q + 1)

    def left_over(j, q):
        return jnp.where(near(j, q), 2 * q + 1, 2 * q)

    def lift(s, b, r):
        @pl.when((s < last) & has_up & (b <= z))
        def _():
            piece_move(s, b, r, up_send, ch=z + 1).start()

        @pl.when((s < last) & has_down & (b >= z))
        def _():
            piece_move(s, b, r, down_send, ch=z - 1).start()

    def to_column(s, b, r):
        piece_move(s, b, r, column_send, sec=column_peer).start()

    def to_row(s, b, r):
        piece_move(s, b, r, row_send, sec=row_peer).start()

    def to_core(s, b, r):
        piece_move(s, b, r, core_send, sec=partner).start()

    def piece_arrived(s, b, r):
        piece_move(s, b, r, core_send, sec=partner).wait_recv()

    def give_own():
        for r in (1, 3, 0, 2):
            to_column(k, z, r)
            to_row(k, z, r)
        for r in (1, 3, 0, 2):
            to_core(k, z, r)

    def home(j):
        s = 2 * j + core

        @pl.when(chip != j)
        def _():
            for r in (1, 3, 0, 2):
                piece_arrived(s, z, r)

                @pl.when(near(j, r // 2))
                def _():
                    (to_column if r // 2 else to_row)(s, z, r)

                to_core(s, z, r)

    def lift_own(j):
        @pl.when(quartered(j))
        def _():
            lift(2 * j + core, z, chip)

        @pl.when(~quartered(j))
        def _():
            for q in range(2):
                lift(2 * j + core, z, carried(j, q))

    def both_sides(j, d, action):
        s = 2 * j + core
        for b in (z - d, z + d):
            @pl.when((s < last) & (b >= 0) & (b < groups))
            def _():
                action(s, b)

    def hop_from(j, d):
        @pl.when(quartered(j))
        def _():
            def action(s, b):
                piece_arrived(s, b, chip)
                lift(s, b, chip)
                to_column(s, b, chip)
                to_row(s, b, chip)
                to_core(s, b, chip)

            both_sides(j, d, action)

        @pl.when(~quartered(j))
        def _():
            for q in range(2):
                def action(s, b):
                    r = carried(j, q)
                    piece_arrived(s, b, r)
                    lift(s, b, r)
                    (to_column if q else to_row)(s, b, r)
                    to_core(s, b, r)

                both_sides(j, d, action)

    def side_from(j, d):
        @pl.when(quartered(j))
        def _():
            def action(s, b):
                piece_arrived(s, b, column_chip)

                @pl.when(core == 1)
                def _():
                    to_row(s, b, column_chip)

                to_core(s, b, column_chip)
                piece_arrived(s, b, row_chip)

                @pl.when(core == 0)
                def _():
                    to_column(s, b, row_chip)

                to_core(s, b, row_chip)

            both_sides(j, d, action)

        @pl.when(~quartered(j))
        def _():
            for q in range(2):
                def action(s, b):
                    r = left_over(j, q)
                    piece_arrived(s, b, r)
                    to_core(s, b, r)

                both_sides(j, d, action)

    def far_from(j, d):
        def action(s, b):
            piece_arrived(s, b, 3 - chip)
            to_core(s, b, 3 - chip)

        both_sides(j, d, action)

    def twin(j):
        s = 2 * j + 1 - core
        for b in range(groups):
            @pl.when((s < last) | (b == z))
            def _():
                for r in range(4):
                    piece_arrived(s, b, r)

    def start_part(e, c):
        return amps.at[0, e, rows_of(c), :]

    def start_move(e, c, send, **where):
        return remote(start_part(e, c), start_part(e, c), send.at[c], start_recv.at[e, c], **where)

    def start_relay(e, c):
        @pl.when(has_up & (c <= z))
        def _():
            start_move(e, c, start_up, ch=z + 1).start()

        @pl.when(has_down & (c >= z))
        def _():
            start_move(e, c, start_down, ch=z - 1).start()

    def start_arrive_and_relay(e, c):
        @pl.when((c >= 0) & (c < groups))
        def _():
            start_move(e, c, start_up, sec=partner).wait_recv()
            start_relay(e, c)

    bounds[k, z] = jnp.concatenate(
        [limits[:, q * LANES : (q + 1) * LANES] for q in range(row_count // LANES)], axis=0
    ).astype(jnp.float32)
    loads = [
        pltpu.make_async_copy(own_block, basis.at[k, rows_of(z), :], local_sem.at[0]),
        pltpu.make_async_copy(
            start.at[:, :, pl.ds(pl.multiple_of(k * width, width), width)],
            amps.at[0, :, rows_of(z), pl.ds(0, width)], local_sem.at[1]),
        pltpu.make_async_copy(
            start.at[:, :, pl.ds(pl.multiple_of(half_cols + k * width, width), width)],
            amps.at[0, :, rows_of(z), pl.ds(width, width)], local_sem.at[2]),
    ]
    for load in loads:
        load.start()

    barrier = pltpu.get_barrier_semaphore()

    @pl.loop(1, devices)
    def _(step):
        pl.semaphore_signal(barrier, inc=1, device_id=other(step), device_id_type=pl.DeviceIdType.MESH)

    pl.semaphore_wait(barrier, devices - 1)
    loads[0].wait()

    give_own()
    for load in loads[1:]:
        load.wait()

    def bound_move(step):
        return pltpu.make_async_remote_copy(
            src_ref=bounds.at[k, z], dst_ref=bounds.at[k, z], send_sem=bound_send.at[step], recv_sem=bound_recv.at[k, z],
            device_id=other(step), device_id_type=pl.DeviceIdType.MESH,
        )

    @pl.loop(1, devices)
    def _(step):
        bound_move(step).start()

    def angles(s):
        for c in range(groups):
            @pl.when((s != k) | (c != z))
            def _():
                remote(bounds.at[s, c], bounds.at[s, c], bound_send.at[0], bound_recv.at[s, c], sec=partner).wait_recv()

        floor = jnp.concatenate([bounds[s, c] for c in range(groups)], axis=0)
        wavenumber = jnp.concatenate([jnp.sqrt(energies[e] - floor) for e in range(energy_count)], axis=0)
        cosine, sine = cos_and_sin(wavenumber)
        shear, turned = (1.0 - cosine) / (wavenumber * sine), -wavenumber * sine
        for e in range(energy_count):
            own = slice(e * chunks, (e + 1) * chunks)
            turn[s, e] = jnp.concatenate([shear[own], turned[own]], axis=0).T

    def rotate(s, e, m):
        source = jnp.minimum(s, 1)
        factors = turn[s, e]
        for q in range(chunks):
            place = pl.ds(q * LANES, LANES)
            both = amps[source, e, place, :].astype(jnp.float32)
            shear, turned = factors[:, q : q + 1], factors[:, chunks + q : chunks + q + 1]
            values_part, slopes_part = both[:, :width], both[:, width:]
            values_part = values_part + shear * slopes_part
            slopes_part = slopes_part + turned * values_part
            values_part = values_part + shear * slopes_part
            rotated[m, place, pl.ds(0, width)] = values_part.astype(jnp.bfloat16)
            rotated[m, place, pl.ds(width, width)] = slopes_part.astype(jnp.bfloat16)

    def keep(s, e, mine):
        kept[s, 0, e] = mine[:, :width]
        kept[s, 1, e] = mine[:, width:]

    def advance(s, group):
        @pl.when(s < last)
        def _():
            for m in range(PAIRED):
                rotate(s, PAIRED * group + m, m)
            for m in range(PAIRED):
                e = PAIRED * group + m
                amps[1, e] = jnp.dot(basis[s], rotated[m], preferred_element_type=jnp.float32).astype(jnp.bfloat16)
            for m in range(PAIRED):
                e = PAIRED * group + m
                keep(s, e, amps[1, e, rows_of(z), :])

        @pl.when(s == last)
        def _():
            for m in range(PAIRED):
                rotate(s, PAIRED * group + m, m)
            for m in range(PAIRED):
                mine = jnp.dot(basis[s, rows_of(z), :], rotated[m], preferred_element_type=jnp.float32)
                keep(s, PAIRED * group + m, mine.astype(jnp.bfloat16))

    def send_out(s, e):
        for half in range(2):
            columns = pl.ds(pl.multiple_of(half * half_cols + k * width, width), width)

            @pl.when(s == k)
            def _():
                pltpu.make_async_copy(kept.at[s, half, e], out.at[e, :, columns], out_local.at[0]).start()

            @pl.when(s != k)
            def _():
                remote(kept.at[s, half, e], out.at[e, :, columns], out_send.at[s], out_recv.at[k], sec=s).start()

    bits = max(sectors - 1, energy_count - 1, groups - 1).bit_length()
    span = 2 * bits + END.bit_length()
    packed = max(1, 30 // span)
    codes = [(kind << 2 * bits) | (first << bits) | second for kind, first, second in (*order, (END, 0, 0))]
    words = [
        sum(code << span * place for place, code in enumerate(codes[at : at + packed]))
        for at in range(0, len(codes), packed)
    ]
    low = 2**bits

    def entry(at, place):
        values = words
        while len(values) > 1:
            odd = (at & 1) == 1
            values = [
                jnp.where(odd, values[i + 1], values[i]) if i + 1 < len(values) else values[i]
                for i in range(0, len(values), 2)
            ]
            at = lax.shift_right_logical(at, jnp.int32(1))
        word = values[0]
        for step in range(1, packed):
            word = jnp.where(place == step, lax.shift_right_logical(values[0], jnp.int32(span * step)), word)
        word = word & (2**span - 1)
        return (
            lax.shift_right_logical(word, jnp.int32(2 * bits)),
            lax.shift_right_logical(word, jnp.int32(bits)) & (low - 1),
            word & (low - 1),
        )

    def act(n, before):
        at, place = before[3:]
        kind, first, second = entry(at, place)
        wrapped = place == packed - 1

        @pl.when(kind == STEP)
        def _():
            advance(first, second)

        @pl.when(kind == ANGLES)
        def _():
            angles(first)

        @pl.when(kind == HOME)
        def _():
            home(first)

        @pl.when(kind == LIFT)
        def _():
            lift_own(first)

        @pl.when(kind == HOP)
        def _():
            hop_from(first, second)

        @pl.when(kind == SIDE)
        def _():
            side_from(first, second)

        @pl.when(kind == FAR)
        def _():
            far_from(first, second)

        @pl.when(kind == TWIN)
        def _():
            twin(first)

        @pl.when(kind == FEED)
        def _():
            start_relay(first, z)

        @pl.when(kind == FEED_HOP)
        def _():
            start_arrive_and_relay(first, z - second)
            start_arrive_and_relay(first, z + second)

        @pl.when(before[0] == STEP)
        def _():
            for m in range(PAIRED):
                send_out(before[1], PAIRED * before[2] + m)

        return kind, first, second, jnp.where(wrapped, at + 1, at), jnp.where(wrapped, 0, place + 1)

    lax.fori_loop(0, len(codes), act, (jnp.int32(END),) + (jnp.int32(0),) * 4)

    @pl.loop(1, devices)
    def _(step):
        bound_move(step).wait_send()

    def drain(send, s, b, count, **where):
        part = part_of(s, 0, 0, count)
        remote(part, part, send.at[s // 2, b], block_recv.at[s, b, 0], **where).wait_send()

    @pl.loop(0, pairs)
    def _(j):
        s = 2 * j + core
        for b in range(groups):
            @pl.when((s < last) | (b == z))
            def _():
                drain(core_send, s, b, 4, sec=partner)

            for pieces, wanted in ((1, quartered(j)), (2, ~quartered(j))):
                @pl.when((s < last) & has_up & (b <= z) & wanted)
                def _():
                    drain(up_send, s, b, pieces, ch=z + 1)

                @pl.when((s < last) & has_down & (b >= z) & wanted)
                def _():
                    drain(down_send, s, b, pieces, ch=z - 1)

            for send, target, turned in ((row_send, row_peer, 0), (column_send, column_peer, 1)):
                @pl.when((b == z) & (chip == j))
                def _():
                    drain(send, s, b, 4, sec=target)

                @pl.when((b == z) & (chip != j) & near(j, turned))
                def _():
                    drain(send, s, b, 2, sec=target)

                twice = quartered(j) & (core == 1 - turned)

                for pieces, wanted in ((2, twice), (1, ~twice)):
                    @pl.when((b != z) & (s < last) & wanted)
                    def _():
                        drain(send, s, b, pieces, sec=target)

    for c in range(groups):
        span = amps.at[0, :, pl.ds(c * row_count, row_count), :]

        @pl.when(has_up & (c <= z))
        def _():
            remote(span, span, start_up.at[c], start_recv.at[0, 0], ch=z + 1).wait_send()

        @pl.when(has_down & (c >= z))
        def _():
            remote(span, span, start_down.at[c], start_recv.at[0, 0], ch=z - 1).wait_send()

    @pl.loop(0, sectors)
    def _(s):
        whole = remote(kept.at[s], kept.at[s], out_send.at[s], out_recv.at[s], sec=partner)

        @pl.when(s != k)
        def _():
            whole.wait_send()
            whole.wait_recv()

        @pl.when(s == k)
        def _():
            pltpu.make_async_copy(kept.at[s], kept.at[s], out_local.at[0]).wait()


def per_device_swept(start_amps, energies, thresholds, intersection):
    sectors = lax.axis_size("sec")
    groups = lax.axis_size("ch")
    energy_count, row_count, width_cols = start_amps.shape
    channel_count = intersection.shape[2]
    width = width_cols // 2 // sectors
    pairs = sectors // 2
    dma = pltpu.SemaphoreType.DMA
    stored = pltpu.VMEM(start_amps.shape, jnp.bfloat16)
    swept = pl.pallas_call(
        functools.partial(sweep_kernel, sectors, groups),
        out_shape=stored,
        in_specs=[
            pl.BlockSpec(memory_space=pl.ANY),
            pl.BlockSpec(memory_space=pltpu.SMEM),
            pl.BlockSpec(memory_space=pltpu.VMEM),
            pl.BlockSpec(memory_space=pl.ANY),
        ],
        out_specs=pl.BlockSpec(memory_space=pltpu.VMEM),
        scratch_shapes=[
            pltpu.VMEM((sectors, channel_count, channel_count), jnp.bfloat16),
            pltpu.VMEM((2, energy_count, channel_count, 2 * width), jnp.bfloat16),
            pltpu.VMEM((PAIRED, channel_count, 2 * width), jnp.bfloat16),
            pltpu.VMEM((sectors, 2, energy_count, row_count, width), jnp.bfloat16),
            pltpu.VMEM((sectors, energy_count, LANES, 2 * (channel_count // LANES)), jnp.float32),
            pltpu.VMEM((sectors, groups, row_count // LANES, LANES), jnp.float32),
            dma((3,)),
            dma((sectors, groups, 4)),
            dma((pairs, groups)),
            dma((pairs, groups)),
            dma((pairs, groups)),
            dma((pairs, groups)),
            dma((pairs, groups)),
            dma((energy_count, groups)),
            dma((groups,)),
            dma((groups,)),
            dma((sectors * groups,)),
            dma((sectors, groups)),
            dma((sectors,)),
            dma((sectors,)),
            dma((1,)),
        ],
        compiler_params=pltpu.CompilerParams(
            collective_id=0, has_side_effects=True, vmem_limit_bytes=56 * 2**20
        ),
    )(start_amps, energies, thresholds, intersection[0])
    return swept[None]


GATHERED_LIMIT = 24 * 2**20


def per_device(start_amps, energies, thresholds, intersection):
    sectors = lax.axis_size("sec")
    row_count, channel_count = intersection.shape[1:]
    gathered_bytes = sectors * channel_count**2 * intersection.dtype.itemsize
    even = sectors // 2 == 4 and (start_amps.shape[2] // 2) % (sectors * LANES) == 0
    even = even and energies.shape[0] % PAIRED == 0 and row_count % (4 * 16) == 0 and row_count % LANES == 0 and 3 * (channel_count // LANES) <= LANES
    if even and gathered_bytes <= GATHERED_LIMIT:
        return per_device_swept(start_amps, energies, thresholds, intersection)
    return per_device_pipelined(start_amps, energies, thresholds, intersection)


def solution(mesh):
    in_specs = (P(None, "ch", None), P(), P("sec", "ch"), P("sec", "ch", None))
    out_specs = P("sec", None, "ch", None)
    return jax.shard_map(
        per_device, mesh=mesh, in_specs=in_specs, out_specs=out_specs, check_vma=False
    )
```

```python
import functools
import math
import jax
import jax.numpy as jnp
from jax import lax
from jax.experimental import pallas as pl
from jax.experimental.pallas import tpu as pltpu
from jax.sharding import PartitionSpec as P


def passed_along(value, axis, steps):
    count = lax.axis_size(axis)
    leading, last = (max(0, -steps), min(count, count - steps))
    return lax.ppermute(value, axis, [(source, source + steps) for source in range(leading, last)])


def per_device_pipelined(start_amps, energies, thresholds, intersection):
    sectors = lax.axis_size("sec")
    sector_index = lax.axis_index("sec")
    groups = lax.axis_size("ch")
    energy_count = energies.shape[0]
    step_count = sectors + energy_count - 1
    row_count = intersection.shape[1]
    width_cols = start_amps.shape[2]
    half_cols = width_cols // 2
    col_width = half_cols // groups
    intersection_whole, thresholds_whole = (
        lax.all_gather(intersection, "ch", axis=1, tiled=True),
        lax.all_gather(thresholds, "ch", axis=1, tiled=True),
    )
    basis_change = intersection_whole[0]
    channel_thresholds = thresholds_whole[0].astype(jnp.float32)
    channel_count = basis_change.shape[0]
    paired = start_amps.reshape(energy_count, row_count, 2, half_cols)
    start_cols = lax.all_to_all(paired, "ch", split_axis=3, concat_axis=1, tiled=True)
    stored_init = jnp.zeros((energy_count, channel_count, 2, col_width), jnp.bfloat16)

    def multiply(flat):
        return jnp.dot(basis_change, flat, preferred_element_type=jnp.float32).astype(jnp.bfloat16)

    def skipped(flat):
        return jnp.zeros((channel_count, 2 * col_width), jnp.bfloat16)

    def step(step_index, state_pair):
        outgoing, stored = state_pair
        incoming = passed_along(outgoing, "sec", 1)
        energy_raw = step_index - sector_index
        active = (energy_raw >= 0) & (energy_raw < energy_count)
        energy_slot = jnp.clip(energy_raw, 0, energy_count - 1)
        initial = lax.dynamic_index_in_dim(start_cols, energy_slot, 0, keepdims=False)
        source = jnp.where(sector_index == 0, initial, incoming).astype(jnp.float32)
        wavenumber = jnp.sqrt(energies[energy_slot] - channel_thresholds)[:, None]
        values_part = source[:, 0, :]
        slopes_part = source[:, 1, :]
        cosine = jnp.cos(wavenumber)
        sine_term = jnp.sin(wavenumber)
        new_values = cosine * values_part + sine_term / wavenumber * slopes_part
        new_slopes = -wavenumber * sine_term * values_part + cosine * slopes_part
        rotated = jnp.stack([new_values, new_slopes], axis=1).astype(jnp.bfloat16)
        flat = rotated.reshape(channel_count, 2 * col_width)
        fresh = lax.cond(active, multiply, skipped, flat)
        fresh = fresh.reshape(channel_count, 2, col_width)
        previous = lax.dynamic_index_in_dim(stored, energy_slot, 0, keepdims=False)
        kept = jnp.where(active, fresh, previous)
        stored = lax.dynamic_update_index_in_dim(stored, kept, energy_slot, 0)
        return (fresh, stored)

    outgoing_init = jnp.zeros((channel_count, 2, col_width), jnp.bfloat16)
    final_pair = lax.fori_loop(0, step_count, step, (outgoing_init, stored_init))
    returned = lax.all_to_all(final_pair[1], "ch", split_axis=1, concat_axis=3, tiled=True)
    return returned.reshape(energy_count, row_count, width_cols)[None]


LANES = 128
PAIRED = 2
EXTRA = 2
QUARTERED = (0, 1)
HOME, LIFT, HOP, SIDE, TWIN, FEED, FEED_HOP, STEP, FAR, ANGLES, END = range(11)
TUNED = (
    (5, 0, 0), (5, 1, 0), (6, 1, 1), (6, 0, 1), (6, 1, 2), (5, 2, 0), (0, 2, 0), (1, 2, 0), (0, 1, 0), (1, 1, 0),
    (0, 0, 0), (0, 3, 0), (2, 1, 1), (2, 1, 2), (1, 0, 0), (2, 1, 3), (3, 1, 1), (2, 0, 1), (2, 0, 2), (8, 1, 1),
    (3, 1, 3), (2, 0, 3), (3, 1, 2), (1, 3, 0), (2, 2, 1), (3, 0, 3), (2, 3, 1), (2, 3, 2), (3, 0, 2), (3, 2, 1),
    (3, 0, 1), (8, 0, 3), (8, 1, 2), (6, 0, 2), (6, 0, 3), (8, 1, 3), (2, 3, 3), (6, 1, 3), (2, 2, 2), (3, 3, 2),
    (8, 0, 2), (8, 0, 1), (5, 7, 0), (2, 2, 3), (6, 2, 1), (5, 4, 0), (3, 3, 1), (4, 1, 0), (4, 0, 0), (7, 0, 0),
    (3, 2, 2), (5, 3, 0), (3, 2, 3), (7, 1, 0), (7, 2, 0), (3, 3, 3), (7, 3, 0), (6, 2, 2), (4, 3, 0), (4, 2, 0),
    (7, 4, 0), (6, 4, 1), (7, 5, 0), (7, 6, 0), (6, 3, 1), (7, 7, 0), (6, 2, 3), (6, 3, 2), (5, 5, 0), (6, 3, 3),
    (7, 0, 1), (7, 1, 1), (7, 2, 1), (7, 3, 1), (6, 4, 2), (6, 5, 1), (7, 4, 1), (5, 6, 0), (7, 5, 1), (6, 5, 2),
    (7, 6, 1), (6, 7, 1), (6, 5, 3), (7, 7, 1), (6, 4, 3), (6, 6, 1), (6, 7, 2), (7, 0, 2), (7, 1, 2), (6, 6, 2),
    (7, 2, 2), (7, 3, 2), (7, 4, 2), (6, 7, 3), (6, 6, 3), (7, 5, 2), (7, 0, 3), (7, 6, 2), (7, 1, 3), (7, 2, 3),
    (7, 7, 2), (7, 3, 3), (7, 4, 3), (7, 5, 3), (7, 6, 3), (7, 7, 3),
)


def plain_order(pairs, sectors, energy_count, groups):
    order = [(HOME, j, 0) for j in range(pairs)]
    order += [(FEED, e, 0) for e in range(energy_count + EXTRA)] + [(LIFT, j, 0) for j in range(pairs)]
    for tick in range(pairs + groups + 1):
        for d in range(groups - 1, 0, -1):
            if 0 <= tick - d < pairs:
                order.append((HOP, tick - d, d))
            if 0 <= tick - d - 1 < pairs:
                order.append((SIDE, tick - d - 1, d))
            if 0 <= tick - d - 2 < pairs and tick - d - 2 in QUARTERED:
                order.append((FAR, tick - d - 2, d))
    order += [(TWIN, j, 0) for j in range(pairs)]
    for e in range(energy_count + EXTRA):
        order += [(FEED_HOP, e, d) for d in range(1, groups)]
        if (e + 1) % PAIRED == 0:
            order += [(STEP, s, e // PAIRED) for s in range(sectors)]
    return order


def order_of(pairs, sectors, energy_count, groups):
    plain = plain_order(pairs, sectors, energy_count, groups)
    chosen = TUNED if sorted(TUNED) == sorted(plain) else plain
    order, left = [], list(range(sectors))
    for entry in chosen:
        while left and entry[0] == STEP:
            order.append((ANGLES, left.pop(0), 0))
        order.append(entry)
        if left:
            order.append((ANGLES, left.pop(0), 0))
    return order


def cos_and_sin(w):
    u = (w - jnp.float32(1.57079637050628662109375)) + jnp.float32(4.37113900018624283e-8)
    square = u * u
    odd = even = None
    for power in range(12, -1, -2):
        even = (0.0 if even is None else even * square) + (-1.0) ** (power // 2) / math.factorial(power)
        odd = (0.0 if odd is None else odd * square) + (-1.0) ** (power // 2) / math.factorial(power + 1)
    return -u * odd, even


def sweep_kernel(
    sectors, groups, start, energies, limits, own_block, out,
    basis, amps, rotated, kept, doubled, turn, bounds,
    local_sem, block_recv, column_send, row_send, up_send, down_send, core_send,
    start_recv, start_up, start_down, bound_send, bound_recv, out_send, out_recv, out_local, doubled_sem,
):
    k = lax.axis_index("sec")
    z = lax.axis_index("ch")
    core = k % 2
    chip = k // 2
    column, row = chip % 2, chip // 2
    partner = k + 1 - 2 * core
    column_peer = k + 2 - 4 * column
    row_peer = k + 4 - 8 * row
    pairs = sectors // 2
    last = sectors - 1
    energy_count, row_count, width_cols = start.shape
    half_cols = width_cols // 2
    width = half_cols // sectors
    channel_count = row_count * groups
    chunks = channel_count // LANES
    devices = sectors * groups
    across = column_peer + row_peer - k
    across_chip = across // 2
    shared = energy_count - EXTRA
    has_up = z + 1 < groups
    has_down = z >= 1
    piece = row_count // 4
    order = order_of(pairs, sectors, energy_count, groups)

    def remote(src, dst, send, recv, **where):
        return pltpu.make_async_remote_copy(
            src_ref=src, dst_ref=dst, send_sem=send, recv_sem=recv,
            device_id=where, device_id_type=pl.DeviceIdType.MESH,
        )

    def rows_of(c):
        return pl.ds(pl.multiple_of(c * row_count, row_count), row_count)

    def other(step):
        place = (k * groups + z + step) % devices
        return {"sec": place // groups, "ch": place % groups}

    def part_of(s, b, r, count=1):
        return basis.at[s, pl.ds(pl.multiple_of(b * row_count + r * piece, piece), count * piece), :]

    def piece_move(s, b, r, send, **where):
        part = part_of(s, b, r)
        return remote(part, part, send.at[s // 2, b], block_recv.at[s, b, r], **where)

    column_chip, row_chip = chip + 1 - 2 * column, chip + 2 - 4 * row

    def quartered(j):
        found = j < 0
        for pair in QUARTERED:
            found = found | (j == pair)
        return found

    def near(j, q):
        return row == j // 2 if q == 0 else column == j % 2

    def carried(j, q):
        return jnp.where(near(j, q), 2 * q, 2 * q + 1)

    def left_over(j, q):
        return jnp.where(near(j, q), 2 * q + 1, 2 * q)

    def lift(s, b, r):
        @pl.when((s < last) & has_up & (b <= z))
        def _():
            piece_move(s, b, r, up_send, ch=z + 1).start()

        @pl.when((s < last) & has_down & (b >= z))
        def _():
            piece_move(s, b, r, down_send, ch=z - 1).start()

    def to_column(s, b, r):
        piece_move(s, b, r, column_send, sec=column_peer).start()

    def to_row(s, b, r):
        piece_move(s, b, r, row_send, sec=row_peer).start()

    def to_core(s, b, r):
        piece_move(s, b, r, core_send, sec=partner).start()

    def piece_arrived(s, b, r):
        piece_move(s, b, r, core_send, sec=partner).wait_recv()

    def give_own():
        for r in (1, 3, 0, 2):
            to_column(k, z, r)
            to_row(k, z, r)
        for r in (1, 3, 0, 2):
            to_core(k, z, r)

    def home(j):
        s = 2 * j + core

        @pl.when(chip != j)
        def _():
            for r in (1, 3, 0, 2):
                piece_arrived(s, z, r)

                @pl.when(near(j, r // 2))
                def _():
                    (to_column if r // 2 else to_row)(s, z, r)

                to_core(s, z, r)

    def lift_own(j):
        @pl.when(quartered(j))
        def _():
            lift(2 * j + core, z, chip)

        @pl.when(~quartered(j))
        def _():
            for q in range(2):
                lift(2 * j + core, z, carried(j, q))

    def both_sides(j, d, action):
        s = 2 * j + core
        for b in (z - d, z + d):
            @pl.when((s < last) & (b >= 0) & (b < groups))
            def _():
                action(s, b)

    def hop_from(j, d):
        @pl.when(quartered(j))
        def _():
            def action(s, b):
                piece_arrived(s, b, chip)
                lift(s, b, chip)
                to_column(s, b, chip)
                to_row(s, b, chip)
                to_core(s, b, chip)

            both_sides(j, d, action)

        @pl.when(~quartered(j))
        def _():
            for q in range(2):
                def action(s, b):
                    r = carried(j, q)
                    piece_arrived(s, b, r)
                    lift(s, b, r)
                    (to_column if q else to_row)(s, b, r)
                    to_core(s, b, r)

                both_sides(j, d, action)

    def side_from(j, d):
        @pl.when(quartered(j))
        def _():
            def action(s, b):
                piece_arrived(s, b, column_chip)

                @pl.when(core == 1)
                def _():
                    to_row(s, b, column_chip)

                to_core(s, b, column_chip)
                piece_arrived(s, b, row_chip)

                @pl.when(core == 0)
                def _():
                    to_column(s, b, row_chip)

                to_core(s, b, row_chip)

            both_sides(j, d, action)

        @pl.when(~quartered(j))
        def _():
            for q in range(2):
                def action(s, b):
                    r = left_over(j, q)
                    piece_arrived(s, b, r)
                    to_core(s, b, r)

                both_sides(j, d, action)

    def far_from(j, d):
        def action(s, b):
            piece_arrived(s, b, 3 - chip)
            to_core(s, b, 3 - chip)

        both_sides(j, d, action)

    def twin(j):
        s = 2 * j + 1 - core
        for b in range(groups):
            @pl.when((s < last) | (b == z))
            def _():
                for r in range(4):
                    piece_arrived(s, b, r)

    def start_part(e, c):
        return amps.at[0, e, rows_of(c), :]

    def start_move(e, c, send, **where):
        return remote(start_part(e, c), start_part(e, c), send.at[c], start_recv.at[e, c], **where)

    def start_relay(e, c):
        @pl.when(has_up & (c <= z))
        def _():
            start_move(e, c, start_up, ch=z + 1).start()

        @pl.when(has_down & (c >= z))
        def _():
            start_move(e, c, start_down, ch=z - 1).start()

    def start_arrive_and_relay(e, c):
        @pl.when((c >= 0) & (c < groups))
        def _():
            start_move(e, c, start_up, sec=partner).wait_recv()
            start_relay(e, c)

    bounds[k, z] = jnp.concatenate(
        [limits[:, q * LANES : (q + 1) * LANES] for q in range(row_count // LANES)], axis=0
    ).astype(jnp.float32)
    loads = [
        pltpu.make_async_copy(own_block, basis.at[k, rows_of(z), :], local_sem.at[0]),
    ]
    for half in range(2):
        for owner, source, target in (
            (k, pl.ds(0, energy_count), pl.ds(0, energy_count)),
            (across, pl.ds(shared, EXTRA), pl.ds(energy_count, EXTRA)),
        ):
            loads.append(pltpu.make_async_copy(
                start.at[source, :, pl.ds(pl.multiple_of(half * half_cols + owner * width, width), width)],
                amps.at[0, target, rows_of(z), pl.ds(half * width, width)], local_sem.at[len(loads)]))
    for load in loads:
        load.start()

    barrier = pltpu.get_barrier_semaphore()

    @pl.loop(1, devices)
    def _(step):
        pl.semaphore_signal(barrier, inc=1, device_id=other(step), device_id_type=pl.DeviceIdType.MESH)

    pl.semaphore_wait(barrier, devices - 1)
    loads[0].wait()

    give_own()
    for load in loads[1:]:
        load.wait()

    def bound_move(step):
        return pltpu.make_async_remote_copy(
            src_ref=bounds.at[k, z], dst_ref=bounds.at[k, z], send_sem=bound_send.at[step], recv_sem=bound_recv.at[k, z],
            device_id=other(step), device_id_type=pl.DeviceIdType.MESH,
        )

    @pl.loop(1, devices)
    def _(step):
        bound_move(step).start()

    def angles(s):
        for c in range(groups):
            @pl.when((s != k) | (c != z))
            def _():
                remote(bounds.at[s, c], bounds.at[s, c], bound_send.at[0], bound_recv.at[s, c], sec=partner).wait_recv()

        floor = jnp.concatenate([bounds[s, c] for c in range(groups)], axis=0)
        wavenumber = jnp.concatenate([jnp.sqrt(energies[e] - floor) for e in range(energy_count)], axis=0)
        cosine, sine = cos_and_sin(wavenumber)
        shear, turned = (1.0 - cosine) / (wavenumber * sine), -wavenumber * sine
        for e in range(energy_count):
            own = slice(e * chunks, (e + 1) * chunks)
            turn[s, e] = jnp.concatenate([shear[own], turned[own]], axis=0).T

    def rotate(s, e, m):
        source = jnp.minimum(s, 1)
        factors = turn[s, jnp.where(e < energy_count, e, e - EXTRA)]
        for q in range(chunks):
            place = pl.ds(q * LANES, LANES)
            both = amps[source, e, place, :].astype(jnp.float32)
            shear, turned = factors[:, q : q + 1], factors[:, chunks + q : chunks + q + 1]
            values_part, slopes_part = both[:, :width], both[:, width:]
            values_part = values_part + shear * slopes_part
            slopes_part = slopes_part + turned * values_part
            values_part = values_part + shear * slopes_part
            rotated[m, place, pl.ds(0, width)] = values_part.astype(jnp.bfloat16)
            rotated[m, place, pl.ds(width, width)] = slopes_part.astype(jnp.bfloat16)

    def keep(s, group, mine_of):
        @pl.when(group < energy_count // PAIRED)
        def _():
            for m in range(PAIRED):
                mine = mine_of(m)
                kept[s, 0, PAIRED * group + m] = mine[:, :width]
                kept[s, 1, PAIRED * group + m] = mine[:, width:]

        @pl.when((group >= energy_count // PAIRED) & (s // 2 == chip))
        def _():
            for m in range(PAIRED):
                mine = mine_of(m)
                doubled[s % 2, 0, PAIRED * group + m - energy_count] = mine[:, :width]
                doubled[s % 2, 1, PAIRED * group + m - energy_count] = mine[:, width:]

    def advance(s, group):
        wanted = (group < energy_count // PAIRED) | (s // 2 <= chip)

        @pl.when(wanted & (s < last))
        def _():
            for m in range(PAIRED):
                rotate(s, PAIRED * group + m, m)
            for m in range(PAIRED):
                e = PAIRED * group + m
                amps[1, e] = jnp.dot(basis[s], rotated[m], preferred_element_type=jnp.float32).astype(jnp.bfloat16)
            keep(s, group, lambda m: amps[1, PAIRED * group + m, rows_of(z), :])

        @pl.when(wanted & (s == last))
        def _():
            for m in range(PAIRED):
                rotate(s, PAIRED * group + m, m)
            for m in range(PAIRED):
                mine = jnp.dot(basis[s, rows_of(z), :], rotated[m], preferred_element_type=jnp.float32)
                amps[1, PAIRED * group + m, rows_of(z), :] = mine.astype(jnp.bfloat16)
            keep(s, group, lambda m: amps[1, PAIRED * group + m, rows_of(z), :])

    def columns_of(owner, half):
        return pl.ds(pl.multiple_of(half * half_cols + owner * width, width), width)

    def send_out(s, e):
        for half in range(2):
            part = kept.at[s, half, e]
            place = out.at[e, :, columns_of(k, half)]

            @pl.when(s == k)
            def _():
                pltpu.make_async_copy(part, place, out_local.at[0]).start()

            @pl.when((s != k) & ((e < shared) | (s // 2 != across_chip)))
            def _():
                remote(part, place, out_send.at[s], out_recv.at[k], sec=s).start()

    def send_doubled(s, e):
        for half in range(2):
            part = doubled.at[s % 2, half, e - energy_count]
            place = out.at[e - EXTRA, :, columns_of(across, half)]

            @pl.when(s == k)
            def _():
                pltpu.make_async_copy(part, place, doubled_sem.at[0]).start()

            @pl.when(s == partner)
            def _():
                remote(part, place, doubled_sem.at[1], doubled_sem.at[2], sec=partner).start()

    bits = max(sectors - 1, energy_count + EXTRA - 1, groups - 1).bit_length()
    span = 2 * bits + END.bit_length()
    packed = max(1, 30 // span)
    codes = [(kind << 2 * bits) | (first << bits) | second for kind, first, second in (*order, (END, 0, 0))]
    words = [
        sum(code << span * place for place, code in enumerate(codes[at : at + packed]))
        for at in range(0, len(codes), packed)
    ]
    low = 2**bits

    def entry(at, place):
        values = words
        while len(values) > 1:
            odd = (at & 1) == 1
            values = [
                jnp.where(odd, values[i + 1], values[i]) if i + 1 < len(values) else values[i]
                for i in range(0, len(values), 2)
            ]
            at = lax.shift_right_logical(at, jnp.int32(1))
        word = values[0]
        for step in range(1, packed):
            word = jnp.where(place == step, lax.shift_right_logical(values[0], jnp.int32(span * step)), word)
        word = word & (2**span - 1)
        return (
            lax.shift_right_logical(word, jnp.int32(2 * bits)),
            lax.shift_right_logical(word, jnp.int32(bits)) & (low - 1),
            word & (low - 1),
        )

    def act(n, before):
        at, place = before[3:]
        kind, first, second = entry(at, place)
        wrapped = place == packed - 1

        @pl.when(kind == STEP)
        def _():
            advance(first, second)

        @pl.when(kind == ANGLES)
        def _():
            angles(first)

        @pl.when(kind == HOME)
        def _():
            home(first)

        @pl.when(kind == LIFT)
        def _():
            lift_own(first)

        @pl.when(kind == HOP)
        def _():
            hop_from(first, second)

        @pl.when(kind == SIDE)
        def _():
            side_from(first, second)

        @pl.when(kind == FAR)
        def _():
            far_from(first, second)

        @pl.when(kind == TWIN)
        def _():
            twin(first)

        @pl.when(kind == FEED)
        def _():
            start_relay(first, z)

        @pl.when(kind == FEED_HOP)
        def _():
            start_arrive_and_relay(first, z - second)
            start_arrive_and_relay(first, z + second)

        @pl.when(before[0] == STEP)
        def _():
            @pl.when(before[2] < energy_count // PAIRED)
            def _():
                for m in range(PAIRED):
                    send_out(before[1], PAIRED * before[2] + m)

            @pl.when(before[2] >= energy_count // PAIRED)
            def _():
                for m in range(PAIRED):
                    send_doubled(before[1], PAIRED * before[2] + m)

        return kind, first, second, jnp.where(wrapped, at + 1, at), jnp.where(wrapped, 0, place + 1)

    lax.fori_loop(0, len(codes), act, (jnp.int32(END),) + (jnp.int32(0),) * 4)

    @pl.loop(1, devices)
    def _(step):
        bound_move(step).wait_send()

    def drain(send, s, b, count, **where):
        part = part_of(s, 0, 0, count)
        remote(part, part, send.at[s // 2, b], block_recv.at[s, b, 0], **where).wait_send()

    @pl.loop(0, pairs)
    def _(j):
        s = 2 * j + core
        for b in range(groups):
            @pl.when((s < last) | (b == z))
            def _():
                drain(core_send, s, b, 4, sec=partner)

            for pieces, wanted in ((1, quartered(j)), (2, ~quartered(j))):
                @pl.when((s < last) & has_up & (b <= z) & wanted)
                def _():
                    drain(up_send, s, b, pieces, ch=z + 1)

                @pl.when((s < last) & has_down & (b >= z) & wanted)
                def _():
                    drain(down_send, s, b, pieces, ch=z - 1)

            for send, target, turned in ((row_send, row_peer, 0), (column_send, column_peer, 1)):
                @pl.when((b == z) & (chip == j))
                def _():
                    drain(send, s, b, 4, sec=target)

                @pl.when((b == z) & (chip != j) & near(j, turned))
                def _():
                    drain(send, s, b, 2, sec=target)

                twice = quartered(j) & (core == 1 - turned)

                for pieces, wanted in ((2, twice), (1, ~twice)):
                    @pl.when((b != z) & (s < last) & wanted)
                    def _():
                        drain(send, s, b, pieces, sec=target)

    for c in range(groups):
        span = amps.at[0, :, pl.ds(c * row_count, row_count), :]

        @pl.when(has_up & (c <= z))
        def _():
            remote(span, span, start_up.at[c], start_recv.at[0, 0], ch=z + 1).wait_send()

        @pl.when(has_down & (c >= z))
        def _():
            remote(span, span, start_down.at[c], start_recv.at[0, 0], ch=z - 1).wait_send()

    @pl.loop(0, sectors)
    def _(s):
        @pl.when(s == k)
        def _():
            pltpu.make_async_copy(kept.at[s], kept.at[s], out_local.at[0]).wait()

        for far in range(2):
            part = kept.at[s, :, pl.ds(0, shared if far else energy_count)]
            move = remote(part, part, out_send.at[s], out_recv.at[s], sec=partner)

            @pl.when((s != k) & (s // 2 == across_chip if far else s // 2 != across_chip))
            def _():
                move.wait_send()
                move.wait_recv()

    pltpu.make_async_copy(doubled.at[0], doubled.at[0], doubled_sem.at[0]).wait()
    crossed = remote(doubled.at[0], doubled.at[0], doubled_sem.at[1], doubled_sem.at[2], sec=partner)
    crossed.wait_send()
    crossed.wait_recv()


def per_device_swept(start_amps, energies, thresholds, intersection):
    sectors = lax.axis_size("sec")
    groups = lax.axis_size("ch")
    energy_count, row_count, width_cols = start_amps.shape
    channel_count = intersection.shape[2]
    width = width_cols // 2 // sectors
    pairs = sectors // 2
    dma = pltpu.SemaphoreType.DMA
    stored = pltpu.VMEM(start_amps.shape, jnp.bfloat16)
    swept = pl.pallas_call(
        functools.partial(sweep_kernel, sectors, groups),
        out_shape=stored,
        in_specs=[
            pl.BlockSpec(memory_space=pl.ANY),
            pl.BlockSpec(memory_space=pltpu.SMEM),
            pl.BlockSpec(memory_space=pltpu.VMEM),
            pl.BlockSpec(memory_space=pl.ANY),
        ],
        out_specs=pl.BlockSpec(memory_space=pltpu.VMEM),
        scratch_shapes=[
            pltpu.VMEM((sectors, channel_count, channel_count), jnp.bfloat16),
            pltpu.VMEM((2, energy_count + EXTRA, channel_count, 2 * width), jnp.bfloat16),
            pltpu.VMEM((PAIRED, channel_count, 2 * width), jnp.bfloat16),
            pltpu.VMEM((sectors, 2, energy_count, row_count, width), jnp.bfloat16),
            pltpu.VMEM((2, 2, EXTRA, row_count, width), jnp.bfloat16),
            pltpu.VMEM((sectors, energy_count, LANES, 2 * (channel_count // LANES)), jnp.float32),
            pltpu.VMEM((sectors, groups, row_count // LANES, LANES), jnp.float32),
            dma((5,)),
            dma((sectors, groups, 4)),
            dma((pairs, groups)),
            dma((pairs, groups)),
            dma((pairs, groups)),
            dma((pairs, groups)),
            dma((pairs, groups)),
            dma((energy_count + EXTRA, groups)),
            dma((groups,)),
            dma((groups,)),
            dma((sectors * groups,)),
            dma((sectors, groups)),
            dma((sectors,)),
            dma((sectors,)),
            dma((1,)),
            dma((3,)),
        ],
        compiler_params=pltpu.CompilerParams(
            collective_id=0, has_side_effects=True, vmem_limit_bytes=56 * 2**20
        ),
    )(start_amps, energies, thresholds, intersection[0])
    return swept[None]


GATHERED_LIMIT = 24 * 2**20


def per_device(start_amps, energies, thresholds, intersection):
    sectors = lax.axis_size("sec")
    row_count, channel_count = intersection.shape[1:]
    gathered_bytes = sectors * channel_count**2 * intersection.dtype.itemsize
    even = sectors // 2 == 4 and (start_amps.shape[2] // 2) % (sectors * LANES) == 0
    even = even and energies.shape[0] % PAIRED == 0 and energies.shape[0] > EXTRA and row_count % (4 * 16) == 0 and row_count % LANES == 0 and 3 * (channel_count // LANES) <= LANES
    if even and gathered_bytes <= GATHERED_LIMIT:
        return per_device_swept(start_amps, energies, thresholds, intersection)
    return per_device_pipelined(start_amps, energies, thresholds, intersection)


def solution(mesh):
    in_specs = (P(None, "ch", None), P(), P("sec", "ch"), P("sec", "ch", None))
    out_specs = P("sec", None, "ch", None)
    return jax.shard_map(
        per_device, mesh=mesh, in_specs=in_specs, out_specs=out_specs, check_vma=False
    )
```

```python
import functools
import math
import jax
import jax.numpy as jnp
from jax import lax
from jax.experimental import pallas as pl
from jax.experimental.pallas import tpu as pltpu
from jax.sharding import PartitionSpec as P


def passed_along(value, axis, steps):
    count = lax.axis_size(axis)
    leading, last = (max(0, -steps), min(count, count - steps))
    return lax.ppermute(value, axis, [(source, source + steps) for source in range(leading, last)])


def per_device_pipelined(start_amps, energies, thresholds, intersection):
    sectors = lax.axis_size("sec")
    sector_index = lax.axis_index("sec")
    groups = lax.axis_size("ch")
    energy_count = energies.shape[0]
    step_count = sectors + energy_count - 1
    row_count = intersection.shape[1]
    width_cols = start_amps.shape[2]
    half_cols = width_cols // 2
    col_width = half_cols // groups
    intersection_whole, thresholds_whole = (
        lax.all_gather(intersection, "ch", axis=1, tiled=True),
        lax.all_gather(thresholds, "ch", axis=1, tiled=True),
    )
    basis_change = intersection_whole[0]
    channel_thresholds = thresholds_whole[0].astype(jnp.float32)
    channel_count = basis_change.shape[0]
    paired = start_amps.reshape(energy_count, row_count, 2, half_cols)
    start_cols = lax.all_to_all(paired, "ch", split_axis=3, concat_axis=1, tiled=True)
    stored_init = jnp.zeros((energy_count, channel_count, 2, col_width), jnp.bfloat16)

    def multiply(flat):
        return jnp.dot(basis_change, flat, preferred_element_type=jnp.float32).astype(jnp.bfloat16)

    def skipped(flat):
        return jnp.zeros((channel_count, 2 * col_width), jnp.bfloat16)

    def step(step_index, state_pair):
        outgoing, stored = state_pair
        incoming = passed_along(outgoing, "sec", 1)
        energy_raw = step_index - sector_index
        active = (energy_raw >= 0) & (energy_raw < energy_count)
        energy_slot = jnp.clip(energy_raw, 0, energy_count - 1)
        initial = lax.dynamic_index_in_dim(start_cols, energy_slot, 0, keepdims=False)
        source = jnp.where(sector_index == 0, initial, incoming).astype(jnp.float32)
        wavenumber = jnp.sqrt(energies[energy_slot] - channel_thresholds)[:, None]
        values_part = source[:, 0, :]
        slopes_part = source[:, 1, :]
        cosine = jnp.cos(wavenumber)
        sine_term = jnp.sin(wavenumber)
        new_values = cosine * values_part + sine_term / wavenumber * slopes_part
        new_slopes = -wavenumber * sine_term * values_part + cosine * slopes_part
        rotated = jnp.stack([new_values, new_slopes], axis=1).astype(jnp.bfloat16)
        flat = rotated.reshape(channel_count, 2 * col_width)
        fresh = lax.cond(active, multiply, skipped, flat)
        fresh = fresh.reshape(channel_count, 2, col_width)
        previous = lax.dynamic_index_in_dim(stored, energy_slot, 0, keepdims=False)
        kept = jnp.where(active, fresh, previous)
        stored = lax.dynamic_update_index_in_dim(stored, kept, energy_slot, 0)
        return (fresh, stored)

    outgoing_init = jnp.zeros((channel_count, 2, col_width), jnp.bfloat16)
    final_pair = lax.fori_loop(0, step_count, step, (outgoing_init, stored_init))
    returned = lax.all_to_all(final_pair[1], "ch", split_axis=1, concat_axis=3, tiled=True)
    return returned.reshape(energy_count, row_count, width_cols)[None]


LANES = 128
PAIRED = 2
EXTRA = 2
QUARTERED = (0, 1)
HOME, LIFT, HOP, SIDE, TWIN, FEED, FEED_HOP, STEP, FAR, ANGLES, MEET, BOUND, SPREAD, END = range(14)
TUNED = (
    (5, 1, 0), (5, 0, 0), (6, 1, 1), (6, 0, 1), (5, 2, 0), (6, 1, 2), (0, 1, 0), (1, 1, 0), (0, 2, 0), (1, 2, 0),
    (0, 0, 0), (0, 3, 0), (2, 1, 1), (1, 0, 0), (2, 1, 2), (2, 0, 1), (2, 1, 3), (2, 0, 2), (3, 1, 2), (6, 1, 3),
    (6, 0, 2), (2, 0, 3), (1, 3, 0), (3, 0, 2), (3, 1, 3), (3, 0, 1), (3, 1, 1), (3, 0, 3), (2, 3, 1), (2, 2, 1),
    (8, 1, 3), (8, 0, 2), (2, 2, 2), (8, 0, 1), (6, 0, 3), (8, 0, 3), (8, 1, 1), (8, 1, 2), (2, 3, 2), (2, 2, 3),
    (4, 0, 0), (5, 3, 0), (3, 3, 1), (7, 0, 0), (2, 3, 3), (7, 1, 0), (3, 2, 1), (5, 4, 0), (6, 2, 1), (4, 1, 0),
    (3, 3, 2), (6, 3, 1), (5, 5, 0), (3, 2, 2), (3, 2, 3), (3, 3, 3), (7, 2, 0), (7, 3, 0), (4, 2, 0), (7, 4, 0),
    (7, 5, 0), (4, 3, 0), (7, 6, 0), (6, 2, 2), (7, 7, 0), (6, 3, 2), (6, 2, 3), (6, 3, 3), (7, 0, 1), (7, 1, 1),
    (6, 5, 1), (6, 5, 2), (7, 2, 1), (7, 3, 1), (5, 6, 0), (7, 4, 1), (6, 4, 1), (7, 5, 1), (6, 6, 1), (7, 6, 1),
    (7, 7, 1), (6, 4, 2), (6, 5, 3), (6, 4, 3), (5, 7, 0), (7, 0, 2), (7, 1, 2), (7, 2, 2), (6, 6, 2), (7, 3, 2),
    (7, 4, 2), (6, 7, 1), (6, 7, 2), (7, 5, 2), (6, 7, 3), (6, 6, 3), (7, 0, 3), (7, 6, 2), (7, 1, 3), (7, 2, 3),
    (7, 3, 3), (7, 4, 3), (7, 5, 3), (7, 6, 3), (7, 7, 3), (7, 7, 2),
)


def plain_order(pairs, sectors, energy_count, groups):
    order = [(HOME, j, 0) for j in range(pairs)]
    order += [(FEED, e, 0) for e in range(energy_count + EXTRA)] + [(LIFT, j, 0) for j in range(pairs)]
    for tick in range(pairs + groups + 1):
        for d in range(groups - 1, 0, -1):
            if 0 <= tick - d < pairs:
                order.append((HOP, tick - d, d))
            if 0 <= tick - d - 1 < pairs:
                order.append((SIDE, tick - d - 1, d))
            if 0 <= tick - d - 2 < pairs and tick - d - 2 in QUARTERED:
                order.append((FAR, tick - d - 2, d))
    order += [(TWIN, j, 0) for j in range(pairs)]
    for e in range(energy_count + EXTRA):
        order += [(FEED_HOP, e, d) for d in range(1, groups)]
        if (e + 1) % PAIRED == 0:
            order += [(STEP, s, e // PAIRED) for s in range(sectors)]
    return order


def order_of(pairs, sectors, energy_count, groups):
    plain = plain_order(pairs, sectors, energy_count, groups)
    chosen = TUNED if sorted(TUNED) == sorted(plain) else plain
    order, left = [], [(MEET, 0, 0), (BOUND, 1, 0), (MEET, 1, 0)]
    left += [(BOUND, d, 0) for d in range(2, groups)] + [(SPREAD, 0, 0)]
    left += [(ANGLES, s, 0) for s in range(sectors)]
    for entry in chosen:
        while left and entry[0] == STEP:
            order.append(left.pop(0))
        order.append(entry)
        if left:
            order.append(left.pop(0))
    return order


def cos_and_sin(w):
    u = (w - jnp.float32(1.57079637050628662109375)) + jnp.float32(4.37113900018624283e-8)
    square = u * u
    odd = even = None
    for power in range(12, -1, -2):
        even = (0.0 if even is None else even * square) + (-1.0) ** (power // 2) / math.factorial(power)
        odd = (0.0 if odd is None else odd * square) + (-1.0) ** (power // 2) / math.factorial(power + 1)
    return -u * odd, even


def sweep_kernel(
    sectors, groups, start, energies, limits, own_block, out,
    basis, amps, rotated, kept, doubled, turn, bounds,
    local_sem, block_recv, column_send, row_send, up_send, down_send, core_send,
    start_recv, start_up, start_down, bound_send, bound_recv, out_send, out_recv, out_local, doubled_sem, met, spread_send, spread_recv,
):
    k = lax.axis_index("sec")
    z = lax.axis_index("ch")
    core = k % 2
    chip = k // 2
    column, row = chip % 2, chip // 2
    partner = k + 1 - 2 * core
    column_peer = k + 2 - 4 * column
    row_peer = k + 4 - 8 * row
    pairs = sectors // 2
    last = sectors - 1
    energy_count, row_count, width_cols = start.shape
    half_cols = width_cols // 2
    width = half_cols // sectors
    channel_count = row_count * groups
    chunks = channel_count // LANES
    across = column_peer + row_peer - k
    across_chip = across // 2
    shared = energy_count - EXTRA
    has_up = z + 1 < groups
    has_down = z >= 1
    piece = row_count // 4
    order = order_of(pairs, sectors, energy_count, groups)

    def remote(src, dst, send, recv, **where):
        return pltpu.make_async_remote_copy(
            src_ref=src, dst_ref=dst, send_sem=send, recv_sem=recv,
            device_id=where, device_id_type=pl.DeviceIdType.MESH,
        )

    def rows_of(c):
        return pl.ds(pl.multiple_of(c * row_count, row_count), row_count)

    def part_of(s, b, r, count=1):
        return basis.at[s, pl.ds(pl.multiple_of(b * row_count + r * piece, piece), count * piece), :]

    def piece_move(s, b, r, send, **where):
        part = part_of(s, b, r)
        return remote(part, part, send.at[s // 2, b], block_recv.at[s, b, r], **where)

    column_chip, row_chip = chip + 1 - 2 * column, chip + 2 - 4 * row

    def quartered(j):
        found = j < 0
        for pair in QUARTERED:
            found = found | (j == pair)
        return found

    def near(j, q):
        return row == j // 2 if q == 0 else column == j % 2

    def carried(j, q):
        return jnp.where(near(j, q), 2 * q, 2 * q + 1)

    def left_over(j, q):
        return jnp.where(near(j, q), 2 * q + 1, 2 * q)

    def lift(s, b, r):
        @pl.when((s < last) & has_up & (b <= z))
        def _():
            piece_move(s, b, r, up_send, ch=z + 1).start()

        @pl.when((s < last) & has_down & (b >= z))
        def _():
            piece_move(s, b, r, down_send, ch=z - 1).start()

    def to_column(s, b, r):
        piece_move(s, b, r, column_send, sec=column_peer).start()

    def to_row(s, b, r):
        piece_move(s, b, r, row_send, sec=row_peer).start()

    def to_core(s, b, r):
        piece_move(s, b, r, core_send, sec=partner).start()

    def piece_arrived(s, b, r):
        piece_move(s, b, r, core_send, sec=partner).wait_recv()

    def give_own():
        for r in (1, 3, 0, 2):
            to_column(k, z, r)
            to_row(k, z, r)
        for r in (1, 3, 0, 2):
            to_core(k, z, r)

    def home(j):
        s = 2 * j + core

        @pl.when(chip != j)
        def _():
            for r in (1, 3, 0, 2):
                piece_arrived(s, z, r)

                @pl.when(near(j, r // 2))
                def _():
                    (to_column if r // 2 else to_row)(s, z, r)

                to_core(s, z, r)

    def lift_own(j):
        @pl.when(quartered(j))
        def _():
            lift(2 * j + core, z, chip)

        @pl.when(~quartered(j))
        def _():
            for q in range(2):
                lift(2 * j + core, z, carried(j, q))

    def both_sides(j, d, action):
        s = 2 * j + core
        for b in (z - d, z + d):
            @pl.when((s < last) & (b >= 0) & (b < groups))
            def _():
                action(s, b)

    def hop_from(j, d):
        @pl.when(quartered(j))
        def _():
            def action(s, b):
                piece_arrived(s, b, chip)
                lift(s, b, chip)
                to_column(s, b, chip)
                to_row(s, b, chip)
                to_core(s, b, chip)

            both_sides(j, d, action)

        @pl.when(~quartered(j))
        def _():
            for q in range(2):
                def action(s, b):
                    r = carried(j, q)
                    piece_arrived(s, b, r)
                    lift(s, b, r)
                    (to_column if q else to_row)(s, b, r)
                    to_core(s, b, r)

                both_sides(j, d, action)

    def side_from(j, d):
        @pl.when(quartered(j))
        def _():
            def action(s, b):
                piece_arrived(s, b, column_chip)

                @pl.when(core == 1)
                def _():
                    to_row(s, b, column_chip)

                to_core(s, b, column_chip)
                piece_arrived(s, b, row_chip)

                @pl.when(core == 0)
                def _():
                    to_column(s, b, row_chip)

                to_core(s, b, row_chip)

            both_sides(j, d, action)

        @pl.when(~quartered(j))
        def _():
            for q in range(2):
                def action(s, b):
                    r = left_over(j, q)
                    piece_arrived(s, b, r)
                    to_core(s, b, r)

                both_sides(j, d, action)

    def far_from(j, d):
        def action(s, b):
            piece_arrived(s, b, 3 - chip)
            to_core(s, b, 3 - chip)

        both_sides(j, d, action)

    def twin(j):
        s = 2 * j + 1 - core
        for b in range(groups):
            @pl.when((s < last) | (b == z))
            def _():
                for r in range(4):
                    piece_arrived(s, b, r)

    def start_part(e, c):
        return amps.at[0, e, rows_of(c), :]

    def start_move(e, c, send, **where):
        return remote(start_part(e, c), start_part(e, c), send.at[c], start_recv.at[e, c], **where)

    def start_relay(e, c):
        @pl.when(has_up & (c <= z))
        def _():
            start_move(e, c, start_up, ch=z + 1).start()

        @pl.when(has_down & (c >= z))
        def _():
            start_move(e, c, start_down, ch=z - 1).start()

    def start_arrive_and_relay(e, c):
        @pl.when((c >= 0) & (c < groups))
        def _():
            start_move(e, c, start_up, sec=partner).wait_recv()
            start_relay(e, c)

    bounds[k, z] = jnp.concatenate(
        [limits[:, q * LANES : (q + 1) * LANES] for q in range(row_count // LANES)], axis=0
    ).astype(jnp.float32)
    loads = [
        pltpu.make_async_copy(own_block, basis.at[k, rows_of(z), :], local_sem.at[0]),
    ]
    for half in range(2):
        for owner, source, target in (
            (k, pl.ds(0, energy_count), pl.ds(0, energy_count)),
            (across, pl.ds(shared, EXTRA), pl.ds(energy_count, EXTRA)),
        ):
            loads.append(pltpu.make_async_copy(
                start.at[source, :, pl.ds(pl.multiple_of(half * half_cols + owner * width, width), width)],
                amps.at[0, target, rows_of(z), pl.ds(half * width, width)], local_sem.at[len(loads)]))
    for load in loads:
        load.start()

    barrier = pltpu.get_barrier_semaphore()

    for near_by in (partner, column_peer, row_peer):
        pl.semaphore_signal(barrier, inc=1, device_id={"sec": near_by}, device_id_type=pl.DeviceIdType.MESH)

    @pl.when(has_up)
    def _():
        pl.semaphore_signal(barrier, inc=1, device_id={"ch": z + 1}, device_id_type=pl.DeviceIdType.MESH)

    @pl.when(has_down)
    def _():
        pl.semaphore_signal(barrier, inc=1, device_id={"ch": z - 1}, device_id_type=pl.DeviceIdType.MESH)

    line_peers = jnp.minimum(z, 1) + jnp.minimum(groups - 1 - z, 1)
    pl.semaphore_wait(barrier, 3 + line_peers)
    loads[0].wait()

    give_own()
    for load in loads[1:]:
        load.wait()

    def bound_move(b, turned):
        send, target = (bound_send.at[1, b], z - 1) if turned else (bound_send.at[0, b], z + 1)
        return remote(bounds.at[k, b], bounds.at[k, b], send, bound_recv.at[b], ch=target)

    def each_bound(b, action):
        @pl.when(has_up & (b <= z))
        def _():
            action(bound_move(b, 0))

        @pl.when(has_down & (b >= z))
        def _():
            action(bound_move(b, 1))

    each_bound(z, lambda move: move.start())

    def bound_from(d):
        for b in (z - d, z + d):
            @pl.when((b >= 0) & (b < groups))
            def _():
                bound_move(b, 0).wait_recv()
                each_bound(b, lambda move: move.start())

    def spread_move(step):
        return remote(bounds.at[k], bounds.at[k], spread_send.at[step], spread_recv.at[k], sec=(k + step) % sectors)

    def spread():
        @pl.loop(1, sectors)
        def _(step):
            spread_move(step).start()

    def meet(turn_of):
        target = jnp.where(turn_of == 0, partner, column_peer)
        pl.semaphore_signal(met.at[turn_of], inc=1, device_id={"sec": target}, device_id_type=pl.DeviceIdType.MESH)
        pl.semaphore_wait(met.at[turn_of], 1)

    def angles(s):
        @pl.when(s != k)
        def _():
            remote(bounds.at[s], bounds.at[s], spread_send.at[0], spread_recv.at[s], sec=partner).wait_recv()

        floor = jnp.concatenate([bounds[s, c] for c in range(groups)], axis=0)
        wavenumber = jnp.concatenate([jnp.sqrt(energies[e] - floor) for e in range(energy_count)], axis=0)
        cosine, sine = cos_and_sin(wavenumber)
        shear, turned = (1.0 - cosine) / (wavenumber * sine), -wavenumber * sine
        for e in range(energy_count):
            own = slice(e * chunks, (e + 1) * chunks)
            turn[s, e] = jnp.concatenate([shear[own], turned[own]], axis=0).T

    def rotate(s, e, m):
        source = jnp.minimum(s, 1)
        factors = turn[s, jnp.where(e < energy_count, e, e - EXTRA)]
        for q in range(chunks):
            place = pl.ds(q * LANES, LANES)
            both = amps[source, e, place, :].astype(jnp.float32)
            shear, turned = factors[:, q : q + 1], factors[:, chunks + q : chunks + q + 1]
            values_part, slopes_part = both[:, :width], both[:, width:]
            values_part = values_part + shear * slopes_part
            slopes_part = slopes_part + turned * values_part
            values_part = values_part + shear * slopes_part
            rotated[m, place, pl.ds(0, width)] = values_part.astype(jnp.bfloat16)
            rotated[m, place, pl.ds(width, width)] = slopes_part.astype(jnp.bfloat16)

    def keep(s, group, mine_of):
        @pl.when(group < energy_count // PAIRED)
        def _():
            for m in range(PAIRED):
                mine = mine_of(m)
                kept[s, 0, PAIRED * group + m] = mine[:, :width]
                kept[s, 1, PAIRED * group + m] = mine[:, width:]

        @pl.when((group >= energy_count // PAIRED) & (s // 2 == chip))
        def _():
            for m in range(PAIRED):
                mine = mine_of(m)
                doubled[s % 2, 0, PAIRED * group + m - energy_count] = mine[:, :width]
                doubled[s % 2, 1, PAIRED * group + m - energy_count] = mine[:, width:]

    def advance(s, group):
        wanted = (group < energy_count // PAIRED) | (s // 2 <= chip)

        @pl.when(wanted & (s < last))
        def _():
            for m in range(PAIRED):
                rotate(s, PAIRED * group + m, m)
            for m in range(PAIRED):
                e = PAIRED * group + m
                amps[1, e] = jnp.dot(basis[s], rotated[m], preferred_element_type=jnp.float32).astype(jnp.bfloat16)
            keep(s, group, lambda m: amps[1, PAIRED * group + m, rows_of(z), :])

        @pl.when(wanted & (s == last))
        def _():
            for m in range(PAIRED):
                rotate(s, PAIRED * group + m, m)
            for m in range(PAIRED):
                mine = jnp.dot(basis[s, rows_of(z), :], rotated[m], preferred_element_type=jnp.float32)
                amps[1, PAIRED * group + m, rows_of(z), :] = mine.astype(jnp.bfloat16)
            keep(s, group, lambda m: amps[1, PAIRED * group + m, rows_of(z), :])

    def columns_of(owner, half):
        return pl.ds(pl.multiple_of(half * half_cols + owner * width, width), width)

    def send_out(s, e):
        for half in range(2):
            part = kept.at[s, half, e]
            place = out.at[e, :, columns_of(k, half)]

            @pl.when(s == k)
            def _():
                pltpu.make_async_copy(part, place, out_local.at[0]).start()

            @pl.when((s != k) & ((e < shared) | (s // 2 != across_chip)))
            def _():
                remote(part, place, out_send.at[s], out_recv.at[k], sec=s).start()

    def send_doubled(s, e):
        for half in range(2):
            part = doubled.at[s % 2, half, e - energy_count]
            place = out.at[e - EXTRA, :, columns_of(across, half)]

            @pl.when(s == k)
            def _():
                pltpu.make_async_copy(part, place, doubled_sem.at[0]).start()

            @pl.when(s == partner)
            def _():
                remote(part, place, doubled_sem.at[1], doubled_sem.at[2], sec=partner).start()

    bits = max(sectors - 1, energy_count + EXTRA - 1, groups - 1).bit_length()
    span = 2 * bits + END.bit_length()
    packed = max(1, 30 // span)
    codes = [(kind << 2 * bits) | (first << bits) | second for kind, first, second in (*order, (END, 0, 0))]
    words = [
        sum(code << span * place for place, code in enumerate(codes[at : at + packed]))
        for at in range(0, len(codes), packed)
    ]
    low = 2**bits

    def entry(at, place):
        values = words
        while len(values) > 1:
            odd = (at & 1) == 1
            values = [
                jnp.where(odd, values[i + 1], values[i]) if i + 1 < len(values) else values[i]
                for i in range(0, len(values), 2)
            ]
            at = lax.shift_right_logical(at, jnp.int32(1))
        word = values[0]
        for step in range(1, packed):
            word = jnp.where(place == step, lax.shift_right_logical(values[0], jnp.int32(span * step)), word)
        word = word & (2**span - 1)
        return (
            lax.shift_right_logical(word, jnp.int32(2 * bits)),
            lax.shift_right_logical(word, jnp.int32(bits)) & (low - 1),
            word & (low - 1),
        )

    def act(n, before):
        at, place = before[3:]
        kind, first, second = entry(at, place)
        wrapped = place == packed - 1

        @pl.when(kind == STEP)
        def _():
            advance(first, second)

        @pl.when(kind == ANGLES)
        def _():
            angles(first)

        @pl.when(kind == HOME)
        def _():
            home(first)

        @pl.when(kind == LIFT)
        def _():
            lift_own(first)

        @pl.when(kind == HOP)
        def _():
            hop_from(first, second)

        @pl.when(kind == SIDE)
        def _():
            side_from(first, second)

        @pl.when(kind == MEET)
        def _():
            meet(first)

        @pl.when(kind == BOUND)
        def _():
            bound_from(first)

        @pl.when(kind == SPREAD)
        def _():
            spread()

        @pl.when(kind == FAR)
        def _():
            far_from(first, second)

        @pl.when(kind == TWIN)
        def _():
            twin(first)

        @pl.when(kind == FEED)
        def _():
            start_relay(first, z)

        @pl.when(kind == FEED_HOP)
        def _():
            start_arrive_and_relay(first, z - second)
            start_arrive_and_relay(first, z + second)

        @pl.when(before[0] == STEP)
        def _():
            @pl.when(before[2] < energy_count // PAIRED)
            def _():
                for m in range(PAIRED):
                    send_out(before[1], PAIRED * before[2] + m)

            @pl.when(before[2] >= energy_count // PAIRED)
            def _():
                for m in range(PAIRED):
                    send_doubled(before[1], PAIRED * before[2] + m)

        return kind, first, second, jnp.where(wrapped, at + 1, at), jnp.where(wrapped, 0, place + 1)

    lax.fori_loop(0, len(codes), act, (jnp.int32(END),) + (jnp.int32(0),) * 4)

    for b in range(groups):
        each_bound(b, lambda move: move.wait_send())

    @pl.loop(1, sectors)
    def _(step):
        spread_move(step).wait_send()

    def drain(send, s, b, count, **where):
        part = part_of(s, 0, 0, count)
        remote(part, part, send.at[s // 2, b], block_recv.at[s, b, 0], **where).wait_send()

    @pl.loop(0, pairs)
    def _(j):
        s = 2 * j + core
        for b in range(groups):
            @pl.when((s < last) | (b == z))
            def _():
                drain(core_send, s, b, 4, sec=partner)

            for pieces, wanted in ((1, quartered(j)), (2, ~quartered(j))):
                @pl.when((s < last) & has_up & (b <= z) & wanted)
                def _():
                    drain(up_send, s, b, pieces, ch=z + 1)

                @pl.when((s < last) & has_down & (b >= z) & wanted)
                def _():
                    drain(down_send, s, b, pieces, ch=z - 1)

            for send, target, turned in ((row_send, row_peer, 0), (column_send, column_peer, 1)):
                @pl.when((b == z) & (chip == j))
                def _():
                    drain(send, s, b, 4, sec=target)

                @pl.when((b == z) & (chip != j) & near(j, turned))
                def _():
                    drain(send, s, b, 2, sec=target)

                twice = quartered(j) & (core == 1 - turned)

                for pieces, wanted in ((2, twice), (1, ~twice)):
                    @pl.when((b != z) & (s < last) & wanted)
                    def _():
                        drain(send, s, b, pieces, sec=target)

    for c in range(groups):
        span = amps.at[0, :, pl.ds(c * row_count, row_count), :]

        @pl.when(has_up & (c <= z))
        def _():
            remote(span, span, start_up.at[c], start_recv.at[0, 0], ch=z + 1).wait_send()

        @pl.when(has_down & (c >= z))
        def _():
            remote(span, span, start_down.at[c], start_recv.at[0, 0], ch=z - 1).wait_send()

    @pl.loop(0, sectors)
    def _(s):
        @pl.when(s == k)
        def _():
            pltpu.make_async_copy(kept.at[s], kept.at[s], out_local.at[0]).wait()

        for far in range(2):
            part = kept.at[s, :, pl.ds(0, shared if far else energy_count)]
            move = remote(part, part, out_send.at[s], out_recv.at[s], sec=partner)

            @pl.when((s != k) & (s // 2 == across_chip if far else s // 2 != across_chip))
            def _():
                move.wait_send()
                move.wait_recv()

    pltpu.make_async_copy(doubled.at[0], doubled.at[0], doubled_sem.at[0]).wait()
    crossed = remote(doubled.at[0], doubled.at[0], doubled_sem.at[1], doubled_sem.at[2], sec=partner)
    crossed.wait_send()
    crossed.wait_recv()


def per_device_swept(start_amps, energies, thresholds, intersection):
    sectors = lax.axis_size("sec")
    groups = lax.axis_size("ch")
    energy_count, row_count, width_cols = start_amps.shape
    channel_count = intersection.shape[2]
    width = width_cols // 2 // sectors
    pairs = sectors // 2
    dma = pltpu.SemaphoreType.DMA
    stored = pltpu.VMEM(start_amps.shape, jnp.bfloat16)
    swept = pl.pallas_call(
        functools.partial(sweep_kernel, sectors, groups),
        out_shape=stored,
        in_specs=[
            pl.BlockSpec(memory_space=pl.ANY),
            pl.BlockSpec(memory_space=pltpu.SMEM),
            pl.BlockSpec(memory_space=pltpu.VMEM),
            pl.BlockSpec(memory_space=pl.ANY),
        ],
        out_specs=pl.BlockSpec(memory_space=pltpu.VMEM),
        scratch_shapes=[
            pltpu.VMEM((sectors, channel_count, channel_count), jnp.bfloat16),
            pltpu.VMEM((2, energy_count + EXTRA, channel_count, 2 * width), jnp.bfloat16),
            pltpu.VMEM((PAIRED, channel_count, 2 * width), jnp.bfloat16),
            pltpu.VMEM((sectors, 2, energy_count, row_count, width), jnp.bfloat16),
            pltpu.VMEM((2, 2, EXTRA, row_count, width), jnp.bfloat16),
            pltpu.VMEM((sectors, energy_count, LANES, 2 * (channel_count // LANES)), jnp.float32),
            pltpu.VMEM((sectors, groups, row_count // LANES, LANES), jnp.float32),
            dma((5,)),
            dma((sectors, groups, 4)),
            dma((pairs, groups)),
            dma((pairs, groups)),
            dma((pairs, groups)),
            dma((pairs, groups)),
            dma((pairs, groups)),
            dma((energy_count + EXTRA, groups)),
            dma((groups,)),
            dma((groups,)),
            dma((2, groups)),
            dma((groups,)),
            dma((sectors,)),
            dma((sectors,)),
            dma((1,)),
            dma((3,)),
            pltpu.SemaphoreType.REGULAR((2,)),
            dma((sectors,)),
            dma((sectors,)),
        ],
        compiler_params=pltpu.CompilerParams(
            collective_id=0, has_side_effects=True, vmem_limit_bytes=56 * 2**20
        ),
    )(start_amps, energies, thresholds, intersection[0])
    return swept[None]


GATHERED_LIMIT = 24 * 2**20


def per_device(start_amps, energies, thresholds, intersection):
    sectors = lax.axis_size("sec")
    row_count, channel_count = intersection.shape[1:]
    gathered_bytes = sectors * channel_count**2 * intersection.dtype.itemsize
    even = sectors // 2 == 4 and (start_amps.shape[2] // 2) % (sectors * LANES) == 0
    even = even and energies.shape[0] % PAIRED == 0 and energies.shape[0] > EXTRA and row_count % (4 * 16) == 0 and row_count % LANES == 0 and 3 * (channel_count // LANES) <= LANES
    if even and gathered_bytes <= GATHERED_LIMIT:
        return per_device_swept(start_amps, energies, thresholds, intersection)
    return per_device_pipelined(start_amps, energies, thresholds, intersection)


def solution(mesh):
    in_specs = (P(None, "ch", None), P(), P("sec", "ch"), P("sec", "ch", None))
    out_specs = P("sec", None, "ch", None)
    return jax.shard_map(
        per_device, mesh=mesh, in_specs=in_specs, out_specs=out_specs, check_vma=False
    )
```

```python
import functools
import math
import jax
import jax.numpy as jnp
from jax import lax
from jax.experimental import pallas as pl
from jax.experimental.pallas import tpu as pltpu
from jax.sharding import PartitionSpec as P


def passed_along(value, axis, steps):
    count = lax.axis_size(axis)
    leading, last = (max(0, -steps), min(count, count - steps))
    return lax.ppermute(value, axis, [(source, source + steps) for source in range(leading, last)])


def per_device_pipelined(start_amps, energies, thresholds, intersection):
    sectors = lax.axis_size("sec")
    sector_index = lax.axis_index("sec")
    groups = lax.axis_size("ch")
    energy_count = energies.shape[0]
    step_count = sectors + energy_count - 1
    row_count = intersection.shape[1]
    width_cols = start_amps.shape[2]
    half_cols = width_cols // 2
    col_width = half_cols // groups
    intersection_whole, thresholds_whole = (
        lax.all_gather(intersection, "ch", axis=1, tiled=True),
        lax.all_gather(thresholds, "ch", axis=1, tiled=True),
    )
    basis_change = intersection_whole[0]
    channel_thresholds = thresholds_whole[0].astype(jnp.float32)
    channel_count = basis_change.shape[0]
    paired = start_amps.reshape(energy_count, row_count, 2, half_cols)
    start_cols = lax.all_to_all(paired, "ch", split_axis=3, concat_axis=1, tiled=True)
    stored_init = jnp.zeros((energy_count, channel_count, 2, col_width), jnp.bfloat16)

    def multiply(flat):
        return jnp.dot(basis_change, flat, preferred_element_type=jnp.float32).astype(jnp.bfloat16)

    def skipped(flat):
        return jnp.zeros((channel_count, 2 * col_width), jnp.bfloat16)

    def step(step_index, state_pair):
        outgoing, stored = state_pair
        incoming = passed_along(outgoing, "sec", 1)
        energy_raw = step_index - sector_index
        active = (energy_raw >= 0) & (energy_raw < energy_count)
        energy_slot = jnp.clip(energy_raw, 0, energy_count - 1)
        initial = lax.dynamic_index_in_dim(start_cols, energy_slot, 0, keepdims=False)
        source = jnp.where(sector_index == 0, initial, incoming).astype(jnp.float32)
        wavenumber = jnp.sqrt(energies[energy_slot] - channel_thresholds)[:, None]
        values_part = source[:, 0, :]
        slopes_part = source[:, 1, :]
        cosine = jnp.cos(wavenumber)
        sine_term = jnp.sin(wavenumber)
        new_values = cosine * values_part + sine_term / wavenumber * slopes_part
        new_slopes = -wavenumber * sine_term * values_part + cosine * slopes_part
        rotated = jnp.stack([new_values, new_slopes], axis=1).astype(jnp.bfloat16)
        flat = rotated.reshape(channel_count, 2 * col_width)
        fresh = lax.cond(active, multiply, skipped, flat)
        fresh = fresh.reshape(channel_count, 2, col_width)
        previous = lax.dynamic_index_in_dim(stored, energy_slot, 0, keepdims=False)
        kept = jnp.where(active, fresh, previous)
        stored = lax.dynamic_update_index_in_dim(stored, kept, energy_slot, 0)
        return (fresh, stored)

    outgoing_init = jnp.zeros((channel_count, 2, col_width), jnp.bfloat16)
    final_pair = lax.fori_loop(0, step_count, step, (outgoing_init, stored_init))
    returned = lax.all_to_all(final_pair[1], "ch", split_axis=1, concat_axis=3, tiled=True)
    return returned.reshape(energy_count, row_count, width_cols)[None]


LANES = 128
PAIRED = 2
EXTRA = 2
QUARTERED = (0, 1)
HOME, LIFT, HOP, SIDE, TWIN, FEED, FEED_HOP, STEP, FAR, ANGLES, MEET, BOUND, SPREAD, END = range(14)
TUNED = (
    (5, 1, 0), (5, 0, 0), (6, 1, 1), (6, 0, 1), (6, 1, 2), (5, 2, 0), (0, 1, 0), (1, 1, 0), (0, 2, 0), (1, 2, 0),
    (0, 3, 0), (0, 0, 0), (2, 1, 1), (1, 0, 0), (2, 1, 2), (2, 0, 1), (2, 1, 3), (2, 0, 2), (3, 1, 2), (1, 3, 0),
    (2, 0, 3), (3, 1, 3), (2, 3, 1), (3, 0, 3), (3, 0, 1), (6, 0, 2), (3, 0, 2), (3, 1, 1), (2, 2, 1), (8, 0, 3),
    (6, 0, 3), (8, 1, 2), (2, 2, 2), (8, 0, 2), (8, 1, 3), (8, 0, 1), (2, 2, 3), (2, 3, 2), (3, 3, 1), (6, 1, 3),
    (8, 1, 1), (4, 0, 0), (5, 3, 0), (7, 0, 0), (2, 3, 3), (7, 1, 0), (3, 2, 1), (6, 2, 1), (3, 2, 3), (3, 2, 2),
    (4, 1, 0), (7, 2, 0), (6, 3, 1), (7, 3, 0), (3, 3, 3), (3, 3, 2), (5, 4, 0), (5, 5, 0), (4, 2, 0), (7, 4, 0),
    (7, 5, 0), (4, 3, 0), (7, 6, 0), (6, 3, 2), (7, 7, 0), (6, 2, 2), (6, 2, 3), (6, 3, 3), (7, 0, 1), (7, 1, 1),
    (5, 6, 0), (6, 4, 1), (7, 2, 1), (6, 5, 1), (7, 3, 1), (7, 4, 1), (6, 4, 2), (7, 5, 1), (6, 5, 2), (7, 6, 1),
    (6, 4, 3), (5, 7, 0), (6, 6, 1), (6, 5, 3), (7, 0, 2), (7, 1, 2), (7, 7, 1), (6, 7, 1), (7, 2, 2), (6, 6, 2),
    (7, 3, 2), (6, 7, 2), (7, 4, 2), (7, 5, 2), (6, 6, 3), (7, 6, 2), (6, 7, 3), (7, 0, 3), (7, 1, 3), (7, 2, 3),
    (7, 3, 3), (7, 7, 2), (7, 4, 3), (7, 5, 3), (7, 6, 3), (7, 7, 3),
)


def plain_order(pairs, sectors, energy_count, groups):
    order = [(HOME, j, 0) for j in range(pairs)]
    order += [(FEED, e, 0) for e in range(energy_count + EXTRA)] + [(LIFT, j, 0) for j in range(pairs)]
    for tick in range(pairs + groups + 1):
        for d in range(groups - 1, 0, -1):
            if 0 <= tick - d < pairs:
                order.append((HOP, tick - d, d))
            if 0 <= tick - d - 1 < pairs:
                order.append((SIDE, tick - d - 1, d))
            if 0 <= tick - d - 2 < pairs and tick - d - 2 in QUARTERED:
                order.append((FAR, tick - d - 2, d))
    order += [(TWIN, j, 0) for j in range(pairs)]
    for e in range(energy_count + EXTRA):
        order += [(FEED_HOP, e, d) for d in range(1, groups)]
        if (e + 1) % PAIRED == 0:
            order += [(STEP, s, e // PAIRED) for s in range(sectors)]
    return order


def order_of(pairs, sectors, energy_count, groups):
    plain = plain_order(pairs, sectors, energy_count, groups)
    chosen = TUNED if sorted(TUNED) == sorted(plain) else plain
    order, left = [], [(MEET, 0, 0), (BOUND, 1, 0), (MEET, 1, 0)]
    left += [(BOUND, d, 0) for d in range(2, groups)] + [(SPREAD, 0, 0)]
    left += [(ANGLES, s, 0) for s in range(sectors)]
    for entry in chosen:
        while left and entry[0] == STEP:
            order.append(left.pop(0))
        order.append(entry)
        if left:
            order.append(left.pop(0))
    return order


def cos_and_sin(w):
    u = (w - jnp.float32(1.57079637050628662109375)) + jnp.float32(4.37113900018624283e-8)
    square = u * u
    odd = even = None
    for power in range(12, -1, -2):
        even = (0.0 if even is None else even * square) + (-1.0) ** (power // 2) / math.factorial(power)
        odd = (0.0 if odd is None else odd * square) + (-1.0) ** (power // 2) / math.factorial(power + 1)
    return -u * odd, even


def sweep_kernel(
    sectors, groups, start, energies, limits, own_block, out,
    basis, amps, rotated, kept, doubled, turn, bounds,
    local_sem, block_recv, column_send, row_send, up_send, down_send, core_send,
    start_recv, start_up, start_down, bound_send, bound_recv, out_send, out_recv, out_local, doubled_sem, met, spread_send, spread_recv,
):
    k = lax.axis_index("sec")
    z = lax.axis_index("ch")
    core = k % 2
    chip = k // 2
    column, row = chip % 2, chip // 2
    partner = k + 1 - 2 * core
    column_peer = k + 2 - 4 * column
    row_peer = k + 4 - 8 * row
    pairs = sectors // 2
    last = sectors - 1
    energy_count, row_count, width_cols = start.shape
    half_cols = width_cols // 2
    width = half_cols // sectors
    channel_count = row_count * groups
    chunks = channel_count // LANES
    across = column_peer + row_peer - k
    across_chip = across // 2
    shared = energy_count - EXTRA
    has_up = z + 1 < groups
    has_down = z >= 1
    piece = row_count // 4
    order = order_of(pairs, sectors, energy_count, groups)

    def remote(src, dst, send, recv, **where):
        return pltpu.make_async_remote_copy(
            src_ref=src, dst_ref=dst, send_sem=send, recv_sem=recv,
            device_id=where, device_id_type=pl.DeviceIdType.MESH,
        )

    def rows_of(c):
        return pl.ds(pl.multiple_of(c * row_count, row_count), row_count)

    def part_of(s, b, r, count=1):
        return basis.at[s, pl.ds(pl.multiple_of(b * row_count + r * piece, piece), count * piece), :]

    def piece_move(s, b, r, send, **where):
        part = part_of(s, b, r)
        return remote(part, part, send.at[s // 2, b], block_recv.at[s, b, r], **where)

    column_chip, row_chip = chip + 1 - 2 * column, chip + 2 - 4 * row

    def quartered(j):
        found = j < 0
        for pair in QUARTERED:
            found = found | (j == pair)
        return found

    def near(j, q):
        return row == j // 2 if q == 0 else column == j % 2

    def carried(j, q):
        return jnp.where(near(j, q), 2 * q, 2 * q + 1)

    def left_over(j, q):
        return jnp.where(near(j, q), 2 * q + 1, 2 * q)

    def lift(s, b, r):
        @pl.when((s < last) & has_up & (b <= z))
        def _():
            piece_move(s, b, r, up_send, ch=z + 1).start()

        @pl.when((s < last) & has_down & (b >= z))
        def _():
            piece_move(s, b, r, down_send, ch=z - 1).start()

    def to_column(s, b, r):
        piece_move(s, b, r, column_send, sec=column_peer).start()

    def to_row(s, b, r):
        piece_move(s, b, r, row_send, sec=row_peer).start()

    def to_core(s, b, r):
        piece_move(s, b, r, core_send, sec=partner).start()

    def piece_arrived(s, b, r):
        piece_move(s, b, r, core_send, sec=partner).wait_recv()

    def give_own():
        for r in (1, 3, 0, 2):
            to_column(k, z, r)
            to_row(k, z, r)
        for r in (1, 3, 0, 2):
            to_core(k, z, r)

    def home(j):
        s = 2 * j + core

        @pl.when(chip != j)
        def _():
            for r in (1, 3, 0, 2):
                piece_arrived(s, z, r)

                @pl.when(near(j, r // 2))
                def _():
                    (to_column if r // 2 else to_row)(s, z, r)

                to_core(s, z, r)

    def lift_own(j):
        @pl.when(quartered(j))
        def _():
            lift(2 * j + core, z, chip)

        @pl.when(~quartered(j))
        def _():
            for q in range(2):
                lift(2 * j + core, z, carried(j, q))

    def both_sides(j, d, action):
        s = 2 * j + core
        for b in (z - d, z + d):
            @pl.when((s < last) & (b >= 0) & (b < groups))
            def _():
                action(s, b)

    def hop_from(j, d):
        @pl.when(quartered(j))
        def _():
            def action(s, b):
                piece_arrived(s, b, chip)
                lift(s, b, chip)
                to_column(s, b, chip)
                to_row(s, b, chip)
                to_core(s, b, chip)

            both_sides(j, d, action)

        @pl.when(~quartered(j))
        def _():
            for q in range(2):
                def action(s, b):
                    r = carried(j, q)
                    piece_arrived(s, b, r)
                    lift(s, b, r)
                    (to_column if q else to_row)(s, b, r)
                    to_core(s, b, r)

                both_sides(j, d, action)

    def side_from(j, d):
        @pl.when(quartered(j))
        def _():
            def action(s, b):
                piece_arrived(s, b, column_chip)

                @pl.when(core == 1)
                def _():
                    to_row(s, b, column_chip)

                to_core(s, b, column_chip)
                piece_arrived(s, b, row_chip)

                @pl.when(core == 0)
                def _():
                    to_column(s, b, row_chip)

                to_core(s, b, row_chip)

            both_sides(j, d, action)

        @pl.when(~quartered(j))
        def _():
            for q in range(2):
                def action(s, b):
                    r = left_over(j, q)
                    piece_arrived(s, b, r)
                    to_core(s, b, r)

                both_sides(j, d, action)

    def far_from(j, d):
        def action(s, b):
            piece_arrived(s, b, 3 - chip)
            to_core(s, b, 3 - chip)

        both_sides(j, d, action)

    def twin(j):
        s = 2 * j + 1 - core
        for b in range(groups):
            @pl.when((s < last) | (b == z))
            def _():
                for r in range(4):
                    piece_arrived(s, b, r)

    def start_part(e, c):
        return amps.at[0, e, rows_of(c), :]

    def start_move(e, c, send, **where):
        return remote(start_part(e, c), start_part(e, c), send.at[c], start_recv.at[e, c], **where)

    def start_relay(e, c):
        @pl.when(has_up & (c <= z))
        def _():
            start_move(e, c, start_up, ch=z + 1).start()

        @pl.when(has_down & (c >= z))
        def _():
            start_move(e, c, start_down, ch=z - 1).start()

    def start_arrive_and_relay(e, c):
        @pl.when((c >= 0) & (c < groups))
        def _():
            start_move(e, c, start_up, sec=partner).wait_recv()
            start_relay(e, c)

    bounds[k, z] = jnp.concatenate(
        [limits[:, q * LANES : (q + 1) * LANES] for q in range(row_count // LANES)], axis=0
    ).astype(jnp.float32)
    loads = [
        pltpu.make_async_copy(own_block, basis.at[k, rows_of(z), :], local_sem.at[0]),
    ]
    for half in range(2):
        for owner, source, target in (
            (k, pl.ds(0, energy_count), pl.ds(0, energy_count)),
            (across, pl.ds(shared, EXTRA), pl.ds(energy_count, EXTRA)),
        ):
            loads.append(pltpu.make_async_copy(
                start.at[source, :, pl.ds(pl.multiple_of(half * half_cols + owner * width, width), width)],
                amps.at[0, target, rows_of(z), pl.ds(half * width, width)], local_sem.at[len(loads)]))
    for load in loads:
        load.start()

    barrier = pltpu.get_barrier_semaphore()

    for near_by in (partner, column_peer, row_peer):
        pl.semaphore_signal(barrier, inc=1, device_id={"sec": near_by}, device_id_type=pl.DeviceIdType.MESH)

    @pl.when(has_up)
    def _():
        pl.semaphore_signal(barrier, inc=1, device_id={"ch": z + 1}, device_id_type=pl.DeviceIdType.MESH)

    @pl.when(has_down)
    def _():
        pl.semaphore_signal(barrier, inc=1, device_id={"ch": z - 1}, device_id_type=pl.DeviceIdType.MESH)

    line_peers = jnp.minimum(z, 1) + jnp.minimum(groups - 1 - z, 1)
    pl.semaphore_wait(barrier, 3 + line_peers)
    loads[0].wait()

    give_own()
    for load in loads[1:]:
        load.wait()

    def bound_move(b, turned):
        send, target = (bound_send.at[1, b], z - 1) if turned else (bound_send.at[0, b], z + 1)
        return remote(bounds.at[k, b], bounds.at[k, b], send, bound_recv.at[b], ch=target)

    def each_bound(b, action):
        @pl.when(has_up & (b <= z))
        def _():
            action(bound_move(b, 0))

        @pl.when(has_down & (b >= z))
        def _():
            action(bound_move(b, 1))

    each_bound(z, lambda move: move.start())

    def bound_from(d):
        for b in (z - d, z + d):
            @pl.when((b >= 0) & (b < groups))
            def _():
                bound_move(b, 0).wait_recv()
                each_bound(b, lambda move: move.start())

    def spread_move(step):
        return remote(bounds.at[k], bounds.at[k], spread_send.at[step], spread_recv.at[k], sec=(k + step) % sectors)

    def spread():
        @pl.loop(1, sectors)
        def _(step):
            spread_move(step).start()

    def meet(turn_of):
        target = jnp.where(turn_of == 0, partner, column_peer)
        pl.semaphore_signal(met.at[turn_of], inc=1, device_id={"sec": target}, device_id_type=pl.DeviceIdType.MESH)
        pl.semaphore_wait(met.at[turn_of], 1)

    def angles(s):
        @pl.when(s != k)
        def _():
            remote(bounds.at[s], bounds.at[s], spread_send.at[0], spread_recv.at[s], sec=partner).wait_recv()

        floor = jnp.concatenate([bounds[s, c] for c in range(groups)], axis=0)
        wavenumber = jnp.concatenate([jnp.sqrt(energies[e] - floor) for e in range(energy_count)], axis=0)
        cosine, sine = cos_and_sin(wavenumber)
        shear, turned = (1.0 - cosine) / (wavenumber * sine), -wavenumber * sine
        for e in range(energy_count):
            own = slice(e * chunks, (e + 1) * chunks)
            turn[s, e] = jnp.concatenate([shear[own], turned[own]], axis=0).T

    def rotate(s, e, m):
        source = jnp.minimum(s, 1)
        factors = turn[s, jnp.where(e < energy_count, e, e - EXTRA)]
        for q in range(chunks):
            place = pl.ds(q * LANES, LANES)
            both = amps[source, e, place, :].astype(jnp.float32)
            shear, turned = factors[:, q : q + 1], factors[:, chunks + q : chunks + q + 1]
            values_part, slopes_part = both[:, :width], both[:, width:]
            values_part = values_part + shear * slopes_part
            slopes_part = slopes_part + turned * values_part
            values_part = values_part + shear * slopes_part
            rotated[m, place, pl.ds(0, width)] = values_part.astype(jnp.bfloat16)
            rotated[m, place, pl.ds(width, width)] = slopes_part.astype(jnp.bfloat16)

    def keep(s, group, mine_of):
        @pl.when(group < energy_count // PAIRED)
        def _():
            for m in range(PAIRED):
                mine = mine_of(m)
                kept[s, 0, PAIRED * group + m] = mine[:, :width]
                kept[s, 1, PAIRED * group + m] = mine[:, width:]

        @pl.when((group >= energy_count // PAIRED) & (s // 2 == chip))
        def _():
            for m in range(PAIRED):
                mine = mine_of(m)
                doubled[s % 2, 0, PAIRED * group + m - energy_count] = mine[:, :width]
                doubled[s % 2, 1, PAIRED * group + m - energy_count] = mine[:, width:]

    def advance(s, group):
        wanted = (group < energy_count // PAIRED) | (s // 2 <= chip)

        @pl.when(wanted & (s < last))
        def _():
            for m in range(PAIRED):
                rotate(s, PAIRED * group + m, m)
            for m in range(PAIRED):
                e = PAIRED * group + m
                amps[1, e] = jnp.dot(basis[s], rotated[m], preferred_element_type=jnp.float32).astype(jnp.bfloat16)
            keep(s, group, lambda m: amps[1, PAIRED * group + m, rows_of(z), :])

        @pl.when(wanted & (s == last))
        def _():
            for m in range(PAIRED):
                rotate(s, PAIRED * group + m, m)
            for m in range(PAIRED):
                mine = jnp.dot(basis[s, rows_of(z), :], rotated[m], preferred_element_type=jnp.float32)
                amps[1, PAIRED * group + m, rows_of(z), :] = mine.astype(jnp.bfloat16)
            keep(s, group, lambda m: amps[1, PAIRED * group + m, rows_of(z), :])

    def columns_of(owner, half):
        return pl.ds(pl.multiple_of(half * half_cols + owner * width, width), width)

    def send_out(s, e):
        for half in range(2):
            part = kept.at[s, half, e]
            place = out.at[e, :, columns_of(k, half)]

            @pl.when(s == k)
            def _():
                pltpu.make_async_copy(part, place, out_local.at[0]).start()

            @pl.when((s != k) & ((e < shared) | (s // 2 != across_chip)))
            def _():
                remote(part, place, out_send.at[s], out_recv.at[k], sec=s).start()

    def send_doubled(s, e):
        for half in range(2):
            part = doubled.at[s % 2, half, e - energy_count]
            place = out.at[e - EXTRA, :, columns_of(across, half)]

            @pl.when(s == k)
            def _():
                pltpu.make_async_copy(part, place, doubled_sem.at[0]).start()

            @pl.when(s == partner)
            def _():
                remote(part, place, doubled_sem.at[1], doubled_sem.at[2], sec=partner).start()

    bits = max(sectors - 1, energy_count + EXTRA - 1, groups - 1).bit_length()
    span = 2 * bits + END.bit_length()
    packed = max(1, 30 // span)
    codes = [(kind << 2 * bits) | (first << bits) | second for kind, first, second in (*order, (END, 0, 0))]
    words = [
        sum(code << span * place for place, code in enumerate(codes[at : at + packed]))
        for at in range(0, len(codes), packed)
    ]
    low = 2**bits

    def entry(at, place):
        values = words
        while len(values) > 1:
            odd = (at & 1) == 1
            values = [
                jnp.where(odd, values[i + 1], values[i]) if i + 1 < len(values) else values[i]
                for i in range(0, len(values), 2)
            ]
            at = lax.shift_right_logical(at, jnp.int32(1))
        word = values[0]
        for step in range(1, packed):
            word = jnp.where(place == step, lax.shift_right_logical(values[0], jnp.int32(span * step)), word)
        word = word & (2**span - 1)
        return (
            lax.shift_right_logical(word, jnp.int32(2 * bits)),
            lax.shift_right_logical(word, jnp.int32(bits)) & (low - 1),
            word & (low - 1),
        )

    def act(n, before):
        at, place = before[3:]
        kind, first, second = entry(at, place)
        wrapped = place == packed - 1

        @pl.when(kind == STEP)
        def _():
            advance(first, second)

        @pl.when(kind == ANGLES)
        def _():
            angles(first)

        @pl.when(kind == HOME)
        def _():
            home(first)

        @pl.when(kind == LIFT)
        def _():
            lift_own(first)

        @pl.when(kind == HOP)
        def _():
            hop_from(first, second)

        @pl.when(kind == SIDE)
        def _():
            side_from(first, second)

        @pl.when(kind == MEET)
        def _():
            meet(first)

        @pl.when(kind == BOUND)
        def _():
            bound_from(first)

        @pl.when(kind == SPREAD)
        def _():
            spread()

        @pl.when(kind == FAR)
        def _():
            far_from(first, second)

        @pl.when(kind == TWIN)
        def _():
            twin(first)

        @pl.when(kind == FEED)
        def _():
            start_relay(first, z)

        @pl.when(kind == FEED_HOP)
        def _():
            start_arrive_and_relay(first, z - second)
            start_arrive_and_relay(first, z + second)

        @pl.when(before[0] == STEP)
        def _():
            @pl.when(before[2] < energy_count // PAIRED)
            def _():
                for m in range(PAIRED):
                    send_out(before[1], PAIRED * before[2] + m)

            @pl.when(before[2] >= energy_count // PAIRED)
            def _():
                for m in range(PAIRED):
                    send_doubled(before[1], PAIRED * before[2] + m)

        return kind, first, second, jnp.where(wrapped, at + 1, at), jnp.where(wrapped, 0, place + 1)

    lax.fori_loop(0, len(codes), act, (jnp.int32(END),) + (jnp.int32(0),) * 4)

    for b in range(groups):
        each_bound(b, lambda move: move.wait_send())

    @pl.loop(1, sectors)
    def _(step):
        spread_move(step).wait_send()

    def drain(send, s, b, count, **where):
        part = part_of(s, 0, 0, count)
        remote(part, part, send.at[s // 2, b], block_recv.at[s, b, 0], **where).wait_send()

    @pl.loop(0, pairs)
    def _(j):
        s = 2 * j + core
        for b in range(groups):
            @pl.when((s < last) | (b == z))
            def _():
                drain(core_send, s, b, 4, sec=partner)

            for pieces, wanted in ((1, quartered(j)), (2, ~quartered(j))):
                @pl.when((s < last) & has_up & (b <= z) & wanted)
                def _():
                    drain(up_send, s, b, pieces, ch=z + 1)

                @pl.when((s < last) & has_down & (b >= z) & wanted)
                def _():
                    drain(down_send, s, b, pieces, ch=z - 1)

            for send, target, turned in ((row_send, row_peer, 0), (column_send, column_peer, 1)):
                @pl.when((b == z) & (chip == j))
                def _():
                    drain(send, s, b, 4, sec=target)

                @pl.when((b == z) & (chip != j) & near(j, turned))
                def _():
                    drain(send, s, b, 2, sec=target)

                twice = quartered(j) & (core == 1 - turned)

                for pieces, wanted in ((2, twice), (1, ~twice)):
                    @pl.when((b != z) & (s < last) & wanted)
                    def _():
                        drain(send, s, b, pieces, sec=target)

    for c in range(groups):
        span = amps.at[0, :, pl.ds(c * row_count, row_count), :]

        @pl.when(has_up & (c <= z))
        def _():
            remote(span, span, start_up.at[c], start_recv.at[0, 0], ch=z + 1).wait_send()

        @pl.when(has_down & (c >= z))
        def _():
            remote(span, span, start_down.at[c], start_recv.at[0, 0], ch=z - 1).wait_send()

    @pl.loop(0, sectors)
    def _(s):
        @pl.when(s == k)
        def _():
            pltpu.make_async_copy(kept.at[s], kept.at[s], out_local.at[0]).wait()

        for far in range(2):
            part = kept.at[s, :, pl.ds(0, shared if far else energy_count)]
            move = remote(part, part, out_send.at[s], out_recv.at[s], sec=partner)

            @pl.when((s != k) & (s // 2 == across_chip if far else s // 2 != across_chip))
            def _():
                move.wait_send()
                move.wait_recv()

    pltpu.make_async_copy(doubled.at[0], doubled.at[0], doubled_sem.at[0]).wait()
    crossed = remote(doubled.at[0], doubled.at[0], doubled_sem.at[1], doubled_sem.at[2], sec=partner)
    crossed.wait_send()
    crossed.wait_recv()


def per_device_swept(start_amps, energies, thresholds, intersection):
    sectors = lax.axis_size("sec")
    groups = lax.axis_size("ch")
    energy_count, row_count, width_cols = start_amps.shape
    channel_count = intersection.shape[2]
    width = width_cols // 2 // sectors
    pairs = sectors // 2
    dma = pltpu.SemaphoreType.DMA
    stored = pltpu.VMEM(start_amps.shape, jnp.bfloat16)
    swept = pl.pallas_call(
        functools.partial(sweep_kernel, sectors, groups),
        out_shape=stored,
        in_specs=[
            pl.BlockSpec(memory_space=pl.ANY),
            pl.BlockSpec(memory_space=pltpu.SMEM),
            pl.BlockSpec(memory_space=pltpu.VMEM),
            pl.BlockSpec(memory_space=pl.ANY),
        ],
        out_specs=pl.BlockSpec(memory_space=pltpu.VMEM),
        scratch_shapes=[
            pltpu.VMEM((sectors, channel_count, channel_count), jnp.bfloat16),
            pltpu.VMEM((2, energy_count + EXTRA, channel_count, 2 * width), jnp.bfloat16),
            pltpu.VMEM((PAIRED, channel_count, 2 * width), jnp.bfloat16),
            pltpu.VMEM((sectors, 2, energy_count, row_count, width), jnp.bfloat16),
            pltpu.VMEM((2, 2, EXTRA, row_count, width), jnp.bfloat16),
            pltpu.VMEM((sectors, energy_count, LANES, 2 * (channel_count // LANES)), jnp.float32),
            pltpu.VMEM((sectors, groups, row_count // LANES, LANES), jnp.float32),
            dma((5,)),
            dma((sectors, groups, 4)),
            dma((pairs, groups)),
            dma((pairs, groups)),
            dma((pairs, groups)),
            dma((pairs, groups)),
            dma((pairs, groups)),
            dma((energy_count + EXTRA, groups)),
            dma((groups,)),
            dma((groups,)),
            dma((2, groups)),
            dma((groups,)),
            dma((sectors,)),
            dma((sectors,)),
            dma((1,)),
            dma((3,)),
            pltpu.SemaphoreType.REGULAR((2,)),
            dma((sectors,)),
            dma((sectors,)),
        ],
        compiler_params=pltpu.CompilerParams(
            collective_id=0, has_side_effects=True, vmem_limit_bytes=56 * 2**20
        ),
    )(start_amps, energies, thresholds, intersection[0])
    return swept[None]


GATHERED_LIMIT = 24 * 2**20


def per_device(start_amps, energies, thresholds, intersection):
    sectors = lax.axis_size("sec")
    row_count, channel_count = intersection.shape[1:]
    gathered_bytes = sectors * channel_count**2 * intersection.dtype.itemsize
    even = sectors // 2 == 4 and (start_amps.shape[2] // 2) % (sectors * LANES) == 0
    even = even and energies.shape[0] % PAIRED == 0 and energies.shape[0] > EXTRA and row_count % (4 * 16) == 0 and row_count % LANES == 0 and 3 * (channel_count // LANES) <= LANES
    if even and gathered_bytes <= GATHERED_LIMIT:
        return per_device_swept(start_amps, energies, thresholds, intersection)
    return per_device_pipelined(start_amps, energies, thresholds, intersection)


def solution(mesh):
    in_specs = (P(None, "ch", None), P(), P("sec", "ch"), P("sec", "ch", None))
    out_specs = P("sec", None, "ch", None)
    return jax.shard_map(
        per_device, mesh=mesh, in_specs=in_specs, out_specs=out_specs, check_vma=False
    )
```

```python
import functools
import math
import jax
import jax.numpy as jnp
from jax import lax
from jax.experimental import pallas as pl
from jax.experimental.pallas import tpu as pltpu
from jax.sharding import PartitionSpec as P


def passed_along(value, axis, steps):
    count = lax.axis_size(axis)
    leading, last = (max(0, -steps), min(count, count - steps))
    return lax.ppermute(value, axis, [(source, source + steps) for source in range(leading, last)])


def per_device_pipelined(start_amps, energies, thresholds, intersection):
    sectors = lax.axis_size("sec")
    sector_index = lax.axis_index("sec")
    groups = lax.axis_size("ch")
    energy_count = energies.shape[0]
    step_count = sectors + energy_count - 1
    row_count = intersection.shape[1]
    width_cols = start_amps.shape[2]
    half_cols = width_cols // 2
    col_width = half_cols // groups
    intersection_whole, thresholds_whole = (
        lax.all_gather(intersection, "ch", axis=1, tiled=True),
        lax.all_gather(thresholds, "ch", axis=1, tiled=True),
    )
    basis_change = intersection_whole[0]
    channel_thresholds = thresholds_whole[0].astype(jnp.float32)
    channel_count = basis_change.shape[0]
    paired = start_amps.reshape(energy_count, row_count, 2, half_cols)
    start_cols = lax.all_to_all(paired, "ch", split_axis=3, concat_axis=1, tiled=True)
    stored_init = jnp.zeros((energy_count, channel_count, 2, col_width), jnp.bfloat16)

    def multiply(flat):
        return jnp.dot(basis_change, flat, preferred_element_type=jnp.float32).astype(jnp.bfloat16)

    def skipped(flat):
        return jnp.zeros((channel_count, 2 * col_width), jnp.bfloat16)

    def step(step_index, state_pair):
        outgoing, stored = state_pair
        incoming = passed_along(outgoing, "sec", 1)
        energy_raw = step_index - sector_index
        active = (energy_raw >= 0) & (energy_raw < energy_count)
        energy_slot = jnp.clip(energy_raw, 0, energy_count - 1)
        initial = lax.dynamic_index_in_dim(start_cols, energy_slot, 0, keepdims=False)
        source = jnp.where(sector_index == 0, initial, incoming).astype(jnp.float32)
        wavenumber = jnp.sqrt(energies[energy_slot] - channel_thresholds)[:, None]
        values_part = source[:, 0, :]
        slopes_part = source[:, 1, :]
        cosine = jnp.cos(wavenumber)
        sine_term = jnp.sin(wavenumber)
        new_values = cosine * values_part + sine_term / wavenumber * slopes_part
        new_slopes = -wavenumber * sine_term * values_part + cosine * slopes_part
        rotated = jnp.stack([new_values, new_slopes], axis=1).astype(jnp.bfloat16)
        flat = rotated.reshape(channel_count, 2 * col_width)
        fresh = lax.cond(active, multiply, skipped, flat)
        fresh = fresh.reshape(channel_count, 2, col_width)
        previous = lax.dynamic_index_in_dim(stored, energy_slot, 0, keepdims=False)
        kept = jnp.where(active, fresh, previous)
        stored = lax.dynamic_update_index_in_dim(stored, kept, energy_slot, 0)
        return (fresh, stored)

    outgoing_init = jnp.zeros((channel_count, 2, col_width), jnp.bfloat16)
    final_pair = lax.fori_loop(0, step_count, step, (outgoing_init, stored_init))
    returned = lax.all_to_all(final_pair[1], "ch", split_axis=1, concat_axis=3, tiled=True)
    return returned.reshape(energy_count, row_count, width_cols)[None]


LANES = 128
PAIRED = 2
EXTRA = 2
QUARTERED = (0, 1)
HOME, LIFT, HOP, SIDE, TWIN, FEED, FEED_HOP, STEP, FAR, ANGLES, MEET, BOUND, SPREAD, END = range(14)
TUNED = (
    (5, 1, 0), (5, 0, 0), (6, 1, 1), (6, 0, 1), (6, 1, 2), (5, 2, 0), (0, 1, 0), (1, 1, 0), (0, 2, 0), (1, 2, 0),
    (0, 3, 0), (0, 0, 0), (2, 1, 1), (1, 0, 0), (2, 1, 2), (2, 0, 1), (2, 1, 3), (2, 0, 2), (3, 1, 2), (1, 3, 0),
    (2, 0, 3), (3, 1, 3), (2, 3, 1), (3, 0, 3), (3, 0, 1), (6, 0, 2), (3, 0, 2), (3, 1, 1), (2, 2, 1), (8, 0, 3),
    (6, 0, 3), (8, 1, 2), (2, 2, 2), (8, 0, 2), (8, 1, 3), (8, 0, 1), (2, 2, 3), (2, 3, 2), (3, 3, 1), (6, 1, 3),
    (8, 1, 1), (4, 0, 0), (5, 3, 0), (7, 0, 0), (2, 3, 3), (7, 1, 0), (3, 2, 1), (6, 2, 1), (3, 2, 3), (3, 2, 2),
    (4, 1, 0), (7, 2, 0), (6, 3, 1), (7, 3, 0), (3, 3, 3), (3, 3, 2), (5, 4, 0), (5, 5, 0), (4, 2, 0), (7, 4, 0),
    (7, 5, 0), (4, 3, 0), (7, 6, 0), (6, 3, 2), (7, 7, 0), (6, 2, 2), (6, 2, 3), (6, 3, 3), (7, 0, 1), (7, 1, 1),
    (5, 6, 0), (6, 4, 1), (7, 2, 1), (6, 5, 1), (7, 3, 1), (7, 4, 1), (6, 4, 2), (7, 5, 1), (6, 5, 2), (7, 6, 1),
    (6, 4, 3), (5, 7, 0), (6, 6, 1), (6, 5, 3), (7, 0, 2), (7, 1, 2), (7, 7, 1), (6, 7, 1), (7, 2, 2), (6, 6, 2),
    (7, 3, 2), (6, 7, 2), (7, 4, 2), (7, 5, 2), (6, 6, 3), (7, 6, 2), (6, 7, 3), (7, 0, 3), (7, 1, 3), (7, 2, 3),
    (7, 3, 3), (7, 7, 2), (7, 4, 3), (7, 5, 3), (7, 6, 3), (7, 7, 3),
)


def plain_order(pairs, sectors, energy_count, groups):
    order = [(HOME, j, 0) for j in range(pairs)]
    order += [(FEED, e, 0) for e in range(energy_count + EXTRA)] + [(LIFT, j, 0) for j in range(pairs)]
    for tick in range(pairs + groups + 1):
        for d in range(groups - 1, 0, -1):
            if 0 <= tick - d < pairs:
                order.append((HOP, tick - d, d))
            if 0 <= tick - d - 1 < pairs:
                order.append((SIDE, tick - d - 1, d))
            if 0 <= tick - d - 2 < pairs and tick - d - 2 in QUARTERED:
                order.append((FAR, tick - d - 2, d))
    order += [(TWIN, j, 0) for j in range(pairs)]
    for e in range(energy_count + EXTRA):
        order += [(FEED_HOP, e, d) for d in range(1, groups)]
        if (e + 1) % PAIRED == 0:
            order += [(STEP, s, e // PAIRED) for s in range(sectors)]
    return order


def order_of(pairs, sectors, energy_count, groups):
    plain = plain_order(pairs, sectors, energy_count, groups)
    chosen = TUNED if sorted(TUNED) == sorted(plain) else plain
    order, left = [], [(MEET, 0, 0), (BOUND, 1, 0), (MEET, 1, 0)]
    left += [(BOUND, d, 0) for d in range(2, groups)] + [(SPREAD, 0, 0)]
    left += [(ANGLES, s, 0) for s in range(sectors)]
    for entry in chosen:
        while left and entry[0] == STEP:
            order.append(left.pop(0))
        order.append(entry)
        if left:
            order.append(left.pop(0))
    return order


def cos_and_sin(w):
    u = (w - jnp.float32(1.57079637050628662109375)) + jnp.float32(4.37113900018624283e-8)
    square = u * u
    odd = even = None
    for power in range(12, -1, -2):
        even = (0.0 if even is None else even * square) + (-1.0) ** (power // 2) / math.factorial(power)
        odd = (0.0 if odd is None else odd * square) + (-1.0) ** (power // 2) / math.factorial(power + 1)
    return -u * odd, even


def sweep_kernel(
    sectors, groups, start, energies, limits, own_block, out,
    basis, amps, rotated, kept, doubled, turn, bounds,
    local_sem, block_recv, column_send, row_send, up_send, down_send, core_send,
    start_recv, start_up, start_down, bound_send, bound_recv, out_send, out_recv, out_local, doubled_sem, met, spread_send, spread_recv,
):
    k = lax.axis_index("sec")
    z = lax.axis_index("ch")
    core = k % 2
    chip = k // 2
    column, row = chip % 2, chip // 2
    partner = k + 1 - 2 * core
    column_peer = k + 2 - 4 * column
    row_peer = k + 4 - 8 * row
    pairs = sectors // 2
    last = sectors - 1
    energy_count, row_count, width_cols = start.shape
    half_cols = width_cols // 2
    width = half_cols // sectors
    channel_count = row_count * groups
    chunks = channel_count // LANES
    across = column_peer + row_peer - k
    across_chip = across // 2
    shared = energy_count - EXTRA
    has_up = z + 1 < groups
    has_down = z >= 1
    piece = row_count // 4
    order = order_of(pairs, sectors, energy_count, groups)

    def remote(src, dst, send, recv, **where):
        return pltpu.make_async_remote_copy(
            src_ref=src, dst_ref=dst, send_sem=send, recv_sem=recv,
            device_id=where, device_id_type=pl.DeviceIdType.MESH,
        )

    def rows_of(c):
        return pl.ds(pl.multiple_of(c * row_count, row_count), row_count)

    def part_of(s, b, r, count=1):
        return basis.at[s, pl.ds(pl.multiple_of(b * row_count + r * piece, piece), count * piece), :]

    def piece_move(s, b, r, send, **where):
        part = part_of(s, b, r)
        return remote(part, part, send.at[s // 2, b], block_recv.at[s, b, r], **where)

    column_chip, row_chip = chip + 1 - 2 * column, chip + 2 - 4 * row

    def quartered(j):
        found = j < 0
        for pair in QUARTERED:
            found = found | (j == pair)
        return found

    def near(j, q):
        return row == j // 2 if q == 0 else column == j % 2

    def carried(j, q):
        return jnp.where(near(j, q), 2 * q, 2 * q + 1)

    def left_over(j, q):
        return jnp.where(near(j, q), 2 * q + 1, 2 * q)

    def lift(s, b, r):
        @pl.when((s < last) & has_up & (b <= z))
        def _():
            piece_move(s, b, r, up_send, ch=z + 1).start()

        @pl.when((s < last) & has_down & (b >= z))
        def _():
            piece_move(s, b, r, down_send, ch=z - 1).start()

    def to_column(s, b, r):
        piece_move(s, b, r, column_send, sec=column_peer).start()

    def to_row(s, b, r):
        piece_move(s, b, r, row_send, sec=row_peer).start()

    def to_core(s, b, r):
        piece_move(s, b, r, core_send, sec=partner).start()

    def piece_arrived(s, b, r):
        piece_move(s, b, r, core_send, sec=partner).wait_recv()

    def give_own():
        for r in (1, 3, 0, 2):
            to_column(k, z, r)
            to_row(k, z, r)
        for r in (1, 3, 0, 2):
            to_core(k, z, r)

    def home(j):
        s = 2 * j + core

        @pl.when(chip != j)
        def _():
            for r in (1, 3, 0, 2):
                piece_arrived(s, z, r)

                @pl.when(near(j, r // 2))
                def _():
                    (to_column if r // 2 else to_row)(s, z, r)

                to_core(s, z, r)

    def lift_own(j):
        @pl.when(quartered(j))
        def _():
            lift(2 * j + core, z, chip)

        @pl.when(~quartered(j))
        def _():
            for q in range(2):
                lift(2 * j + core, z, carried(j, q))

    def both_sides(j, d, action):
        s = 2 * j + core
        for b in (z - d, z + d):
            @pl.when((s < last) & (b >= 0) & (b < groups))
            def _():
                action(s, b)

    def hop_from(j, d):
        @pl.when(quartered(j))
        def _():
            def action(s, b):
                piece_arrived(s, b, chip)
                lift(s, b, chip)
                to_column(s, b, chip)
                to_row(s, b, chip)
                to_core(s, b, chip)

            both_sides(j, d, action)

        @pl.when(~quartered(j))
        def _():
            for q in range(2):
                def action(s, b):
                    r = carried(j, q)
                    piece_arrived(s, b, r)
                    lift(s, b, r)
                    (to_column if q else to_row)(s, b, r)
                    to_core(s, b, r)

                both_sides(j, d, action)

    def side_from(j, d):
        @pl.when(quartered(j))
        def _():
            def action(s, b):
                piece_arrived(s, b, column_chip)

                @pl.when(core == 1)
                def _():
                    to_row(s, b, column_chip)

                to_core(s, b, column_chip)
                piece_arrived(s, b, row_chip)

                @pl.when(core == 0)
                def _():
                    to_column(s, b, row_chip)

                to_core(s, b, row_chip)

            both_sides(j, d, action)

        @pl.when(~quartered(j))
        def _():
            for q in range(2):
                def action(s, b):
                    r = left_over(j, q)
                    piece_arrived(s, b, r)
                    to_core(s, b, r)

                both_sides(j, d, action)

    def far_from(j, d):
        def action(s, b):
            piece_arrived(s, b, 3 - chip)
            to_core(s, b, 3 - chip)

        both_sides(j, d, action)

    def twin(j):
        s = 2 * j + 1 - core
        for b in range(groups):
            @pl.when((s < last) | (b == z))
            def _():
                for r in range(4):
                    piece_arrived(s, b, r)

    def start_part(e, c):
        return amps.at[0, e, rows_of(c), :]

    def start_move(e, c, send, **where):
        return remote(start_part(e, c), start_part(e, c), send.at[c], start_recv.at[e, c], **where)

    def start_relay(e, c):
        @pl.when(has_up & (c <= z))
        def _():
            start_move(e, c, start_up, ch=z + 1).start()

        @pl.when(has_down & (c >= z))
        def _():
            start_move(e, c, start_down, ch=z - 1).start()

    def start_arrive_and_relay(e, c):
        @pl.when((c >= 0) & (c < groups))
        def _():
            start_move(e, c, start_up, sec=partner).wait_recv()
            start_relay(e, c)

    bounds[k, z] = jnp.concatenate(
        [limits[:, q * LANES : (q + 1) * LANES] for q in range(row_count // LANES)], axis=0
    ).astype(jnp.float32)
    loads = [
        pltpu.make_async_copy(own_block, basis.at[k, rows_of(z), :], local_sem.at[0]),
    ]
    for half in range(2):
        for owner, source, target in (
            (k, pl.ds(0, energy_count), pl.ds(0, energy_count)),
            (across, pl.ds(shared, EXTRA), pl.ds(energy_count, EXTRA)),
        ):
            loads.append(pltpu.make_async_copy(
                start.at[source, :, pl.ds(pl.multiple_of(half * half_cols + owner * width, width), width)],
                amps.at[0, target, rows_of(z), pl.ds(half * width, width)], local_sem.at[len(loads)]))
    for load in loads:
        load.start()

    barrier = pltpu.get_barrier_semaphore()

    for near_by in (partner, column_peer, row_peer):
        pl.semaphore_signal(barrier, inc=1, device_id={"sec": near_by}, device_id_type=pl.DeviceIdType.MESH)

    @pl.when(has_up)
    def _():
        pl.semaphore_signal(barrier, inc=1, device_id={"ch": z + 1}, device_id_type=pl.DeviceIdType.MESH)

    @pl.when(has_down)
    def _():
        pl.semaphore_signal(barrier, inc=1, device_id={"ch": z - 1}, device_id_type=pl.DeviceIdType.MESH)

    line_peers = jnp.minimum(z, 1) + jnp.minimum(groups - 1 - z, 1)
    pl.semaphore_wait(barrier, 3 + line_peers)
    loads[0].wait()

    give_own()
    for load in loads[1:]:
        load.wait()

    def bound_move(b, turned):
        send, target = (bound_send.at[1, b], z - 1) if turned else (bound_send.at[0, b], z + 1)
        return remote(bounds.at[k, b], bounds.at[k, b], send, bound_recv.at[b], ch=target)

    def each_bound(b, action):
        @pl.when(has_up & (b <= z))
        def _():
            action(bound_move(b, 0))

        @pl.when(has_down & (b >= z))
        def _():
            action(bound_move(b, 1))

    each_bound(z, lambda move: move.start())

    def bound_from(d):
        for b in (z - d, z + d):
            @pl.when((b >= 0) & (b < groups))
            def _():
                bound_move(b, 0).wait_recv()
                each_bound(b, lambda move: move.start())

    def spread_move(step):
        return remote(bounds.at[k], bounds.at[k], spread_send.at[step], spread_recv.at[k], sec=(k + step) % sectors)

    def spread():
        @pl.loop(1, sectors)
        def _(step):
            spread_move(step).start()

    def meet(turn_of):
        target = jnp.where(turn_of == 0, partner, column_peer)
        pl.semaphore_signal(met.at[turn_of], inc=1, device_id={"sec": target}, device_id_type=pl.DeviceIdType.MESH)
        pl.semaphore_wait(met.at[turn_of], 1)

    def angles(s):
        @pl.when(s != k)
        def _():
            remote(bounds.at[s], bounds.at[s], spread_send.at[0], spread_recv.at[s], sec=partner).wait_recv()

        floor = jnp.concatenate([bounds[s, c] for c in range(groups)], axis=0)
        wavenumber = jnp.concatenate([jnp.sqrt(energies[e] - floor) for e in range(energy_count)], axis=0)
        cosine, sine = cos_and_sin(wavenumber)
        shear, turned = (1.0 - cosine) / (wavenumber * sine), -wavenumber * sine
        for e in range(energy_count):
            own = slice(e * chunks, (e + 1) * chunks)
            turn[s, e] = jnp.concatenate([shear[own], turned[own]], axis=0).T

    def rotate(s, e, m):
        source = jnp.minimum(s, 1)
        factors = turn[s, jnp.where(e < energy_count, e, e - EXTRA)]
        for q in range(chunks):
            place = pl.ds(q * LANES, LANES)
            both = amps[source, e, place, :].astype(jnp.float32)
            shear, turned = factors[:, q : q + 1], factors[:, chunks + q : chunks + q + 1]
            values_part, slopes_part = both[:, :width], both[:, width:]
            values_part = values_part + shear * slopes_part
            slopes_part = slopes_part + turned * values_part
            values_part = values_part + shear * slopes_part
            rotated[m, place, pl.ds(0, width)] = values_part.astype(jnp.bfloat16)
            rotated[m, place, pl.ds(width, width)] = slopes_part.astype(jnp.bfloat16)

    def keep(s, group, mine_of):
        @pl.when(group < energy_count // PAIRED)
        def _():
            for m in range(PAIRED):
                mine = mine_of(m)
                kept[s, 0, PAIRED * group + m] = mine[:, :width]
                kept[s, 1, PAIRED * group + m] = mine[:, width:]

        @pl.when((group >= energy_count // PAIRED) & (s // 2 == chip))
        def _():
            for m in range(PAIRED):
                mine = mine_of(m)
                doubled[s % 2, 0, PAIRED * group + m - energy_count] = mine[:, :width]
                doubled[s % 2, 1, PAIRED * group + m - energy_count] = mine[:, width:]

    def advance(s, group):
        wanted = (group < energy_count // PAIRED) | (s // 2 <= chip)

        @pl.when(wanted & (s < last))
        def _():
            for m in range(PAIRED):
                rotate(s, PAIRED * group + m, m)
            for m in range(PAIRED):
                e = PAIRED * group + m
                amps[1, e] = jnp.dot(basis[s], rotated[m], preferred_element_type=jnp.float32).astype(jnp.bfloat16)
            keep(s, group, lambda m: amps[1, PAIRED * group + m, rows_of(z), :])

        @pl.when(wanted & (s == last))
        def _():
            for m in range(PAIRED):
                rotate(s, PAIRED * group + m, m)
            for m in range(PAIRED):
                mine = jnp.dot(basis[s, rows_of(z), :], rotated[m], preferred_element_type=jnp.float32)
                amps[1, PAIRED * group + m, rows_of(z), :] = mine.astype(jnp.bfloat16)
            keep(s, group, lambda m: amps[1, PAIRED * group + m, rows_of(z), :])

    def columns_of(owner, half):
        return pl.ds(pl.multiple_of(half * half_cols + owner * width, width), width)

    def send_out(s, e):
        for half in range(2):
            part = kept.at[s, half, e]
            place = out.at[e, :, columns_of(k, half)]

            @pl.when(s == k)
            def _():
                pltpu.make_async_copy(part, place, out_local.at[0]).start()

            @pl.when((s != k) & ((e < shared) | (s // 2 != across_chip)))
            def _():
                remote(part, place, out_send.at[s], out_recv.at[k], sec=s).start()

    def send_doubled(s, e):
        for half in range(2):
            part = doubled.at[s % 2, half, e - energy_count]
            place = out.at[e - EXTRA, :, columns_of(across, half)]

            @pl.when(s == k)
            def _():
                pltpu.make_async_copy(part, place, doubled_sem.at[0]).start()

            @pl.when(s == partner)
            def _():
                remote(part, place, doubled_sem.at[1], doubled_sem.at[2], sec=partner).start()

    bits = max(sectors - 1, energy_count + EXTRA - 1, groups - 1).bit_length()
    span = 2 * bits + END.bit_length()
    packed = max(1, 30 // span)
    codes = [(kind << 2 * bits) | (first << bits) | second for kind, first, second in (*order, (END, 0, 0))]
    words = [
        sum(code << span * place for place, code in enumerate(codes[at : at + packed]))
        for at in range(0, len(codes), packed)
    ]
    low = 2**bits

    def entry(at, place):
        values = words
        while len(values) > 1:
            odd = (at & 1) == 1
            values = [
                jnp.where(odd, values[i + 1], values[i]) if i + 1 < len(values) else values[i]
                for i in range(0, len(values), 2)
            ]
            at = lax.shift_right_logical(at, jnp.int32(1))
        word = values[0]
        for step in range(1, packed):
            word = jnp.where(place == step, lax.shift_right_logical(values[0], jnp.int32(span * step)), word)
        word = word & (2**span - 1)
        return (
            lax.shift_right_logical(word, jnp.int32(2 * bits)),
            lax.shift_right_logical(word, jnp.int32(bits)) & (low - 1),
            word & (low - 1),
        )

    def act(n, before):
        at, place = before[3:]
        kind, first, second = entry(at, place)
        wrapped = place == packed - 1

        @pl.when(kind == STEP)
        def _():
            advance(first, second)

        @pl.when(kind == ANGLES)
        def _():
            angles(first)

        @pl.when(kind == HOME)
        def _():
            home(first)

        @pl.when(kind == LIFT)
        def _():
            lift_own(first)

        @pl.when(kind == HOP)
        def _():
            hop_from(first, second)

        @pl.when(kind == SIDE)
        def _():
            side_from(first, second)

        @pl.when(kind == MEET)
        def _():
            meet(first)

        @pl.when(kind == BOUND)
        def _():
            bound_from(first)

        @pl.when(kind == SPREAD)
        def _():
            spread()

        @pl.when(kind == FAR)
        def _():
            far_from(first, second)

        @pl.when(kind == TWIN)
        def _():
            twin(first)

        @pl.when(kind == FEED)
        def _():
            start_relay(first, z)

        @pl.when(kind == FEED_HOP)
        def _():
            start_arrive_and_relay(first, z - second)
            start_arrive_and_relay(first, z + second)

        @pl.when(before[0] == STEP)
        def _():
            @pl.when(before[2] < energy_count // PAIRED)
            def _():
                for m in range(PAIRED):
                    send_out(before[1], PAIRED * before[2] + m)

            @pl.when(before[2] >= energy_count // PAIRED)
            def _():
                for m in range(PAIRED):
                    send_doubled(before[1], PAIRED * before[2] + m)

        return kind, first, second, jnp.where(wrapped, at + 1, at), jnp.where(wrapped, 0, place + 1)

    lax.fori_loop(0, len(codes), act, (jnp.int32(END),) + (jnp.int32(0),) * 4)

    for b in range(groups):
        each_bound(b, lambda move: move.wait_send())

    @pl.loop(1, sectors)
    def _(step):
        spread_move(step).wait_send()

    def drain(send, s, b, count, **where):
        part = part_of(s, 0, 0, count)
        remote(part, part, send.at[s // 2, b], block_recv.at[s, b, 0], **where).wait_send()

    @pl.loop(0, pairs)
    def _(j):
        s = 2 * j + core
        for b in range(groups):
            @pl.when((s < last) | (b == z))
            def _():
                drain(core_send, s, b, 4, sec=partner)

            for pieces, wanted in ((1, quartered(j)), (2, ~quartered(j))):
                @pl.when((s < last) & has_up & (b <= z) & wanted)
                def _():
                    drain(up_send, s, b, pieces, ch=z + 1)

                @pl.when((s < last) & has_down & (b >= z) & wanted)
                def _():
                    drain(down_send, s, b, pieces, ch=z - 1)

            for send, target, turned in ((row_send, row_peer, 0), (column_send, column_peer, 1)):
                @pl.when((b == z) & (chip == j))
                def _():
                    drain(send, s, b, 4, sec=target)

                @pl.when((b == z) & (chip != j) & near(j, turned))
                def _():
                    drain(send, s, b, 2, sec=target)

                twice = quartered(j) & (core == 1 - turned)

                for pieces, wanted in ((2, twice), (1, ~twice)):
                    @pl.when((b != z) & (s < last) & wanted)
                    def _():
                        drain(send, s, b, pieces, sec=target)

    for c in range(groups):
        span = amps.at[0, :, pl.ds(c * row_count, row_count), :]

        @pl.when(has_up & (c <= z))
        def _():
            remote(span, span, start_up.at[c], start_recv.at[0, 0], ch=z + 1).wait_send()

        @pl.when(has_down & (c >= z))
        def _():
            remote(span, span, start_down.at[c], start_recv.at[0, 0], ch=z - 1).wait_send()

    @pl.loop(0, sectors)
    def _(s):
        @pl.when(s == k)
        def _():
            pltpu.make_async_copy(kept.at[s], kept.at[s], out_local.at[0]).wait()

        for far in range(2):
            part = kept.at[s, :, pl.ds(0, shared if far else energy_count)]
            move = remote(part, part, out_send.at[s], out_recv.at[s], sec=partner)

            @pl.when((s != k) & (s // 2 == across_chip if far else s // 2 != across_chip))
            def _():
                move.wait_send()
                move.wait_recv()

    pltpu.make_async_copy(doubled.at[0], doubled.at[0], doubled_sem.at[0]).wait()
    crossed = remote(doubled.at[0], doubled.at[0], doubled_sem.at[1], doubled_sem.at[2], sec=partner)
    crossed.wait_send()
    crossed.wait_recv()


def per_device_swept(start_amps, energies, thresholds, intersection):
    sectors = lax.axis_size("sec")
    groups = lax.axis_size("ch")
    energy_count, row_count, width_cols = start_amps.shape
    channel_count = intersection.shape[2]
    width = width_cols // 2 // sectors
    pairs = sectors // 2
    dma = pltpu.SemaphoreType.DMA
    stored = pltpu.VMEM(start_amps.shape, jnp.bfloat16)
    swept = pl.pallas_call(
        functools.partial(sweep_kernel, sectors, groups),
        out_shape=stored,
        in_specs=[
            pl.BlockSpec(memory_space=pl.ANY),
            pl.BlockSpec(memory_space=pltpu.SMEM),
            pl.BlockSpec(memory_space=pltpu.VMEM),
            pl.BlockSpec(memory_space=pl.ANY),
        ],
        out_specs=pl.BlockSpec(memory_space=pltpu.VMEM),
        scratch_shapes=[
            pltpu.VMEM((sectors, channel_count, channel_count), jnp.bfloat16),
            pltpu.VMEM((2, energy_count + EXTRA, channel_count, 2 * width), jnp.bfloat16),
            pltpu.VMEM((PAIRED, channel_count, 2 * width), jnp.bfloat16),
            pltpu.VMEM((sectors, 2, energy_count, row_count, width), jnp.bfloat16),
            pltpu.VMEM((2, 2, EXTRA, row_count, width), jnp.bfloat16),
            pltpu.VMEM((sectors, energy_count, LANES, 2 * (channel_count // LANES)), jnp.float32),
            pltpu.VMEM((sectors, groups, row_count // LANES, LANES), jnp.float32),
            dma((5,)),
            dma((sectors, groups, 4)),
            dma((pairs, groups)),
            dma((pairs, groups)),
            dma((pairs, groups)),
            dma((pairs, groups)),
            dma((pairs, groups)),
            dma((energy_count + EXTRA, groups)),
            dma((groups,)),
            dma((groups,)),
            dma((2, groups)),
            dma((groups,)),
            dma((sectors,)),
            dma((sectors,)),
            dma((1,)),
            dma((3,)),
            pltpu.SemaphoreType.REGULAR((2,)),
            dma((sectors,)),
            dma((sectors,)),
        ],
        compiler_params=pltpu.CompilerParams(
            collective_id=0, has_side_effects=True, vmem_limit_bytes=115 * 2**19
        ),
    )(start_amps, energies, thresholds, intersection[0])
    return swept[None]


GATHERED_LIMIT = 24 * 2**20


def per_device(start_amps, energies, thresholds, intersection):
    sectors = lax.axis_size("sec")
    row_count, channel_count = intersection.shape[1:]
    gathered_bytes = sectors * channel_count**2 * intersection.dtype.itemsize
    even = sectors // 2 == 4 and (start_amps.shape[2] // 2) % (sectors * LANES) == 0
    even = even and energies.shape[0] % PAIRED == 0 and energies.shape[0] > EXTRA and row_count % (4 * 16) == 0 and row_count % LANES == 0 and 3 * (channel_count // LANES) <= LANES
    if even and gathered_bytes <= GATHERED_LIMIT:
        return per_device_swept(start_amps, energies, thresholds, intersection)
    return per_device_pipelined(start_amps, energies, thresholds, intersection)


def solution(mesh):
    in_specs = (P(None, "ch", None), P(), P("sec", "ch"), P("sec", "ch", None))
    out_specs = P("sec", None, "ch", None)
    return jax.shard_map(
        per_device, mesh=mesh, in_specs=in_specs, out_specs=out_specs, check_vma=False
    )
```
